32 devices in a mesh: pairs: 2 (over x), tgt: 16 (over z, y, core).
Axes of the slice: x: 2, y: 2, z: 4, core: 2. Of those that a mesh axis runs over, the one named last changes fastest.
Arguments:
- source_features: bfloat16 [256, 1024], P(('pairs', 'tgt')), parts along dimension 0, may hold values from -6 to 6
- target_features: bfloat16 [64, 128, 1024], P(('pairs', 'tgt')), parts along dimension 0, may hold values from -6 to 6
- conv_first: float32 [16, 3, 3, 3, 3], replicated, may hold values from -2 to 2
- conv_second: float32 [16, 3, 3, 3, 3], replicated, may hold values from -0.625 to 0.625
Outputs:
- filtered: float32 [2, 128, 32, 128], P('pairs', None, 'tgt'), parts along dimension 0
The draws below stay inside these ranges and needn't reach their ends.
There are 2 independent parts, one for each index of `pairs`. The reference program is written for one: setup_inputs(seed, part) draws one part's arguments, and reference() takes and returns one part's arrays. A program takes and returns all parts, laid end to end along the dimension named above; an argument that names none is the same for every part. Nothing has to cross between parts.
All inputs are finite; a program needn't handle non-finite values.
Results may differ from the reference program's by a relative error of at most 0.0028.
Values may be sent and summed in bfloat16 or wider, within the bound.
No kernel may reach another device: no remote copies, remote signals or barrier semaphores. Data moves between devices by JAX's collectives and lax.ppermute only.
A program may use at most 128 MiB of HBM per device.

```python
import math
from functools import reduce
import jax
import jax.numpy as jnp
from jax import lax

C = 1024
HID = 16
SR = 1
WA = 128
WB = 128
RB_DEV = 2
SA = 128
HB = 32
N_TGT = 16


pattern_count = 64


def pattern_table(key):
    channel_picks = jax.random.randint(jax.random.fold_in(key, 11), (pattern_count, C), 0, 8)
    return (channel_picks < 3).astype(jnp.float32)


def cell_support(key, row_count, pattern_rows):
    pattern_ids = jax.random.randint(jax.random.fold_in(key, 1), (row_count,), 0, pattern_count)
    kept_mask = (jax.random.randint(jax.random.fold_in(key, 2), (row_count, C), 0, 10) < 7).astype(jnp.float32)
    return pattern_rows[pattern_ids] * kept_mask


def cell_levels(key, row_count):
    levels = jax.random.uniform(key, (row_count, C), jnp.float32, 0.05, 1.0)
    return levels


def assemble(key, support, levels):
    row_count = support.shape[0]
    scales = jnp.exp(jax.random.uniform(jax.random.fold_in(key, 1), (row_count, 1), jnp.float32, math.log(0.6), math.log(6.0)))
    jitter_field = 0.15 * jax.random.normal(jax.random.fold_in(key, 2), (row_count, C), jnp.float32)
    background = -0.5 + jitter_field
    values = scales * (support * levels + (1.0 - support) * background)
    return jnp.clip(values, -6.0, 6.0)


def source_parts(key):
    pattern_rows = pattern_table(key)
    support = cell_support(jax.random.fold_in(key, 21), SA, pattern_rows)
    levels = cell_levels(jax.random.fold_in(key, 22), SA)
    return (support, levels)


def draw_source_features(key, part):
    support, levels = source_parts(key)
    values = assemble(jax.random.fold_in(key, 23), support, levels)
    return values.astype(jnp.bfloat16)


def draw_target_features(key, part):
    pattern_rows = pattern_table(key)
    cell_count = HB * WB
    support = cell_support(jax.random.fold_in(key, 31), cell_count, pattern_rows)
    levels = cell_levels(jax.random.fold_in(key, 32), cell_count)
    source_support, source_levels = source_parts(key)
    chosen = jax.random.permutation(jax.random.fold_in(key, 33), cell_count)[:SA].astype(jnp.int32)
    jitter = 0.03 * jax.random.normal(jax.random.fold_in(key, 34), (SA, C), jnp.float32)
    matched = jnp.clip(source_levels + jitter, 0.01, 1.0)
    support = support.at[chosen].set(source_support)
    levels = levels.at[chosen].set(matched)
    values = assemble(jax.random.fold_in(key, 35), support, levels)
    return values.reshape(HB, WB, C).astype(jnp.bfloat16)


def gaussian(stream_key, dims, deviation, most, kind=jnp.bfloat16):
    array = jax.random.normal(stream_key, dims, jnp.float32) * deviation
    return jnp.minimum(jnp.maximum(array, -most), most).astype(kind)


def setup_inputs(seed: int = 0, part: int = 0) -> dict:
    key_list = jax.random.split(jax.random.key(seed), 5)
    part_keys = jax.random.split(jax.random.fold_in(key_list[4], part), 5)
    source_features = draw_source_features(jax.random.fold_in(jax.random.fold_in(key_list[4], part), 71), part)
    target_features = draw_target_features(jax.random.fold_in(jax.random.fold_in(key_list[4], part), 71), part)
    conv_first = gaussian(key_list[2], (HID, 3, 3, 3, 3), 9 ** -0.5, 2.0, jnp.float32)
    conv_second = gaussian(key_list[3], (HID, 3, 3, 3, 3), 81 ** -0.5, 0.625, jnp.float32)
    return dict(source_features=source_features, target_features=target_features, conv_first=conv_first, conv_second=conv_second)


EPSILON = 1e-05

def normalize(features):
    positive = jax.nn.relu(features.astype(jnp.float32))
    length = jnp.sqrt(lax.optimization_barrier(jnp.sum(positive * positive, axis=-1, keepdims=True)) + 1e-06)
    return (positive / length).astype(jnp.bfloat16)

def mutual_filter(volume, target_best):
    source_best = lax.optimization_barrier(jnp.max(volume, axis=(0, 1), keepdims=True))
    return volume * (volume / (source_best + EPSILON)) * (volume / (target_best[:, :, None, None] + EPSILON))

def offsets_used(source_rows):
    picks = []
    for first in range(3):
        if abs(first - 1) < source_rows:
            for second in range(3):
                for third in range(3):
                    for fourth in range(3):
                        picks.append((first, second, third, fourth))
    return picks

def layer_one(volume, kernel):
    src_rows, src_cols, rows_in, tgt_cols = volume.shape
    rows_out = rows_in - 2
    padded = jnp.pad(volume, ((1, 1), (1, 1), (0, 0), (1, 1)))
    picks = offsets_used(src_rows)
    stacked = jnp.stack([padded[a:a + src_rows, b:b + src_cols, c:c + rows_out, d:d + tgt_cols] for a, b, c, d in picks]).reshape(len(picks), -1)
    weights = jnp.stack([kernel[:, a, b, c, d] for a, b, c, d in picks], axis=1)
    hidden = jnp.dot(weights, stacked, precision=lax.Precision.HIGHEST, preferred_element_type=jnp.float32)
    return hidden.reshape(kernel.shape[0], src_rows, src_cols, rows_out, tgt_cols)

def layer_two(hidden, kernel):
    channels, src_rows, src_cols, rows_in, tgt_cols = hidden.shape
    rows_out = rows_in - 2
    picks = offsets_used(src_rows)
    weights = jnp.stack([kernel[:, a, b, c, d] for a, b, c, d in picks], axis=0)
    spread = jnp.dot(weights, hidden.reshape(channels, -1), precision=lax.Precision.HIGHEST, preferred_element_type=jnp.float32)
    spread = spread.reshape(len(picks), src_rows, src_cols, rows_in, tgt_cols)
    padded = jnp.pad(spread, ((0, 0), (1, 1), (1, 1), (0, 0), (1, 1)))
    pieces = [padded[number, a:a + src_rows, b:b + src_cols, c:c + rows_out, d:d + tgt_cols] for number, (a, b, c, d) in enumerate(picks)]
    return reduce(lambda left, right: left + right, pieces)

def transpose_kernel(kernel):
    return jnp.transpose(kernel, (0, 3, 4, 1, 2))

def consensus_deep(margin_volume, conv_first, conv_second, inside_grid):
    result = None
    kernel_pairs = ((conv_first, conv_second), (transpose_kernel(conv_first), transpose_kernel(conv_second)))
    for first_kernel, second_kernel in kernel_pairs:
        hidden = jax.nn.relu(layer_one(margin_volume, first_kernel))
        hidden = jnp.where(inside_grid[None, None, None, :, None], hidden, jnp.zeros_like(hidden))
        output = jax.nn.relu(layer_two(hidden, second_kernel))
        result = output if result is None else result + output
    return result

def reference(source_features, target_features, conv_first, conv_second):
    source_unit = normalize(source_features)
    target_unit = normalize(target_features.reshape(HB * WB, C))
    correlation = jnp.dot(source_unit, target_unit.T, preferred_element_type=jnp.float32).reshape(SR, WA, HB, WB)
    target_best = lax.optimization_barrier(jnp.max(correlation, axis=(2, 3)))
    mutual_first = mutual_filter(correlation, target_best)
    padded = jnp.pad(mutual_first, ((0, 0), (0, 0), (2, 2), (0, 0)))

    def one_block(block):
        start_row = (block * RB_DEV).astype(jnp.int32)
        window = lax.dynamic_slice_in_dim(padded, start_row, RB_DEV + 4, axis=2)
        global_rows = start_row - 1 + jnp.arange(RB_DEV + 2, dtype=jnp.int32)
        inside_grid = (global_rows >= 0) & (global_rows < HB)
        return consensus_deep(window, conv_first, conv_second, inside_grid)
    blocks = lax.map(one_block, jnp.arange(N_TGT, dtype=jnp.int32))
    consensus = jnp.transpose(blocks, (1, 2, 0, 3, 4)).reshape(SR, WA, HB, WB)
    final_best = lax.optimization_barrier(jnp.max(consensus, axis=(2, 3)))
    return mutual_filter(consensus, final_best)
```

```python
import functools

import jax
import jax.numpy as jnp
import numpy as np
from jax import lax
from jax.experimental import pallas as pl
from jax.experimental.pallas import tpu as pltpu
from jax.sharding import PartitionSpec as P

EPSILON = 1e-05
F32 = jnp.float32
BF16 = jnp.bfloat16
JJ = 2
PASSES = 3
TAPS = 27
TAP_PAD = 32


def round_up(value, multiple):
    return -(-value // multiple) * multiple


def first_selector(rows_in, rows_hid, slot):
    select = np.zeros((2 * TAP_PAD, JJ * rows_hid, JJ + 2, slot), np.float32)
    for jj in range(JJ):
        for k in range(rows_hid):
            for b in range(3):
                for c in range(3):
                    for d in range(3):
                        tap = (b * 3 + c) * 3 + d
                        for part in range(PASSES):
                            column = (part * 3 + d) * rows_in + k + c
                            base = TAP_PAD if part == 2 else 0
                            select[base + tap, jj * rows_hid + k, jj + b, column] = 1
    return select.reshape(2 * TAP_PAD, -1)


def second_selector(rows_hid, rows_out, group):
    select = np.zeros((3, group, rows_hid, 2, TAP_PAD), np.float32)
    for b in range(3):
        for c in range(3):
            for d in range(3):
                tap = (b * 3 + c) * 3 + d
                for branch in range(2):
                    for k in range(rows_out):
                        row = (d * 2 + branch) * rows_out + k
                        select[b, row, k + c, branch, tap] = 1
    return select.reshape(3 * group, -1)


def unit(features):
    positive = jnp.maximum(features.astype(F32), 0.0)
    length = jnp.sqrt(jnp.sum(positive * positive, axis=-1, keepdims=True) + 1e-06)
    return (positive / length).astype(BF16)


def split(value):
    high = value.astype(BF16)
    return high, (value - high.astype(F32)).astype(BF16)


def prepare_kernel(
    hid, rows_hid, edge_ref, target_ref, first_ref, second_ref, pick_ref, spread_ref,
    unit_ref, first_out, second_out,
):
    rows, columns = target_ref.shape[:2]
    for row in range(rows):
        unit_ref[row * columns : (row + 1) * columns] = unit(target_ref[row])
    width = first_out.shape[1]
    taps = jnp.concatenate(split(first_ref[...]), axis=1)
    for block in range(JJ * rows_hid):
        piece = jnp.dot(
            taps, pick_ref[:, block * width : (block + 1) * width], preferred_element_type=F32
        )
        k = block % rows_hid
        if k == 0:
            piece = piece * edge_ref[0]
        if k == rows_hid - 1:
            piece = piece * edge_ref[1]
        first_out[block * 2 * hid : (block + 1) * 2 * hid] = piece.astype(BF16)
    depth = rows_hid * 2 * hid
    groups = rows_hid * 2
    row_group = lax.broadcasted_iota(jnp.int32, (groups * TAP_PAD, depth), 0) // TAP_PAD
    lane_group = lax.broadcasted_iota(jnp.int32, (groups * TAP_PAD, depth), 1) // hid
    tiled = jnp.concatenate([second_ref[...]] * groups, axis=0)
    tiled = jnp.where(row_group == lane_group, tiled, 0.0)
    high, low = split(tiled)
    half = second_out.shape[0] // 2
    high = jnp.dot(spread_ref[...], high, preferred_element_type=F32).astype(BF16)
    low = jnp.dot(spread_ref[...], low, preferred_element_type=F32).astype(BF16)
    second_out[:half, :depth] = high
    second_out[:half, depth:] = high
    second_out[half:, :depth] = low
    second_out[half:, depth:] = jnp.zeros_like(low)


def row_of_maxima(per_row):
    return jnp.max(jnp.transpose(per_row), axis=0, keepdims=True)


def column_scale(best_ref):
    best = jnp.max(best_ref[...], axis=0, keepdims=True)
    square = jnp.broadcast_to(best, (best.shape[1], best.shape[1]))
    return 1.0 / (jnp.transpose(square) + EPSILON)


def half_filter(volume):
    source_best = jnp.max(volume, axis=0, keepdims=True)
    return volume * (volume * (1.0 / (source_best + EPSILON))) * volume


def match_kernel(
    masks, position_ref, near_ref, far_ref, target_ref, half_ref, best_ref, order_ref
):
    chunk = (near_ref.shape[0] + far_ref.shape[0]) // len(masks)
    position = position_ref[0]
    placed = 0
    for ref in (near_ref, far_ref):
        correlation = lax.dot_general(
            unit(ref[...]), target_ref[...], (((1,), (1,)), ((), ())), preferred_element_type=F32
        )
        for piece in range(ref.shape[0] // chunk):
            start = (position ^ masks[placed]) * chunk
            if chunk % 8 == 0:
                start = pl.multiple_of(start, 8)
            order_ref[pl.ds(start, chunk), :] = correlation[piece * chunk : (piece + 1) * chunk]
            placed += 1
    rows, _, columns = half_ref.shape
    most = None
    for row in range(rows):
        volume = order_ref[:, row * columns : (row + 1) * columns]
        half_ref[row] = half_filter(volume)
        most = volume if most is None else jnp.maximum(most, volume)
    best_ref[...] = jnp.broadcast_to(row_of_maxima(most), best_ref.shape)


def shifted(value, offset):
    lanes = value.shape[1]
    lane = lax.broadcasted_iota(jnp.int32, value.shape, 1)
    if offset == -1:
        return jnp.where(lane == 0, 0.0, pltpu.roll(value, 1, 1))
    if offset == 1:
        return jnp.where(lane == lanes - 1, 0.0, pltpu.roll(value, lanes - 1, 1))
    return value


def consensus_kernel(
    slot, group, before_ref, here_ref, after_ref, best_ref, first_ref, second_ref,
    half_ref, most_ref, wide_ref, narrow_ref, partial_ref,
):
    rows, cells, columns = here_ref.shape
    halo = before_ref.shape[0]
    rows_in = rows + 2 * halo
    scale = column_scale(best_ref)
    used = PASSES * 3 * rows_in
    tail = used // 8 * 8
    wide_ref[pl.ds(0, slot), :] = jnp.zeros((slot, columns), F32)
    wide_ref[pl.ds((cells + 1) * slot, slot), :] = jnp.zeros((slot, columns), F32)
    for row in range(used, slot):
        wide_ref[pl.ds(slot + row, cells, stride=slot), :] = jnp.zeros((cells, columns), F32)
    sources = (
        [(before_ref, i) for i in range(halo)]
        + [(here_ref, i) for i in range(rows)]
        + [(after_ref, i) for i in range(halo)]
    )
    for number, (ref, index) in enumerate(sources):
        value = ref[index] * scale
        for d in range(3):
            moved = shifted(value, d - 1)
            high = moved.astype(BF16).astype(F32)
            low = moved - high
            for part, piece in enumerate((high, low, high)):
                row = (part * 3 + d) * rows_in + number
                wide_ref[pl.ds(slot + row, cells, stride=slot), :] = piece

    def narrow(step, carry):
        start = pl.multiple_of(step * slot, slot)
        narrow_ref[pl.ds(start, slot), :] = wide_ref[pl.ds(start, slot), :].astype(BF16)
        return carry

    lax.fori_loop(0, cells + 2, narrow, 0, unroll=5)

    partial_rows = 3 * group
    partial_ref[pl.ds(0, partial_rows), :] = jnp.zeros((partial_rows, columns), F32)
    partial_ref[pl.ds((cells + 1) * partial_rows, partial_rows), :] = jnp.zeros(
        (partial_rows, columns), F32
    )
    depth = first_ref.shape[0] // JJ
    window = (JJ + 2) * slot

    def step_body(step, carry):
        base = step * (2 * JJ)
        taps = jnp.concatenate(
            [
                narrow_ref[pl.ds(pl.multiple_of((base + JJ * side) * slot, slot), window), :]
                for side in range(2)
            ],
            axis=1,
        )
        hidden = jnp.dot(first_ref[...], taps, preferred_element_type=F32)
        hidden = jnp.maximum(hidden, 0.0)
        high, low = split(hidden)
        for jj in range(JJ):
            pair = jnp.concatenate(
                [high[jj * depth : (jj + 1) * depth], low[jj * depth : (jj + 1) * depth]], axis=0
            )
            partial = jnp.dot(second_ref[...], pair, preferred_element_type=F32)
            partial = partial[:partial_rows] + partial[partial_rows:]
            for side in range(2):
                place = (base + JJ * side + jj + 1) * partial_rows
                partial_ref[pl.ds(pl.multiple_of(place, 8), partial_rows), :] = partial[
                    :, side * columns : (side + 1) * columns
                ]
        return carry

    lax.fori_loop(0, cells // (2 * JJ), step_body, 0)

    most = None
    for k in range(rows):
        total = None
        for branch in range(2):
            output = None
            for d in range(3):
                row = (d * 2 + branch) * rows + k
                gathered = None
                for b in range(3):
                    piece = partial_ref[
                        pl.ds(b * partial_rows + b * group + row, cells, stride=partial_rows), :
                    ]
                    gathered = piece if gathered is None else gathered + piece
                gathered = shifted(gathered, 1 - (2 - d))
                output = gathered if output is None else output + gathered
            output = jnp.maximum(output, 0.0)
            total = output if total is None else total + output
        half_ref[k] = half_filter(total)
        most = total if most is None else jnp.maximum(most, total)
    most_ref[...] = jnp.broadcast_to(row_of_maxima(most), most_ref.shape)


def gather_sources(value, devices):
    bits = []
    bit = 1
    while bit < devices:
        bits.append(bit)
        bit *= 2
    bits = bits[2:] + bits[:2][::-1]
    masks = [0]
    near, far = value, value
    for number, bit in enumerate(bits):
        if number:
            near = jnp.concatenate([near, far], axis=0)
        far = lax.ppermute(near, "tgt", [(i, i ^ bit) for i in range(devices)])
        masks = masks + [mask ^ bit for mask in masks]
    return near, far, masks


def exchange_best(rows):
    return lax.all_to_all(rows, "tgt", 0, 0, tiled=True)


VMEM = pl.BlockSpec(memory_space=pltpu.VMEM)
SMEM = pl.BlockSpec(memory_space=pltpu.SMEM)


def shards(source_features, target_features, conv_first, conv_second):
    devices = lax.axis_size("tgt")
    position = lax.axis_index("tgt")
    rows, columns, channels = target_features.shape
    cells = source_features.shape[0] * devices
    hid = conv_first.shape[0]
    halo = 2
    rows_in, rows_hid = rows + 2 * halo, rows + 2
    slot = round_up(PASSES * 3 * rows_in, 16)
    group = round_up(3 * 2 * rows, 8)

    near, far, masks = gather_sources(source_features, devices)

    direct = conv_first[:, 1].reshape(hid, TAPS)
    turned = jnp.transpose(conv_first[:, :, :, 1, :], (0, 3, 1, 2)).reshape(hid, TAPS)
    first_taps = jnp.pad(jnp.concatenate([direct, turned]), ((0, 0), (0, TAP_PAD - TAPS)))
    direct = conv_second[:, 1].reshape(hid, TAPS)
    turned = jnp.transpose(conv_second[:, :, :, 1, :], (0, 3, 1, 2)).reshape(hid, TAPS)
    second_taps = jnp.pad(jnp.concatenate([direct, turned]), ((0, 0), (0, TAP_PAD - TAPS)))
    second_taps = jnp.tile(second_taps.T, (1, rows_hid))
    edges = jnp.stack([position > 0, position < devices - 1]).astype(F32)
    depth = rows_hid * 2 * hid
    target_unit, first_weights, second_weights = pl.pallas_call(
        functools.partial(prepare_kernel, hid, rows_hid),
        out_shape=(
            jax.ShapeDtypeStruct((rows * columns, channels), BF16),
            jax.ShapeDtypeStruct((JJ * depth, (JJ + 2) * slot), BF16),
            jax.ShapeDtypeStruct((6 * group, 2 * depth), BF16),
        ),
        in_specs=[SMEM] + [VMEM] * 5,
        out_specs=(VMEM,) * 3,
        cost_estimate=pl.CostEstimate(flops=10**6, bytes_accessed=2 * 10**6, transcendentals=0),
        name="prepare",
    )(
        edges,
        target_features,
        first_taps,
        second_taps,
        jnp.asarray(first_selector(rows_in, rows_hid, slot), BF16),
        jnp.asarray(second_selector(rows_hid, rows, group), BF16),
    )

    half, best = pl.pallas_call(
        functools.partial(match_kernel, masks),
        out_shape=(
            jax.ShapeDtypeStruct((rows, cells, columns), F32),
            jax.ShapeDtypeStruct((devices, cells), F32),
        ),
        in_specs=[SMEM] + [VMEM] * 3,
        out_specs=(VMEM,) * 2,
        scratch_shapes=[pltpu.VMEM((cells, rows * columns), F32)],
        name="match",
    )(position.reshape(1), near, far, target_unit)

    up = [(i, i + 1) for i in range(devices - 1)]
    down = [(i + 1, i) for i in range(devices - 1)]
    before = lax.ppermute(half[rows - halo :], "tgt", up)
    after = lax.ppermute(half[:halo], "tgt", down)
    best = exchange_best(best)

    half, best = pl.pallas_call(
        functools.partial(consensus_kernel, slot, group),
        out_shape=(
            jax.ShapeDtypeStruct((rows, cells, columns), F32),
            jax.ShapeDtypeStruct((devices, cells), F32),
        ),
        in_specs=[VMEM] * 6,
        out_specs=(VMEM,) * 2,
        scratch_shapes=[
            pltpu.VMEM(((cells + 2) * slot, columns), F32),
            pltpu.VMEM(((cells + 2) * slot, columns), BF16),
            pltpu.VMEM(((cells + 2) * 3 * group, columns), F32),
        ],
        name="consensus",
    )(before, half, after, best, first_weights, second_weights)
    best = jnp.max(exchange_best(best), axis=0)
    filtered = jnp.transpose(half, (1, 0, 2)) * (1.0 / (best + EPSILON))[:, None, None]
    return filtered[None]


def solution(mesh):
    placed = (P(("pairs", "tgt"), None), P(("pairs", "tgt"), None, None), P(), P())
    return jax.shard_map(
        shards, mesh=mesh, in_specs=placed, out_specs=P("pairs", None, "tgt", None), check_vma=False
    )
```

```python
import functools

import jax
import jax.numpy as jnp
import numpy as np
from jax import lax
from jax.experimental import pallas as pl
from jax.experimental.pallas import tpu as pltpu
from jax.sharding import PartitionSpec as P

EPSILON = 1e-05
F32 = jnp.float32
BF16 = jnp.bfloat16
TAPS = 27
TAP_PAD = 32
SUBLANES = 8
ORDER = ((0, 0), (1, 0), (2, 0), (0, 1), (1, 1), (2, 1))
REPEATED = 4


def parts_of(local):
    hidden = local + 2
    count = -(-hidden // (SUBLANES - 2))
    size = -(-hidden // count)
    parts = []
    for start in range(0, hidden, size):
        first = min(start, max(0, local + 4 - SUBLANES))
        parts.append((first, start, min(size, hidden - start)))
    return parts


def first_selector(parts):
    tile = len(ORDER) * SUBLANES
    width = 3 * (tile + REPEATED * SUBLANES)
    blocks = [(first, hidden) for first, start, size in parts for hidden in range(start, start + size)]
    select = np.zeros((2 * TAP_PAD, len(blocks), width), np.float32)
    for number, (first, hidden) in enumerate(blocks):
        for b in range(3):
            for c in range(3):
                for d in range(3):
                    tap = (b * 3 + c) * 3 + d
                    for place, (offset, low) in enumerate(ORDER):
                        if offset != d:
                            continue
                        row = place * SUBLANES + hidden + b - first
                        select[tap, number, c * tile + row] = 1
                        if not low:
                            column = 3 * tile + c * REPEATED * SUBLANES + row
                            select[TAP_PAD + tap, number, column] = 1
    return select.reshape(2 * TAP_PAD, -1)


def second_selector(local):
    select = np.zeros((3, 3, 2, SUBLANES, local + 2, 2, TAP_PAD), np.float32)
    for b in range(3):
        for c in range(3):
            for d in range(3):
                tap = (b * 3 + c) * 3 + d
                for branch in range(2):
                    for cell in range(local):
                        select[c, d, branch, cell, cell + b, branch, tap] = 1
    return select.reshape(18 * SUBLANES, -1)


def unit(features):
    positive = jnp.maximum(features.astype(F32), 0.0)
    length = jnp.sqrt(jnp.sum(positive * positive, axis=-1, keepdims=True) + 1e-06)
    return (positive / length).astype(BF16)


def split(value):
    high = value.astype(BF16)
    return high, (value - high.astype(F32)).astype(BF16)


def prepare_kernel(
    hid, edge_ref, target_ref, first_ref, second_ref, pick_ref, spread_ref,
    unit_ref, first_out, second_out,
):
    rows, columns = target_ref.shape[:2]
    for row in range(rows):
        unit_ref[row * columns : (row + 1) * columns] = unit(target_ref[row])
    width = first_out.shape[1]
    taps = jnp.concatenate(split(first_ref[...]), axis=1)
    blocks = first_out.shape[0] // (2 * hid)
    for block in range(blocks):
        piece = jnp.dot(
            taps, pick_ref[:, block * width : (block + 1) * width], preferred_element_type=F32
        )
        if block == 0:
            piece = piece * edge_ref[0]
        if block == blocks - 1:
            piece = piece * edge_ref[1]
        first_out[block * 2 * hid : (block + 1) * 2 * hid] = piece.astype(BF16)
    depth = blocks * 2 * hid
    groups = blocks * 2
    row_group = lax.broadcasted_iota(jnp.int32, (groups * TAP_PAD, depth), 0) // TAP_PAD
    lane_group = lax.broadcasted_iota(jnp.int32, (groups * TAP_PAD, depth), 1) // hid
    tiled = jnp.concatenate([second_ref[...]] * groups, axis=0)
    tiled = jnp.where(row_group == lane_group, tiled, 0.0)
    high, low = split(tiled)
    half = second_out.shape[0] // 2
    high = jnp.dot(spread_ref[...], high, preferred_element_type=F32).astype(BF16)
    low = jnp.dot(spread_ref[...], low, preferred_element_type=F32).astype(BF16)
    second_out[:half, :depth] = high
    second_out[:half, depth:] = high
    second_out[half:, :depth] = low
    second_out[half:, depth:] = jnp.zeros_like(low)


def match_kernel(
    local, source_ref, target_ref, send_ref, order_ref
):
    rows, padded, columns = order_ref.shape
    cells = padded - 2 * SUBLANES
    correlation = lax.dot_general(
        unit(source_ref[...]), target_ref[...], (((1,), (1,)), ((), ())), preferred_element_type=F32
    )
    window = max(SUBLANES, local + 4)
    blank = jnp.zeros((SUBLANES, columns), F32)
    for row in range(rows):
        order_ref[row, :SUBLANES, :] = blank
        order_ref[row, SUBLANES + cells :, :] = blank
        order_ref[row, SUBLANES : SUBLANES + cells, :] = correlation[
            :, row * columns : (row + 1) * columns
        ]
        source_best = jnp.max(order_ref[row], axis=0, keepdims=True)
        inverse = 1.0 / (source_best + EPSILON)
        for target in range(send_ref.shape[0]):
            first = SUBLANES + target * local - 2
            send_ref[target, row * window : (row + 1) * window] = order_ref[
                row, first : first + window, :
            ]
            place = rows * window + row
            send_ref[target, place : place + 1] = inverse


def lane_shifts(value):
    lanes = value.shape[-1]
    lane = lax.broadcasted_iota(jnp.int32, value.shape, value.ndim - 1)
    axis = value.ndim - 1
    left = jnp.where(lane == 0, 0.0, pltpu.roll(value, 1, axis))
    right = jnp.where(lane == lanes - 1, 0.0, pltpu.roll(value, lanes - 1, axis))
    return left, right


def consensus_kernel(
    parts, local, rows, came_ref, first_ref, second_ref, send_ref, tile_ref, partial_ref
):
    devices, _, columns = came_ref.shape
    window = max(SUBLANES, local + 4)
    grid_rows = devices * rows
    tile = len(ORDER) * SUBLANES
    again = REPEATED * SUBLANES
    zero = jnp.zeros((SUBLANES, columns), F32)

    def piece_of(device, row, first):
        return came_ref[device, row * window + first : row * window + first + SUBLANES, :]

    def survey(device, best):
        best = list(best)
        for number, (first, _, _) in enumerate(parts):
            for row in range(rows):
                best[number] = jnp.maximum(best[number], piece_of(device, row, first))
        return tuple(best)

    best = lax.fori_loop(0, devices, survey, (zero,) * len(parts), unroll=4)
    scales = [
        jnp.broadcast_to(1.0 / (jnp.max(most, axis=1, keepdims=True) + EPSILON), most.shape)
        for most in best
    ]

    blank = jnp.zeros((tile, columns), BF16)
    for number in range(len(parts)):
        tile_ref[0, number] = blank
        tile_ref[grid_rows + 1, number] = blank

    def build(device, carry):
        for row in range(rows):
            place = rows * window + row
            inverse = came_ref[device, place : place + 1, :]
            for number, (first, _, _) in enumerate(parts):
                value = piece_of(device, row, first)
                value = value * (value * inverse) * (value * scales[number])
                left, right = lane_shifts(value)
                moved = (left, value, right)
                high = [piece.astype(BF16).astype(F32) for piece in moved]
                low = [piece - rounded for piece, rounded in zip(moved, high)]
                stacked = jnp.concatenate(
                    [(low if part else high)[offset] for offset, part in ORDER], axis=0
                )
                tile_ref[device * rows + row + 1, number] = stacked.astype(BF16)
        return carry

    lax.fori_loop(0, devices, build, 0, unroll=2)

    partial_rows = second_ref.shape[0] // 2
    empty = jnp.zeros((partial_rows, columns), F32)
    partial_ref[0] = empty
    partial_ref[grid_rows + 1] = empty
    sides = 2
    unroll = 2

    def layers(step, carry):
        for index in range(unroll):
            base = (step * unroll + index) * sides
            hidden = []
            offset = 0
            for number, (_, _, size) in enumerate(parts):
                taps = []
                for side in range(sides):
                    pieces = [tile_ref[base + side + c, number] for c in range(3)]
                    pieces += [tile_ref[base + side + c, number, :again] for c in range(3)]
                    taps.append(jnp.concatenate(pieces, axis=0))
                count = size * first_ref.shape[0] // (local + 2)
                hidden.append(
                    jnp.dot(
                        first_ref[offset : offset + count],
                        jnp.concatenate(taps, axis=1),
                        preferred_element_type=F32,
                    )
                )
                offset += count
            halves = [split(jnp.maximum(piece, 0.0)) for piece in hidden]
            pair = jnp.concatenate(
                [high for high, _ in halves] + [low for _, low in halves], axis=0
            )
            partial = jnp.dot(second_ref[...], pair, preferred_element_type=F32)
            partial = partial[:partial_rows] + partial[partial_rows:]
            for side in range(sides):
                partial_ref[base + side + 1] = partial[:, side * columns : (side + 1) * columns]
        return carry

    lax.fori_loop(0, grid_rows // (sides * unroll), layers, 0)

    def gather(device, most):
        for row in range(rows):
            total = None
            for branch in range(2):
                sums = []
                for d in range(3):
                    value = None
                    for c in range(3):
                        start = ((c * 3 + d) * 2 + branch) * SUBLANES
                        piece = partial_ref[device * rows + row + c, start : start + SUBLANES, :]
                        value = piece if value is None else value + piece
                    sums.append(value)
                output = lane_shifts(sums[0])[0] + sums[1] + lane_shifts(sums[2])[1]
                output = jnp.maximum(output, 0.0)
                total = output if total is None else total + output
            send_ref[device, row * SUBLANES : (row + 1) * SUBLANES] = total
            most = jnp.maximum(most, total)
        return most

    most = lax.fori_loop(0, devices, gather, zero, unroll=2)
    scale = jnp.broadcast_to(
        1.0 / (jnp.max(most, axis=1, keepdims=True) + EPSILON), most.shape
    )
    for device in range(devices):
        send_ref[device, rows * SUBLANES :] = scale


def finish_kernel(local, came_ref, out_ref):
    devices = came_ref.shape[0]
    rows = out_ref.shape[1]
    for row in range(rows):
        first = row * SUBLANES
        most = came_ref[0, first : first + SUBLANES]
        for device in range(1, devices):
            most = jnp.maximum(most, came_ref[device, first : first + SUBLANES])
        inverse = 1.0 / (jnp.max(most, axis=0, keepdims=True) + EPSILON)
        for device in range(devices):
            value = came_ref[device, first : first + SUBLANES]
            scale = came_ref[device, rows * SUBLANES :]
            value = value * (value * inverse) * (value * scale)
            out_ref[device * local : (device + 1) * local, row, :] = value[:local]


def exchange(slots):
    return lax.all_to_all(slots, "tgt", 0, 0, tiled=True)


def room(*shapes):
    scratch = sum(int(np.prod(shape)) * jnp.dtype(kind).itemsize for shape, kind in shapes)
    return pltpu.CompilerParams(vmem_limit_bytes=scratch + 6 * 2**20)


VMEM = pl.BlockSpec(memory_space=pltpu.VMEM)
SMEM = pl.BlockSpec(memory_space=pltpu.SMEM)


def shards(source_features, target_features, conv_first, conv_second):
    devices = lax.axis_size("tgt")
    position = lax.axis_index("tgt")
    rows, columns, channels = target_features.shape
    cells = source_features.shape[0] * devices
    hid = conv_first.shape[0]
    local = cells // devices
    parts = parts_of(local)
    hidden = local + 2
    window = max(SUBLANES, local + 4)
    tile = len(ORDER) * SUBLANES
    width = 3 * (tile + REPEATED * SUBLANES)
    depth = hidden * 2 * hid
    assert local <= SUBLANES and rows * devices % 4 == 0

    spread = jnp.broadcast_to(source_features[None], (devices,) + source_features.shape)
    sources = exchange(spread).reshape(cells, channels)

    direct = conv_first[:, 1].reshape(hid, TAPS)
    turned = jnp.transpose(conv_first[:, :, :, 1, :], (0, 3, 1, 2)).reshape(hid, TAPS)
    first_taps = jnp.pad(jnp.concatenate([direct, turned]), ((0, 0), (0, TAP_PAD - TAPS)))
    direct = conv_second[:, 1].reshape(hid, TAPS)
    turned = jnp.transpose(conv_second[:, :, :, 1, :], (0, 3, 1, 2)).reshape(hid, TAPS)
    second_taps = jnp.pad(jnp.concatenate([direct, turned]), ((0, 0), (0, TAP_PAD - TAPS)))
    second_taps = jnp.tile(second_taps.T, (1, hidden))
    edges = jnp.stack([position > 0, position < devices - 1]).astype(F32)
    second_rows = 18 * SUBLANES
    target_unit, first_weights, second_weights = pl.pallas_call(
        functools.partial(prepare_kernel, hid),
        out_shape=(
            jax.ShapeDtypeStruct((rows * columns, channels), BF16),
            jax.ShapeDtypeStruct((depth, width), BF16),
            jax.ShapeDtypeStruct((2 * second_rows, 2 * depth), BF16),
        ),
        in_specs=[SMEM] + [VMEM] * 5,
        out_specs=(VMEM,) * 3,
        cost_estimate=pl.CostEstimate(flops=10**6, bytes_accessed=2 * 10**6, transcendentals=0),
        compiler_params=room(),
        name="prepare",
    )(
        edges,
        target_features,
        first_taps,
        second_taps,
        jnp.asarray(first_selector(parts), BF16),
        jnp.asarray(second_selector(local), BF16),
    )

    slots = pl.pallas_call(
        functools.partial(match_kernel, local),
        out_shape=jax.ShapeDtypeStruct((devices, rows * window + rows, columns), F32),
        in_specs=[VMEM] * 2,
        out_specs=VMEM,
        scratch_shapes=[
            pltpu.VMEM((rows, cells + 2 * SUBLANES, columns), F32),
        ],
        compiler_params=room(),
        name="match",
    )(sources, target_unit)

    stores = (
        ((rows * devices + 2, len(parts), tile, columns), BF16),
        ((rows * devices + 2, second_rows, columns), F32),
    )
    slots = pl.pallas_call(
        functools.partial(consensus_kernel, parts, local, rows),
        out_shape=jax.ShapeDtypeStruct((devices, (rows + 1) * SUBLANES, columns), F32),
        in_specs=[VMEM] * 3,
        out_specs=VMEM,
        scratch_shapes=[pltpu.VMEM(shape, kind) for shape, kind in stores],
        compiler_params=room(*stores),
        name="consensus",
    )(exchange(slots), first_weights, second_weights)

    filtered = pl.pallas_call(
        functools.partial(finish_kernel, local),
        out_shape=jax.ShapeDtypeStruct((cells, rows, columns), F32),
        in_specs=[VMEM],
        out_specs=VMEM,
        compiler_params=room(),
        name="finish",
    )(exchange(slots))
    return filtered[None]


def solution(mesh):
    placed = (P(("pairs", "tgt"), None), P(("pairs", "tgt"), None, None), P(), P())
    return jax.shard_map(
        shards, mesh=mesh, in_specs=placed, out_specs=P("pairs", None, "tgt", None), check_vma=False
    )
```

```python
import functools

import jax
import jax.numpy as jnp
import numpy as np
from jax import lax
from jax.experimental import pallas as pl
from jax.experimental.pallas import tpu as pltpu
from jax.sharding import PartitionSpec as P

EPSILON = 1e-05
F32 = jnp.float32
BF16 = jnp.bfloat16
TAP_PAD = 32
SUBLANES = 8
ORDER = ((0, 0), (1, 0), (2, 0), (0, 1), (1, 1), (2, 1))
REPEATED = 4


def parts_of(local):
    hidden = local + 2
    count = -(-hidden // (SUBLANES - 2))
    size = -(-hidden // count)
    parts = []
    for start in range(0, hidden, size):
        first = min(start, max(0, local + 4 - SUBLANES))
        parts.append((first, start, min(size, hidden - start)))
    return parts


def first_selector(parts):
    tile = len(ORDER) * SUBLANES
    width = 3 * (tile + REPEATED * SUBLANES)
    blocks = [(first, hidden) for first, start, size in parts for hidden in range(start, start + size)]
    select = np.zeros((2 * TAP_PAD, len(blocks), width), np.float32)
    for number, (first, hidden) in enumerate(blocks):
        for b in range(3):
            for c in range(3):
                for d in range(3):
                    tap = (b * 3 + c) * 3 + d
                    for place, (offset, low) in enumerate(ORDER):
                        if offset != d:
                            continue
                        row = place * SUBLANES + hidden + b - first
                        select[tap, number, c * tile + row] = 1
                        if not low:
                            column = 3 * tile + c * REPEATED * SUBLANES + row
                            select[TAP_PAD + tap, number, column] = 1
    return select.reshape(2 * TAP_PAD, -1)


def second_selector(local):
    select = np.zeros((3, 3, 2, SUBLANES, local + 2, 2, TAP_PAD), np.float32)
    for b in range(3):
        for c in range(3):
            for d in range(3):
                tap = (b * 3 + c) * 3 + d
                for branch in range(2):
                    for cell in range(local):
                        select[c, d, branch, cell, cell + b, branch, tap] = 1
    return select.reshape(18 * SUBLANES, -1)


def unit(features):
    positive = jnp.maximum(features.astype(F32), 0.0)
    length = jnp.sqrt(jnp.sum(positive * positive, axis=-1, keepdims=True) + 1e-06)
    return (positive / length).astype(BF16)


def split(value):
    high = value.astype(BF16)
    return high, (value - high.astype(F32)).astype(BF16)


def prepare_kernel(
    devices, target_ref, first_ref, second_ref, pick_ref, spread_ref, gate_ref,
    unit_ref, first_out, second_out, taps_ref,
):
    rows, columns = target_ref.shape[:2]
    for row in range(rows):
        unit_ref[row * columns : (row + 1) * columns] = unit(target_ref[row])
    hid = first_ref.shape[-1]
    taps_ref[...] = jnp.zeros(taps_ref.shape, F32)
    for number, ref in enumerate((first_ref, second_ref)):
        base = 2 * TAP_PAD * number
        for b in range(3):
            for c in range(3):
                start = base + (b * 3 + c) * 3
                taps_ref[start : start + 3, :hid] = ref[1, b, c]
        for c in range(3):
            for d in range(3):
                piece = ref[c, d, 1]
                for b in range(3):
                    start = base + TAP_PAD + (b * 3 + c) * 3 + d
                    taps_ref[start : start + 1, :hid] = piece[b : b + 1]
    branches = [taps_ref[i * TAP_PAD : (i + 1) * TAP_PAD, :hid] for i in range(4)]
    width = first_out.shape[1]
    taps = jnp.concatenate(split(jnp.concatenate(branches[:2], axis=1)), axis=0)
    blocks = first_out.shape[0] // (2 * hid)
    for block in range(blocks):
        piece = lax.dot_general(
            taps, pick_ref[:, block * width : (block + 1) * width],
            (((0,), (0,)), ((), ())), preferred_element_type=F32,
        )
        if block == 0:
            piece = piece * jnp.where(lax.axis_index("tgt") == 0, 0.0, 1.0)
        if block == blocks - 1:
            piece = piece * jnp.where(lax.axis_index("tgt") == devices - 1, 0.0, 1.0)
        first_out[block * 2 * hid : (block + 1) * 2 * hid] = piece.astype(BF16)
    depth = blocks * 2 * hid
    groups = blocks * 2
    row_group = lax.broadcasted_iota(jnp.int32, (groups * TAP_PAD, depth), 0) // TAP_PAD
    lane_group = lax.broadcasted_iota(jnp.int32, (groups * TAP_PAD, depth), 1) // hid
    tiled = jnp.concatenate([jnp.concatenate(branches[2:], axis=1)] * blocks, axis=1)
    tiled = jnp.concatenate([tiled] * groups, axis=0)
    tiled = jnp.where(row_group == lane_group, tiled, 0.0)
    high, low = split(tiled)
    half = second_out.shape[0] // 2
    high = jnp.dot(spread_ref[...], high, preferred_element_type=F32).astype(BF16)
    low = jnp.dot(spread_ref[...], low, preferred_element_type=F32).astype(BF16)
    second_out[:half, :depth] = high
    second_out[:half, depth:] = high
    second_out[half:, :depth] = low
    second_out[half:, depth:] = jnp.zeros_like(low)


def spread_kernel(
    source_ref, target_ref, pick_ref, scatter_ref,
    out_ref, target_out, pick_out, scatter_out, source_copy, sems,
):
    copies = [
        pltpu.make_async_copy(start, end, sems.at[number])
        for number, (start, end) in enumerate(
            (
                (source_ref, source_copy),
                (target_ref, target_out),
                (pick_ref, pick_out),
                (scatter_ref, scatter_out),
            )
        )
    ]
    for copy in copies:
        copy.start()
    copies[0].wait()
    half = out_ref.shape[2]
    for device in range(out_ref.shape[0]):
        start = device % 2 * half
        out_ref[device] = source_copy[:, start : start + half]
    for copy in copies[1:]:
        copy.wait()


def match_kernel(
    local, mine_ref, other_ref, target_ref, send_ref, source_ref, order_ref
):
    rows, padded, columns = order_ref.shape
    cells = padded - 2 * SUBLANES
    half = mine_ref.shape[1]
    side = lax.axis_index("tgt") % 2
    block = min(cells, 32)
    for first in range(0, cells, block):
        halves = [
            jnp.maximum(ref[first : first + block].astype(F32), 0.0)
            for ref in (mine_ref, other_ref)
        ]
        squares = [jnp.sum(piece * piece, axis=-1, keepdims=True) for piece in halves]
        length = jnp.sqrt(squares[0] + squares[1] + 1e-06)
        for number, piece in enumerate(halves):
            start = pl.multiple_of((side ^ number) * half, half)
            source_ref[first : first + block, pl.ds(start, half)] = (piece / length).astype(BF16)
    correlation = lax.dot_general(
        source_ref[...], target_ref[...], (((1,), (1,)), ((), ())), preferred_element_type=F32
    )
    window = max(SUBLANES, local + 4)
    blank = jnp.zeros((SUBLANES, columns), F32)
    for row in range(rows):
        order_ref[row, :SUBLANES, :] = blank
        order_ref[row, SUBLANES + cells :, :] = blank
        order_ref[row, SUBLANES : SUBLANES + cells, :] = correlation[
            :, row * columns : (row + 1) * columns
        ]
        source_best = jnp.max(order_ref[row], axis=0, keepdims=True)
        inverse = 1.0 / (source_best + EPSILON)
        for target in range(send_ref.shape[0]):
            first = SUBLANES + target * local - 2
            send_ref[target, row * window : (row + 1) * window] = order_ref[
                row, first : first + window, :
            ]
            place = rows * window + row
            send_ref[target, place : place + 1] = inverse


def lane_shifts(value):
    lanes = value.shape[-1]
    lane = lax.broadcasted_iota(jnp.int32, value.shape, value.ndim - 1)
    axis = value.ndim - 1
    left = jnp.where(lane == 0, 0.0, pltpu.roll(value, 1, axis))
    right = jnp.where(lane == lanes - 1, 0.0, pltpu.roll(value, lanes - 1, axis))
    return left, right


def consensus_kernel(
    parts, local, rows, came_ref, first_ref, second_ref, send_ref, tile_ref, partial_ref
):
    devices, _, columns = came_ref.shape
    window = max(SUBLANES, local + 4)
    grid_rows = devices * rows
    tile = len(ORDER) * SUBLANES
    again = REPEATED * SUBLANES
    zero = jnp.zeros((SUBLANES, columns), F32)

    def piece_of(device, row, first):
        return came_ref[device, row * window + first : row * window + first + SUBLANES, :]

    def survey(device, best):
        best = list(best)
        for number, (first, _, _) in enumerate(parts):
            for row in range(rows):
                best[number] = jnp.maximum(best[number], piece_of(device, row, first))
        return tuple(best)

    best = lax.fori_loop(0, devices, survey, (zero,) * len(parts), unroll=4)
    scales = [
        jnp.broadcast_to(1.0 / (jnp.max(most, axis=1, keepdims=True) + EPSILON), most.shape)
        for most in best
    ]

    blank = jnp.zeros((tile, columns), BF16)
    for number in range(len(parts)):
        tile_ref[0, number] = blank

    def build(device, present):
        source = jnp.minimum(device, devices - 1)
        for row in range(rows):
            place = rows * window + row
            inverse = came_ref[source, place : place + 1, :] * present
            for number, (first, _, _) in enumerate(parts):
                value = piece_of(source, row, first)
                value = value * (value * inverse) * (value * scales[number])
                left, right = lane_shifts(value)
                moved = (left, value, right)
                high = [piece.astype(BF16).astype(F32) for piece in moved]
                low = [piece - rounded for piece, rounded in zip(moved, high)]
                stacked = jnp.concatenate(
                    [(low if part else high)[offset] for offset, part in ORDER], axis=0
                )
                tile_ref[device * rows + row + 1, number] = stacked.astype(BF16)

    partial_rows = second_ref.shape[0] // 2
    empty = jnp.zeros((partial_rows, columns), F32)
    partial_ref[0] = empty
    partial_ref[grid_rows + 1] = empty

    def layers(device):
        base = device * rows
        hidden = []
        offset = 0
        for number, (_, _, size) in enumerate(parts):
            taps = []
            for side in range(rows):
                pieces = [tile_ref[base + side + c, number] for c in range(3)]
                pieces += [tile_ref[base + side + c, number, :again] for c in range(3)]
                taps.append(jnp.concatenate(pieces, axis=0))
            count = size * first_ref.shape[0] // (local + 2)
            hidden.append(
                jnp.dot(
                    first_ref[offset : offset + count],
                    jnp.concatenate(taps, axis=1),
                    preferred_element_type=F32,
                )
            )
            offset += count
        halves = [split(jnp.maximum(piece, 0.0)) for piece in hidden]
        pair = jnp.concatenate([high for high, _ in halves] + [low for _, low in halves], axis=0)
        partial = jnp.dot(second_ref[...], pair, preferred_element_type=F32)
        partial = partial[:partial_rows] + partial[partial_rows:]
        for side in range(rows):
            partial_ref[base + side + 1] = partial[:, side * columns : (side + 1) * columns]

    def gather(device, most):
        for row in range(rows):
            total = None
            for branch in range(2):
                sums = []
                for d in range(3):
                    value = None
                    for c in range(3):
                        start = ((c * 3 + d) * 2 + branch) * SUBLANES
                        piece = partial_ref[device * rows + row + c, start : start + SUBLANES, :]
                        value = piece if value is None else value + piece
                    sums.append(value)
                output = lane_shifts(sums[0])[0] + sums[1] + lane_shifts(sums[2])[1]
                output = jnp.maximum(output, 0.0)
                total = output if total is None else total + output
            send_ref[device, row * SUBLANES : (row + 1) * SUBLANES] = total
            most = jnp.maximum(most, total)
        return most

    def present(device):
        return jnp.where(device < devices, 1.0, 0.0).astype(F32)

    build(0, 1.0)
    build(1, 1.0)
    layers(0)
    build(2, present(2))
    layers(1)
    build(3, present(3))

    def step(device, most):
        most = gather(device - 2, most)
        build(device + 2, present(device + 2))
        layers(device)
        return most

    most = lax.fori_loop(2, devices, step, zero, unroll=2)
    most = gather(devices - 2, most)
    most = gather(devices - 1, most)
    scale = jnp.broadcast_to(
        1.0 / (jnp.max(most, axis=1, keepdims=True) + EPSILON), most.shape
    )
    for device in range(devices):
        send_ref[device, rows * SUBLANES :] = scale


def finish_kernel(local, came_ref, out_ref):
    devices = came_ref.shape[0]
    rows = out_ref.shape[1]
    for row in range(rows):
        first = row * SUBLANES
        most = came_ref[0, first : first + SUBLANES]
        for device in range(1, devices):
            most = jnp.maximum(most, came_ref[device, first : first + SUBLANES])
        inverse = 1.0 / (jnp.max(most, axis=0, keepdims=True) + EPSILON)
        for device in range(devices):
            value = came_ref[device, first : first + SUBLANES]
            scale = came_ref[device, rows * SUBLANES :]
            value = value * (value * inverse) * (value * scale)
            out_ref[device * local : (device + 1) * local, row, :] = value[:local]


def exchange(slots):
    return lax.all_to_all(slots, "tgt", 0, 0, tiled=True)


def room(*shapes):
    scratch = sum(int(np.prod(shape)) * jnp.dtype(kind).itemsize for shape, kind in shapes)
    return pltpu.CompilerParams(vmem_limit_bytes=scratch + 6 * 2**20)


VMEM = pl.BlockSpec(memory_space=pltpu.VMEM)
ANY = pl.BlockSpec(memory_space=pltpu.HBM)


def shards(source_features, target_features, conv_first, conv_second):
    devices = lax.axis_size("tgt")
    rows, columns, channels = target_features.shape
    cells = source_features.shape[0] * devices
    hid = conv_first.shape[0]
    local = cells // devices
    parts = parts_of(local)
    hidden = local + 2
    window = max(SUBLANES, local + 4)
    tile = len(ORDER) * SUBLANES
    width = 3 * (tile + REPEATED * SUBLANES)
    depth = hidden * 2 * hid
    assert local <= SUBLANES and rows * devices % 4 == 0

    pick = jnp.asarray(first_selector(parts), BF16)
    scatter = jnp.asarray(second_selector(local), BF16)
    spread, target_features, pick, scatter = pl.pallas_call(
        spread_kernel,
        out_shape=(
            jax.ShapeDtypeStruct((devices, source_features.shape[0], channels // 2), BF16),
            jax.ShapeDtypeStruct(target_features.shape, BF16),
            jax.ShapeDtypeStruct(pick.shape, BF16),
            jax.ShapeDtypeStruct(scatter.shape, BF16),
        ),
        in_specs=[ANY] * 4,
        out_specs=(VMEM,) * 4,
        scratch_shapes=[
            pltpu.VMEM(source_features.shape, BF16),
            pltpu.SemaphoreType.DMA((4,)),
        ],
        compiler_params=room(),
        name="spread",
    )(
        *(
            pltpu.with_memory_space_constraint(value, pltpu.HBM)
            for value in (source_features, target_features, pick, scatter)
        )
    )
    mine = exchange(spread).reshape(cells, channels // 2)
    other = lax.ppermute(mine, "tgt", [(i, i ^ 1) for i in range(devices)])

    second_rows = 18 * SUBLANES
    target_unit, first_weights, second_weights = pl.pallas_call(
        functools.partial(prepare_kernel, devices),
        out_shape=(
            jax.ShapeDtypeStruct((rows * columns, channels), BF16),
            jax.ShapeDtypeStruct((depth, width), BF16),
            jax.ShapeDtypeStruct((2 * second_rows, 2 * depth), BF16),
        ),
        in_specs=[VMEM] * 5 + [pl.BlockSpec(memory_space=pl.ANY)],
        out_specs=(VMEM,) * 3,
        scratch_shapes=[pltpu.VMEM((4 * TAP_PAD, 128), F32)],
        cost_estimate=pl.CostEstimate(flops=10**6, bytes_accessed=2 * 10**6, transcendentals=0),
        compiler_params=room(),
        name="prepare",
    )(
        target_features,
        jnp.transpose(conv_first, (1, 2, 3, 4, 0)),
        jnp.transpose(conv_second, (1, 2, 3, 4, 0)),
        pick,
        scatter,
        mine,
    )

    slots = pl.pallas_call(
        functools.partial(match_kernel, local),
        out_shape=jax.ShapeDtypeStruct((devices, rows * window + rows, columns), F32),
        in_specs=[VMEM] * 3,
        out_specs=VMEM,
        scratch_shapes=[
            pltpu.VMEM((cells, channels), BF16),
            pltpu.VMEM((rows, cells + 2 * SUBLANES, columns), F32),
        ],
        compiler_params=room(),
        name="match",
    )(mine, other, target_unit)

    stores = (
        ((rows * (devices + 2) + 2, len(parts), tile, columns), BF16),
        ((rows * devices + 2, second_rows, columns), F32),
    )
    slots = pl.pallas_call(
        functools.partial(consensus_kernel, parts, local, rows),
        out_shape=jax.ShapeDtypeStruct((devices, (rows + 1) * SUBLANES, columns), F32),
        in_specs=[VMEM] * 3,
        out_specs=VMEM,
        scratch_shapes=[pltpu.VMEM(shape, kind) for shape, kind in stores],
        compiler_params=room(*stores),
        name="consensus",
    )(exchange(slots), first_weights, second_weights)

    filtered = pl.pallas_call(
        functools.partial(finish_kernel, local),
        out_shape=jax.ShapeDtypeStruct((cells, rows, columns), F32),
        in_specs=[VMEM],
        out_specs=VMEM,
        compiler_params=room(),
        name="finish",
    )(exchange(slots))
    return filtered[None]


def solution(mesh):
    placed = (P(("pairs", "tgt"), None), P(("pairs", "tgt"), None, None), P(), P())
    return jax.shard_map(
        shards, mesh=mesh, in_specs=placed, out_specs=P("pairs", None, "tgt", None), check_vma=False
    )
```

```python
import functools

import jax
import jax.numpy as jnp
import numpy as np
from jax import lax
from jax.experimental import pallas as pl
from jax.experimental.pallas import tpu as pltpu
from jax.sharding import PartitionSpec as P

EPSILON = 1e-05
F32 = jnp.float32
BF16 = jnp.bfloat16
TAP_PAD = 32
SUBLANES = 8
ORDER = ((0, 0), (1, 0), (2, 0), (0, 1), (1, 1), (2, 1))
REPEATED = 4


def parts_of(local):
    hidden = local + 2
    count = -(-hidden // (SUBLANES - 2))
    size = -(-hidden // count)
    parts = []
    for start in range(0, hidden, size):
        first = min(start, max(0, local + 4 - SUBLANES))
        parts.append((first, start, min(size, hidden - start)))
    return parts


def first_selector(parts):
    tile = len(ORDER) * SUBLANES
    width = 3 * (tile + REPEATED * SUBLANES)
    blocks = [(first, hidden) for first, start, size in parts for hidden in range(start, start + size)]
    select = np.zeros((2 * TAP_PAD, len(blocks), width), np.float32)
    for number, (first, hidden) in enumerate(blocks):
        for b in range(3):
            for c in range(3):
                for d in range(3):
                    tap = (b * 3 + c) * 3 + d
                    for place, (offset, low) in enumerate(ORDER):
                        if offset != d:
                            continue
                        row = place * SUBLANES + hidden + b - first
                        select[tap, number, c * tile + row] = 1
                        if not low:
                            column = 3 * tile + c * REPEATED * SUBLANES + row
                            select[TAP_PAD + tap, number, column] = 1
    return select.reshape(2 * TAP_PAD, -1)


def second_selector(local):
    select = np.zeros((3, 3, 2, SUBLANES, local + 2, 2, TAP_PAD), np.float32)
    for b in range(3):
        for c in range(3):
            for d in range(3):
                tap = (b * 3 + c) * 3 + d
                for branch in range(2):
                    for cell in range(local):
                        select[c, d, branch, cell, cell + b, branch, tap] = 1
    return select.reshape(18 * SUBLANES, -1)


def unit(features):
    positive = jnp.maximum(features.astype(F32), 0.0)
    length = jnp.sqrt(jnp.sum(positive * positive, axis=-1, keepdims=True) + 1e-06)
    return (positive / length).astype(BF16)


def split(value):
    high = value.astype(BF16)
    return high, (value - high.astype(F32)).astype(BF16)


def prepare_kernel(
    devices, target_ref, first_ref, second_ref, pick_ref, spread_ref, gate_ref,
    unit_ref, first_out, second_out, taps_ref,
):
    rows, columns = target_ref.shape[:2]
    for row in range(rows):
        unit_ref[row * columns : (row + 1) * columns] = unit(target_ref[row])
    hid = first_ref.shape[-1]
    taps_ref[...] = jnp.zeros(taps_ref.shape, F32)
    for number, ref in enumerate((first_ref, second_ref)):
        base = 2 * TAP_PAD * number
        for b in range(3):
            for c in range(3):
                start = base + (b * 3 + c) * 3
                taps_ref[start : start + 3, :hid] = ref[1, b, c]
        for c in range(3):
            for d in range(3):
                piece = ref[c, d, 1]
                for b in range(3):
                    start = base + TAP_PAD + (b * 3 + c) * 3 + d
                    taps_ref[start : start + 1, :hid] = piece[b : b + 1]
    branches = [taps_ref[i * TAP_PAD : (i + 1) * TAP_PAD, :hid] for i in range(4)]
    width = first_out.shape[1]
    taps = jnp.concatenate(split(jnp.concatenate(branches[:2], axis=1)), axis=0)
    blocks = first_out.shape[0] // (2 * hid)
    for block in range(blocks):
        piece = lax.dot_general(
            taps, pick_ref[:, block * width : (block + 1) * width],
            (((0,), (0,)), ((), ())), preferred_element_type=F32,
        )
        if block == 0:
            piece = piece * jnp.where(lax.axis_index("tgt") == 0, 0.0, 1.0)
        if block == blocks - 1:
            piece = piece * jnp.where(lax.axis_index("tgt") == devices - 1, 0.0, 1.0)
        first_out[block * 2 * hid : (block + 1) * 2 * hid] = piece.astype(BF16)
    depth = blocks * 2 * hid
    groups = blocks * 2
    row_group = lax.broadcasted_iota(jnp.int32, (groups * TAP_PAD, depth), 0) // TAP_PAD
    lane_group = lax.broadcasted_iota(jnp.int32, (groups * TAP_PAD, depth), 1) // hid
    tiled = jnp.concatenate([jnp.concatenate(branches[2:], axis=1)] * blocks, axis=1)
    tiled = jnp.concatenate([tiled] * groups, axis=0)
    tiled = jnp.where(row_group == lane_group, tiled, 0.0)
    high, low = split(tiled)
    half = second_out.shape[0] // 2
    high = jnp.dot(spread_ref[...], high, preferred_element_type=F32).astype(BF16)
    low = jnp.dot(spread_ref[...], low, preferred_element_type=F32).astype(BF16)
    second_out[:half, :depth] = high
    second_out[:half, depth:] = high
    second_out[half:, :depth] = low
    second_out[half:, depth:] = jnp.zeros_like(low)


def spread_kernel(
    source_ref, target_ref, pick_ref, scatter_ref,
    out_ref, target_out, pick_out, scatter_out, source_copy, sems,
):
    copies = [
        pltpu.make_async_copy(start, end, sems.at[number])
        for number, (start, end) in enumerate(
            (
                (source_ref, source_copy),
                (target_ref, target_out),
                (pick_ref, pick_out),
                (scatter_ref, scatter_out),
            )
        )
    ]
    for copy in copies:
        copy.start()
    copies[0].wait()
    half = out_ref.shape[2]
    for device in range(out_ref.shape[0]):
        start = device % 2 * half
        out_ref[device] = source_copy[:, start : start + half]
    for copy in copies[1:]:
        copy.wait()


def match_kernel(
    local, mine_ref, other_ref, target_ref, send_ref, source_ref, order_ref
):
    rows, padded, columns = order_ref.shape
    cells = padded - 2 * SUBLANES
    half = mine_ref.shape[1]
    side = lax.axis_index("tgt") % 2
    block = min(cells, 32)
    for first in range(0, cells, block):
        halves = [
            jnp.maximum(ref[first : first + block].astype(F32), 0.0)
            for ref in (mine_ref, other_ref)
        ]
        squares = [jnp.sum(piece * piece, axis=-1, keepdims=True) for piece in halves]
        length = jnp.sqrt(squares[0] + squares[1] + 1e-06)
        for number, piece in enumerate(halves):
            start = pl.multiple_of((side ^ number) * half, half)
            source_ref[first : first + block, pl.ds(start, half)] = (piece / length).astype(BF16)
    correlation = lax.dot_general(
        source_ref[...], target_ref[...], (((1,), (1,)), ((), ())), preferred_element_type=F32
    )
    window = max(SUBLANES, local + 4)
    blank = jnp.zeros((SUBLANES, columns), F32)
    for row in range(rows):
        order_ref[row, :SUBLANES, :] = blank
        order_ref[row, SUBLANES + cells :, :] = blank
        order_ref[row, SUBLANES : SUBLANES + cells, :] = correlation[
            :, row * columns : (row + 1) * columns
        ]
        source_best = jnp.max(order_ref[row], axis=0, keepdims=True)
        inverse = 1.0 / (source_best + EPSILON)
        for target in range(send_ref.shape[0]):
            first = SUBLANES + target * local - 2
            send_ref[target, row * window : (row + 1) * window, 0, :] = order_ref[
                row, first : first + window, :
            ]
            place = rows * window + row
            send_ref[target, place : place + 1, 0, :] = inverse


def row_of_column(column, lanes):
    row = lax.broadcasted_iota(jnp.int32, (column.shape[0], lanes), 0)
    lane = lax.broadcasted_iota(jnp.int32, (column.shape[0], lanes), 1)
    return jnp.sum(jnp.where(row == lane, column, 0.0), axis=0, keepdims=True)


def column_of_row(values, count):
    row = lax.broadcasted_iota(jnp.int32, (count, values.shape[1]), 0)
    lane = lax.broadcasted_iota(jnp.int32, (count, values.shape[1]), 1)
    return jnp.sum(jnp.where(row == lane, values, 0.0), axis=1, keepdims=True)


def lane_shifts(value):
    lanes = value.shape[-1]
    lane = lax.broadcasted_iota(jnp.int32, value.shape, value.ndim - 1)
    axis = value.ndim - 1
    left = jnp.where(lane == 0, 0.0, pltpu.roll(value, 1, axis))
    right = jnp.where(lane == lanes - 1, 0.0, pltpu.roll(value, lanes - 1, axis))
    return left, right


def consensus_kernel(
    parts, local, rows, came_ref, first_ref, second_ref, send_ref, tile_ref, partial_ref, rows_ref
):
    devices, columns = came_ref.shape[0], came_ref.shape[3]
    window = max(SUBLANES, local + 4)
    grid_rows = devices * rows
    tile = len(ORDER) * SUBLANES
    again = REPEATED * SUBLANES
    zero = jnp.zeros((SUBLANES, columns), F32)

    def piece_of(device, row, first):
        return rows_ref[device * rows + row, first : first + SUBLANES, :]

    def survey(device, best):
        best = list(best)
        for row in range(rows):
            block = came_ref[device, row * window : (row + 1) * window, 0, :]
            rows_ref[device * rows + row, :window] = block
            for number, (first, _, _) in enumerate(parts):
                best[number] = jnp.maximum(best[number], block[first : first + SUBLANES])
        return tuple(best)

    best = lax.fori_loop(0, devices, survey, (zero,) * len(parts), unroll=4)
    scales = [
        jnp.broadcast_to(1.0 / (jnp.max(most, axis=1, keepdims=True) + EPSILON), most.shape)
        for most in best
    ]

    blank = jnp.zeros((tile, columns), BF16)
    for number in range(len(parts)):
        tile_ref[0, number] = blank

    def build(device, present):
        source = jnp.minimum(device, devices - 1)
        for row in range(rows):
            place = rows * window + row
            inverse = came_ref[source, place : place + 1, 0, :] * present
            for number, (first, _, _) in enumerate(parts):
                value = piece_of(source, row, first)
                value = value * (value * inverse) * (value * scales[number])
                left, right = lane_shifts(value)
                moved = (left, value, right)
                high = [piece.astype(BF16).astype(F32) for piece in moved]
                low = [piece - rounded for piece, rounded in zip(moved, high)]
                stacked = jnp.concatenate(
                    [(low if part else high)[offset] for offset, part in ORDER], axis=0
                )
                tile_ref[device * rows + row + 1, number] = stacked.astype(BF16)

    partial_rows = second_ref.shape[0] // 2
    empty = jnp.zeros((partial_rows, columns), F32)
    partial_ref[0] = empty
    partial_ref[grid_rows + 1] = empty

    def layers(device):
        base = device * rows
        hidden = []
        offset = 0
        for number, (_, _, size) in enumerate(parts):
            taps = []
            for side in range(rows):
                pieces = [tile_ref[base + side + c, number] for c in range(3)]
                pieces += [tile_ref[base + side + c, number, :again] for c in range(3)]
                taps.append(jnp.concatenate(pieces, axis=0))
            count = size * first_ref.shape[0] // (local + 2)
            hidden.append(
                jnp.dot(
                    first_ref[offset : offset + count],
                    jnp.concatenate(taps, axis=1),
                    preferred_element_type=F32,
                )
            )
            offset += count
        halves = [split(jnp.maximum(piece, 0.0)) for piece in hidden]
        pair = jnp.concatenate([high for high, _ in halves] + [low for _, low in halves], axis=0)
        partial = jnp.dot(second_ref[...], pair, preferred_element_type=F32)
        partial = partial[:partial_rows] + partial[partial_rows:]
        for side in range(rows):
            partial_ref[base + side + 1] = partial[:, side * columns : (side + 1) * columns]

    def gather(device, most):
        for row in range(rows):
            total = None
            for branch in range(2):
                sums = []
                for d in range(3):
                    value = None
                    for c in range(3):
                        start = ((c * 3 + d) * 2 + branch) * SUBLANES
                        piece = partial_ref[device * rows + row + c, start : start + SUBLANES, :]
                        value = piece if value is None else value + piece
                    sums.append(value)
                output = lane_shifts(sums[0])[0] + sums[1] + lane_shifts(sums[2])[1]
                output = jnp.maximum(output, 0.0)
                total = output if total is None else total + output
            send_ref[device, row * SUBLANES : (row + 1) * SUBLANES, 0, :] = total
            most = jnp.maximum(most, total)
        return most

    def present(device):
        return jnp.where(device < devices, 1.0, 0.0).astype(F32)

    build(0, 1.0)
    build(1, 1.0)
    layers(0)
    build(2, present(2))
    layers(1)
    build(3, present(3))

    def step(device, most):
        most = gather(device - 2, most)
        build(device + 2, present(device + 2))
        layers(device)
        return most

    most = lax.fori_loop(2, devices, step, zero, unroll=2)
    most = gather(devices - 2, most)
    most = gather(devices - 1, most)
    best = jnp.max(most, axis=1, keepdims=True)
    scale = row_of_column(1.0 / (best + EPSILON), columns)
    for device in range(devices):
        send_ref[device, rows * SUBLANES : rows * SUBLANES + 1, 0, :] = scale


def finish_kernel(local, came_ref, out_ref):
    devices = came_ref.shape[0]
    rows = out_ref.shape[1]
    place = rows * SUBLANES
    scales = [
        column_of_row(came_ref[device, place : place + 1, 0, :], SUBLANES)
        for device in range(devices)
    ]
    for row in range(rows):
        first = row * SUBLANES
        most = came_ref[0, first : first + SUBLANES, 0, :]
        for device in range(1, devices):
            most = jnp.maximum(most, came_ref[device, first : first + SUBLANES, 0, :])
        inverse = 1.0 / (jnp.max(most, axis=0, keepdims=True) + EPSILON)
        for device in range(devices):
            value = came_ref[device, first : first + SUBLANES, 0, :]
            value = value * (value * inverse) * (value * scales[device])
            out_ref[device * local : (device + 1) * local, row, :] = value[:local]


def exchange(slots):
    return lax.all_to_all(slots, "tgt", 0, 0, tiled=True)


def room(*shapes):
    scratch = sum(int(np.prod(shape)) * jnp.dtype(kind).itemsize for shape, kind in shapes)
    return pltpu.CompilerParams(vmem_limit_bytes=scratch + 6 * 2**20)


VMEM = pl.BlockSpec(memory_space=pltpu.VMEM)
ANY = pl.BlockSpec(memory_space=pltpu.HBM)


def shards(source_features, target_features, conv_first, conv_second):
    devices = lax.axis_size("tgt")
    rows, columns, channels = target_features.shape
    cells = source_features.shape[0] * devices
    hid = conv_first.shape[0]
    local = cells // devices
    parts = parts_of(local)
    hidden = local + 2
    window = max(SUBLANES, local + 4)
    tile = len(ORDER) * SUBLANES
    width = 3 * (tile + REPEATED * SUBLANES)
    depth = hidden * 2 * hid
    assert local <= SUBLANES and rows * devices % 4 == 0

    pick = jnp.asarray(first_selector(parts), BF16)
    scatter = jnp.asarray(second_selector(local), BF16)
    spread, target_features, pick, scatter = pl.pallas_call(
        spread_kernel,
        out_shape=(
            jax.ShapeDtypeStruct((devices, source_features.shape[0], channels // 2), BF16),
            jax.ShapeDtypeStruct(target_features.shape, BF16),
            jax.ShapeDtypeStruct(pick.shape, BF16),
            jax.ShapeDtypeStruct(scatter.shape, BF16),
        ),
        in_specs=[ANY] * 4,
        out_specs=(VMEM,) * 4,
        scratch_shapes=[
            pltpu.VMEM(source_features.shape, BF16),
            pltpu.SemaphoreType.DMA((4,)),
        ],
        compiler_params=room(),
        name="spread",
    )(
        *(
            pltpu.with_memory_space_constraint(value, pltpu.HBM)
            for value in (source_features, target_features, pick, scatter)
        )
    )
    mine = exchange(spread).reshape(cells, channels // 2)
    other = lax.ppermute(mine, "tgt", [(i, i ^ 1) for i in range(devices)])

    second_rows = 18 * SUBLANES
    target_unit, first_weights, second_weights = pl.pallas_call(
        functools.partial(prepare_kernel, devices),
        out_shape=(
            jax.ShapeDtypeStruct((rows * columns, channels), BF16),
            jax.ShapeDtypeStruct((depth, width), BF16),
            jax.ShapeDtypeStruct((2 * second_rows, 2 * depth), BF16),
        ),
        in_specs=[VMEM] * 5 + [pl.BlockSpec(memory_space=pl.ANY)],
        out_specs=(VMEM,) * 3,
        scratch_shapes=[pltpu.VMEM((4 * TAP_PAD, 128), F32)],
        cost_estimate=pl.CostEstimate(flops=10**6, bytes_accessed=2 * 10**6, transcendentals=0),
        compiler_params=room(),
        name="prepare",
    )(
        target_features,
        jnp.transpose(conv_first, (1, 2, 3, 4, 0)),
        jnp.transpose(conv_second, (1, 2, 3, 4, 0)),
        pick,
        scatter,
        mine,
    )

    slots = pl.pallas_call(
        functools.partial(match_kernel, local),
        out_shape=jax.ShapeDtypeStruct((devices, rows * window + rows, 1, columns), F32),
        in_specs=[VMEM] * 3,
        out_specs=VMEM,
        scratch_shapes=[
            pltpu.VMEM((cells, channels), BF16),
            pltpu.VMEM((rows, cells + 2 * SUBLANES, columns), F32),
        ],
        compiler_params=room(),
        name="match",
    )(mine, other, target_unit)

    stores = (
        ((rows * (devices + 2) + 2, len(parts), tile, columns), BF16),
        ((rows * devices + 2, second_rows, columns), F32),
        ((rows * devices, -(-window // SUBLANES) * SUBLANES, columns), F32),
    )
    slots = pl.pallas_call(
        functools.partial(consensus_kernel, parts, local, rows),
        out_shape=jax.ShapeDtypeStruct((devices, rows * SUBLANES + 1, 1, columns), F32),
        in_specs=[VMEM] * 3,
        out_specs=VMEM,
        scratch_shapes=[pltpu.VMEM(shape, kind) for shape, kind in stores],
        compiler_params=room(*stores),
        name="consensus",
    )(exchange(slots), first_weights, second_weights)

    filtered = pl.pallas_call(
        functools.partial(finish_kernel, local),
        out_shape=jax.ShapeDtypeStruct((cells, rows, columns), F32),
        in_specs=[VMEM],
        out_specs=VMEM,
        compiler_params=room(),
        name="finish",
    )(exchange(slots))
    return filtered[None]


def solution(mesh):
    placed = (P(("pairs", "tgt"), None), P(("pairs", "tgt"), None, None), P(), P())
    return jax.shard_map(
        shards, mesh=mesh, in_specs=placed, out_specs=P("pairs", None, "tgt", None), check_vma=False
    )
```

```python
import functools

import jax
import jax.numpy as jnp
import numpy as np
from jax import lax
from jax.experimental import pallas as pl
from jax.experimental.pallas import tpu as pltpu
from jax.sharding import PartitionSpec as P

EPSILON = 1e-05
TINY = 1e-30
F32 = jnp.float32
BF16 = jnp.bfloat16
TAP_PAD = 32
SUBLANES = 8
ORDER = ((0, 0), (1, 0), (2, 0), (0, 1), (1, 1), (2, 1))
REPEATED = 4


def whole_tiles(count):
    return -(-count // SUBLANES) * SUBLANES


def parts_of(local):
    hidden = local + 2
    count = -(-hidden // (SUBLANES - 2))
    size = -(-hidden // count)
    parts = []
    for start in range(0, hidden, size):
        first = min(start, max(0, local + 4 - SUBLANES))
        parts.append((first, start, min(size, hidden - start)))
    return parts


def first_selector(parts):
    tile = len(ORDER) * SUBLANES
    width = 3 * (tile + REPEATED * SUBLANES)
    blocks = [(first, hidden) for first, start, size in parts for hidden in range(start, start + size)]
    select = np.zeros((2 * TAP_PAD, len(blocks), width), np.float32)
    for number, (first, hidden) in enumerate(blocks):
        for b in range(3):
            for c in range(3):
                for d in range(3):
                    tap = (b * 3 + c) * 3 + d
                    for place, (offset, low) in enumerate(ORDER):
                        if offset != d:
                            continue
                        row = place * SUBLANES + hidden + b - first
                        select[tap, number, c * tile + row] = 1
                        if not low:
                            column = 3 * tile + c * REPEATED * SUBLANES + row
                            select[TAP_PAD + tap, number, column] = 1
    return select.reshape(2 * TAP_PAD, -1)


def second_selector(local):
    select = np.zeros((3, 3, 2, SUBLANES, local + 2, 2, TAP_PAD), np.float32)
    for b in range(3):
        for c in range(3):
            for d in range(3):
                tap = (b * 3 + c) * 3 + d
                for branch in range(2):
                    for cell in range(local):
                        select[c, d, branch, cell, cell + b, branch, tap] = 1
    return select.reshape(18 * SUBLANES, -1)


def unit(features):
    positive = jnp.maximum(features.astype(F32), 0.0)
    length = jnp.sqrt(jnp.sum(positive * positive, axis=-1, keepdims=True) + 1e-06)
    return (positive / length).astype(BF16)


def split(value):
    high = value.astype(BF16)
    return high, (value - high.astype(F32)).astype(BF16)


def prepare_kernel(
    devices, target_ref, first_ref, second_ref, pick_ref, spread_ref, gate_ref,
    unit_ref, first_out, second_out, taps_ref,
):
    rows, columns = target_ref.shape[:2]
    for row in range(rows):
        unit_ref[row * columns : (row + 1) * columns] = unit(target_ref[row])
    hid = first_ref.shape[-1]
    taps_ref[...] = jnp.zeros(taps_ref.shape, F32)
    for number, ref in enumerate((first_ref, second_ref)):
        base = 2 * TAP_PAD * number
        for b in range(3):
            for c in range(3):
                start = base + (b * 3 + c) * 3
                taps_ref[start : start + 3, :hid] = ref[1, b, c]
        for c in range(3):
            for d in range(3):
                piece = ref[c, d, 1]
                for b in range(3):
                    start = base + TAP_PAD + (b * 3 + c) * 3 + d
                    taps_ref[start : start + 1, :hid] = piece[b : b + 1]
    branches = [taps_ref[i * TAP_PAD : (i + 1) * TAP_PAD, :hid] for i in range(4)]
    width = first_out.shape[1]
    taps = jnp.concatenate(split(jnp.concatenate(branches[:2], axis=1)), axis=0)
    blocks = first_out.shape[0] // (2 * hid)
    for block in range(blocks):
        piece = lax.dot_general(
            taps, pick_ref[:, block * width : (block + 1) * width],
            (((0,), (0,)), ((), ())), preferred_element_type=F32,
        )
        if block == 0:
            piece = piece * jnp.where(lax.axis_index("tgt") == 0, 0.0, 1.0)
        if block == blocks - 1:
            piece = piece * jnp.where(lax.axis_index("tgt") == devices - 1, 0.0, 1.0)
        first_out[block * 2 * hid : (block + 1) * 2 * hid] = piece.astype(BF16)
    depth = blocks * 2 * hid
    groups = blocks * 2
    row_group = lax.broadcasted_iota(jnp.int32, (groups * TAP_PAD, depth), 0) // TAP_PAD
    lane_group = lax.broadcasted_iota(jnp.int32, (groups * TAP_PAD, depth), 1) // hid
    tiled = jnp.concatenate([jnp.concatenate(branches[2:], axis=1)] * blocks, axis=1)
    tiled = jnp.concatenate([tiled] * groups, axis=0)
    tiled = jnp.where(row_group == lane_group, tiled, 0.0)
    high, low = split(tiled)
    half = second_out.shape[0] // 2
    high = jnp.dot(spread_ref[...], high, preferred_element_type=F32).astype(BF16)
    low = jnp.dot(spread_ref[...], low, preferred_element_type=F32).astype(BF16)
    second_out[:half, :depth] = high
    second_out[:half, depth:] = high
    second_out[half:, :depth] = low
    second_out[half:, depth:] = jnp.zeros_like(low)


def spread_kernel(
    source_ref, target_ref, pick_ref, scatter_ref,
    out_ref, target_out, pick_out, scatter_out, source_copy, sems,
):
    copies = [
        pltpu.make_async_copy(start, end, sems.at[number])
        for number, (start, end) in enumerate(
            (
                (source_ref, source_copy),
                (target_ref, target_out),
                (pick_ref, pick_out),
                (scatter_ref, scatter_out),
            )
        )
    ]
    for copy in copies:
        copy.start()
    copies[0].wait()
    half = out_ref.shape[2]
    for device in range(out_ref.shape[0]):
        start = device % 2 * half
        out_ref[device] = source_copy[:, start : start + half]
    for copy in copies[1:]:
        copy.wait()


def match_kernel(
    local, mine_ref, other_ref, target_ref, send_ref, source_ref, order_ref
):
    rows, padded, columns = order_ref.shape
    cells = padded - 2 * SUBLANES
    half = mine_ref.shape[1]
    side = lax.axis_index("tgt") % 2
    block = min(cells, 32)
    for first in range(0, cells, block):
        halves = [
            jnp.maximum(ref[first : first + block].astype(F32), 0.0)
            for ref in (mine_ref, other_ref)
        ]
        squares = [jnp.sum(piece * piece, axis=-1, keepdims=True) for piece in halves]
        length = jnp.sqrt(squares[0] + squares[1] + 1e-06)
        for number, piece in enumerate(halves):
            start = pl.multiple_of((side ^ number) * half, half)
            source_ref[first : first + block, pl.ds(start, half)] = (piece / length).astype(BF16)
    correlation = lax.dot_general(
        source_ref[...], target_ref[...], (((1,), (1,)), ((), ())), preferred_element_type=F32
    )
    window = max(SUBLANES, local + 4)
    blank = jnp.zeros((SUBLANES, columns), F32)
    for row in range(rows):
        order_ref[row, :SUBLANES, :] = blank
        order_ref[row, SUBLANES + cells :, :] = blank
        order_ref[row, SUBLANES : SUBLANES + cells, :] = correlation[
            :, row * columns : (row + 1) * columns
        ]
        source_best = jnp.max(order_ref[row], axis=0, keepdims=True)
        scale = 1.0 / jnp.maximum(source_best, TINY)
        root = jnp.concatenate(root_rows(source_best), axis=0)
        place = rows * window + 2 * row
        for target in range(send_ref.shape[0]):
            first = SUBLANES + target * local - 2
            send_ref[target, row * window : (row + 1) * window] = (
                order_ref[row, first : first + window, :] * scale
            )
            send_ref[target, place : place + 2] = root
    used = rows * (window + 2)
    spare = send_ref.shape[1] - used
    if spare:
        for target in range(send_ref.shape[0]):
            send_ref[target, used:] = jnp.zeros((spare, columns), F32)


def root_rows(best):
    root = jnp.sqrt(jnp.sqrt(jnp.sqrt(best)))
    high = root.astype(BF16).astype(F32)
    return high, root - high


def best_of_root(rows):
    root = rows[:1] + rows[1:]
    for _ in range(3):
        root = root * root
    return root


def row_of_column(column, lanes):
    row = lax.broadcasted_iota(jnp.int32, (column.shape[0], lanes), 0)
    lane = lax.broadcasted_iota(jnp.int32, (column.shape[0], lanes), 1)
    return jnp.sum(jnp.where(row == lane, column, 0.0), axis=0, keepdims=True)


def column_of_row(values, count):
    row = lax.broadcasted_iota(jnp.int32, (count, values.shape[1]), 0)
    lane = lax.broadcasted_iota(jnp.int32, (count, values.shape[1]), 1)
    return jnp.sum(jnp.where(row == lane, values, 0.0), axis=1, keepdims=True)


def lane_shifts(value):
    lanes = value.shape[-1]
    lane = lax.broadcasted_iota(jnp.int32, value.shape, value.ndim - 1)
    axis = value.ndim - 1
    left = jnp.where(lane == 0, 0.0, pltpu.roll(value, 1, axis))
    right = jnp.where(lane == lanes - 1, 0.0, pltpu.roll(value, lanes - 1, axis))
    return left, right


def consensus_kernel(
    parts, local, rows, came_ref, first_ref, second_ref, send_ref, tile_ref, partial_ref, rows_ref
):
    devices, _, columns = came_ref.shape
    window = max(SUBLANES, local + 4)
    grid_rows = devices * rows
    tile = len(ORDER) * SUBLANES
    again = REPEATED * SUBLANES
    zero = jnp.zeros((SUBLANES, columns), F32)

    def piece_of(device, row, first):
        return rows_ref[device * rows + row, first : first + SUBLANES, :]

    def survey(device, best):
        best = list(best)
        for row in range(rows):
            place = rows * window + 2 * row
            largest = best_of_root(came_ref[device, place : place + 2])
            block = came_ref[device, row * window : (row + 1) * window] * largest
            rows_ref[device * rows + row, :window] = block
            rows_ref[device * rows + row, window : window + 1] = 1.0 / (largest + EPSILON)
            for number, (first, _, _) in enumerate(parts):
                best[number] = jnp.maximum(best[number], block[first : first + SUBLANES])
        return tuple(best)

    best = lax.fori_loop(0, devices, survey, (zero,) * len(parts), unroll=4)
    scales = [
        jnp.broadcast_to(1.0 / (jnp.max(most, axis=1, keepdims=True) + EPSILON), most.shape)
        for most in best
    ]

    blank = jnp.zeros((tile, columns), BF16)
    for number in range(len(parts)):
        tile_ref[0, number] = blank

    def build(device, present):
        source = jnp.minimum(device, devices - 1)
        for row in range(rows):
            inverse = rows_ref[source * rows + row, window : window + 1, :] * present
            for number, (first, _, _) in enumerate(parts):
                value = piece_of(source, row, first)
                value = value * (value * inverse) * (value * scales[number])
                left, right = lane_shifts(value)
                moved = (left, value, right)
                high = [piece.astype(BF16).astype(F32) for piece in moved]
                low = [piece - rounded for piece, rounded in zip(moved, high)]
                stacked = jnp.concatenate(
                    [(low if part else high)[offset] for offset, part in ORDER], axis=0
                )
                tile_ref[device * rows + row + 1, number] = stacked.astype(BF16)

    partial_rows = second_ref.shape[0] // 2
    empty = jnp.zeros((partial_rows, columns), F32)
    partial_ref[0] = empty
    partial_ref[grid_rows + 1] = empty

    def layers(device):
        base = device * rows
        hidden = []
        offset = 0
        for number, (_, _, size) in enumerate(parts):
            taps = []
            for side in range(rows):
                pieces = [tile_ref[base + side + c, number] for c in range(3)]
                pieces += [tile_ref[base + side + c, number, :again] for c in range(3)]
                taps.append(jnp.concatenate(pieces, axis=0))
            count = size * first_ref.shape[0] // (local + 2)
            hidden.append(
                jnp.dot(
                    first_ref[offset : offset + count],
                    jnp.concatenate(taps, axis=1),
                    preferred_element_type=F32,
                )
            )
            offset += count
        halves = [split(jnp.maximum(piece, 0.0)) for piece in hidden]
        pair = jnp.concatenate([high for high, _ in halves] + [low for _, low in halves], axis=0)
        partial = jnp.dot(second_ref[...], pair, preferred_element_type=F32)
        partial = partial[:partial_rows] + partial[partial_rows:]
        for side in range(rows):
            partial_ref[base + side + 1] = partial[:, side * columns : (side + 1) * columns]

    def gather(device, most):
        for row in range(rows):
            total = None
            for branch in range(2):
                sums = []
                for d in range(3):
                    value = None
                    for c in range(3):
                        start = ((c * 3 + d) * 2 + branch) * SUBLANES
                        piece = partial_ref[device * rows + row + c, start : start + SUBLANES, :]
                        value = piece if value is None else value + piece
                    sums.append(value)
                output = lane_shifts(sums[0])[0] + sums[1] + lane_shifts(sums[2])[1]
                output = jnp.maximum(output, 0.0)
                total = output if total is None else total + output
            send_ref[device, row * SUBLANES : (row + 1) * SUBLANES] = total
            most = jnp.maximum(most, total)
        return most

    def present(device):
        return jnp.where(device < devices, 1.0, 0.0).astype(F32)

    build(0, 1.0)
    build(1, 1.0)
    layers(0)
    build(2, present(2))
    layers(1)
    build(3, present(3))

    def step(device, most):
        most = gather(device - 2, most)
        build(device + 2, present(device + 2))
        layers(device)
        return most

    most = lax.fori_loop(2, devices, step, zero, unroll=2)
    most = gather(devices - 2, most)
    most = gather(devices - 1, most)
    best = jnp.max(most, axis=1, keepdims=True)
    scale = 1.0 / jnp.maximum(best, TINY)
    root = jnp.concatenate(
        [row_of_column(piece, columns) for piece in root_rows(best)]
        + [jnp.zeros((SUBLANES - 2, columns), F32)],
        axis=0,
    )
    for device in range(devices):
        for row in range(rows):
            start = row * SUBLANES
            send_ref[device, start : start + SUBLANES] = (
                send_ref[device, start : start + SUBLANES] * scale
            )
        send_ref[device, rows * SUBLANES :] = root


def finish_kernel(local, came_ref, out_ref):
    devices, _, columns = came_ref.shape
    rows = out_ref.shape[1]
    place = rows * SUBLANES
    bests = [
        column_of_row(best_of_root(came_ref[device, place : place + 2]), SUBLANES)
        for device in range(devices)
    ]
    for row in range(rows):
        first = row * SUBLANES
        most = jnp.zeros((SUBLANES, columns), F32)
        for device in range(devices):
            most = jnp.maximum(most, came_ref[device, first : first + SUBLANES] * bests[device])
        inverse = 1.0 / (jnp.max(most, axis=0, keepdims=True) + EPSILON)
        for device in range(devices):
            value = came_ref[device, first : first + SUBLANES] * bests[device]
            value = value * (value * inverse) * (value * (1.0 / (bests[device] + EPSILON)))
            out_ref[device * local : (device + 1) * local, row, :] = value[:local]


def exchange(slots):
    return lax.all_to_all(slots, "tgt", 0, 0, tiled=True)


def exchange_relative(slots):
    return exchange(slots.astype(jnp.float16)).astype(F32)


def room(*shapes):
    scratch = sum(int(np.prod(shape)) * jnp.dtype(kind).itemsize for shape, kind in shapes)
    return pltpu.CompilerParams(vmem_limit_bytes=scratch + 6 * 2**20)


VMEM = pl.BlockSpec(memory_space=pltpu.VMEM)
ANY = pl.BlockSpec(memory_space=pltpu.HBM)


def shards(source_features, target_features, conv_first, conv_second):
    devices = lax.axis_size("tgt")
    rows, columns, channels = target_features.shape
    cells = source_features.shape[0] * devices
    hid = conv_first.shape[0]
    local = cells // devices
    parts = parts_of(local)
    hidden = local + 2
    window = max(SUBLANES, local + 4)
    tile = len(ORDER) * SUBLANES
    width = 3 * (tile + REPEATED * SUBLANES)
    depth = hidden * 2 * hid
    assert local <= SUBLANES and rows * devices % 4 == 0

    pick = jnp.asarray(first_selector(parts), BF16)
    scatter = jnp.asarray(second_selector(local), BF16)
    spread, target_features, pick, scatter = pl.pallas_call(
        spread_kernel,
        out_shape=(
            jax.ShapeDtypeStruct((devices, source_features.shape[0], channels // 2), BF16),
            jax.ShapeDtypeStruct(target_features.shape, BF16),
            jax.ShapeDtypeStruct(pick.shape, BF16),
            jax.ShapeDtypeStruct(scatter.shape, BF16),
        ),
        in_specs=[ANY] * 4,
        out_specs=(VMEM,) * 4,
        scratch_shapes=[
            pltpu.VMEM(source_features.shape, BF16),
            pltpu.SemaphoreType.DMA((4,)),
        ],
        compiler_params=room(),
        name="spread",
    )(
        *(
            pltpu.with_memory_space_constraint(value, pltpu.HBM)
            for value in (source_features, target_features, pick, scatter)
        )
    )
    mine = exchange(spread).reshape(cells, channels // 2)
    other = lax.ppermute(mine, "tgt", [(i, i ^ 1) for i in range(devices)])

    second_rows = 18 * SUBLANES
    target_unit, first_weights, second_weights = pl.pallas_call(
        functools.partial(prepare_kernel, devices),
        out_shape=(
            jax.ShapeDtypeStruct((rows * columns, channels), BF16),
            jax.ShapeDtypeStruct((depth, width), BF16),
            jax.ShapeDtypeStruct((2 * second_rows, 2 * depth), BF16),
        ),
        in_specs=[VMEM] * 5 + [pl.BlockSpec(memory_space=pl.ANY)],
        out_specs=(VMEM,) * 3,
        scratch_shapes=[pltpu.VMEM((4 * TAP_PAD, 128), F32)],
        cost_estimate=pl.CostEstimate(flops=10**6, bytes_accessed=2 * 10**6, transcendentals=0),
        compiler_params=room(),
        name="prepare",
    )(
        target_features,
        jnp.transpose(conv_first, (1, 2, 3, 4, 0)),
        jnp.transpose(conv_second, (1, 2, 3, 4, 0)),
        pick,
        scatter,
        mine,
    )

    slots = pl.pallas_call(
        functools.partial(match_kernel, local),
        out_shape=jax.ShapeDtypeStruct((devices, whole_tiles(rows * (window + 2)), columns), F32),
        in_specs=[VMEM] * 3,
        out_specs=VMEM,
        scratch_shapes=[
            pltpu.VMEM((cells, channels), BF16),
            pltpu.VMEM((rows, cells + 2 * SUBLANES, columns), F32),
        ],
        compiler_params=room(),
        name="match",
    )(mine, other, target_unit)

    stores = (
        ((rows * (devices + 2) + 2, len(parts), tile, columns), BF16),
        ((rows * devices + 2, second_rows, columns), F32),
        ((rows * devices, whole_tiles(window + 1), columns), F32),
    )
    slots = pl.pallas_call(
        functools.partial(consensus_kernel, parts, local, rows),
        out_shape=jax.ShapeDtypeStruct((devices, (rows + 1) * SUBLANES, columns), F32),
        in_specs=[VMEM] * 3,
        out_specs=VMEM,
        scratch_shapes=[pltpu.VMEM(shape, kind) for shape, kind in stores],
        compiler_params=room(*stores),
        name="consensus",
    )(exchange_relative(slots), first_weights, second_weights)

    filtered = pl.pallas_call(
        functools.partial(finish_kernel, local),
        out_shape=jax.ShapeDtypeStruct((cells, rows, columns), F32),
        in_specs=[VMEM],
        out_specs=VMEM,
        compiler_params=room(),
        name="finish",
    )(exchange_relative(slots))
    return filtered[None]


def solution(mesh):
    placed = (P(("pairs", "tgt"), None), P(("pairs", "tgt"), None, None), P(), P())
    return jax.shard_map(
        shards, mesh=mesh, in_specs=placed, out_specs=P("pairs", None, "tgt", None), check_vma=False
    )
```

```python
import functools

import jax
import jax.numpy as jnp
import numpy as np
from jax import lax
from jax.experimental import pallas as pl
from jax.experimental.pallas import tpu as pltpu
from jax.sharding import PartitionSpec as P

EPSILON = 1e-05
TINY = 1e-30
MATRIX = 256
F32 = jnp.float32
BF16 = jnp.bfloat16
TAP_PAD = 32
SUBLANES = 8
ORDER = ((0, 0), (1, 0), (2, 0), (0, 1), (1, 1), (2, 1))
REPEATED = 4


def whole_tiles(count):
    return -(-count // SUBLANES) * SUBLANES


def parts_of(local):
    hidden = local + 2
    count = -(-hidden // (SUBLANES - 2))
    size = -(-hidden // count)
    parts = []
    for start in range(0, hidden, size):
        first = min(start, max(0, local + 4 - SUBLANES))
        parts.append((first, start, min(size, hidden - start)))
    return parts


def first_selector(parts):
    tile = len(ORDER) * SUBLANES
    width = 3 * (tile + REPEATED * SUBLANES)
    blocks = [(first, hidden) for first, start, size in parts for hidden in range(start, start + size)]
    select = np.zeros((2 * TAP_PAD, len(blocks), width), np.float32)
    for number, (first, hidden) in enumerate(blocks):
        for b in range(3):
            for c in range(3):
                for d in range(3):
                    tap = (b * 3 + c) * 3 + d
                    for place, (offset, low) in enumerate(ORDER):
                        if offset != d:
                            continue
                        row = place * SUBLANES + hidden + b - first
                        select[tap, number, c * tile + row] = 1
                        if not low:
                            column = 3 * tile + c * REPEATED * SUBLANES + row
                            select[TAP_PAD + tap, number, column] = 1
    return select.reshape(2 * TAP_PAD, -1)


def second_selector(local):
    select = np.zeros((3, 3, 2, SUBLANES, local + 2, 2, TAP_PAD), np.float32)
    for b in range(3):
        for c in range(3):
            for d in range(3):
                tap = (b * 3 + c) * 3 + d
                for branch in range(2):
                    for cell in range(local):
                        select[c, d, branch, cell, cell + b, branch, tap] = 1
    return select.reshape(18 * SUBLANES, -1)


def unit(features):
    positive = jnp.maximum(features.astype(F32), 0.0)
    length = jnp.sqrt(jnp.sum(positive * positive, axis=-1, keepdims=True) + 1e-06)
    return (positive / length).astype(BF16)


def split(value):
    high = value.astype(BF16)
    return high, (value - high.astype(F32)).astype(BF16)


def prepare_kernel(
    devices, target_ref, first_ref, second_ref, pick_ref, spread_ref, gate_ref,
    unit_ref, first_out, second_out, taps_ref,
):
    rows, columns = target_ref.shape[:2]
    for row in range(rows):
        unit_ref[row * columns : (row + 1) * columns] = unit(target_ref[row])
    hid = first_ref.shape[-1]
    taps_ref[...] = jnp.zeros(taps_ref.shape, F32)
    for number, ref in enumerate((first_ref, second_ref)):
        base = 2 * TAP_PAD * number
        for b in range(3):
            for c in range(3):
                start = base + (b * 3 + c) * 3
                taps_ref[start : start + 3, :hid] = ref[1, b, c]
        for c in range(3):
            for d in range(3):
                piece = ref[c, d, 1]
                for b in range(3):
                    start = base + TAP_PAD + (b * 3 + c) * 3 + d
                    taps_ref[start : start + 1, :hid] = piece[b : b + 1]
    branches = [taps_ref[i * TAP_PAD : (i + 1) * TAP_PAD, :hid] for i in range(4)]
    width = first_out.shape[1]
    taps = jnp.concatenate(split(jnp.concatenate(branches[:2], axis=1)), axis=0)
    blocks = first_out.shape[0] // (2 * hid)
    for block in range(blocks):
        piece = lax.dot_general(
            taps, pick_ref[:, block * width : (block + 1) * width],
            (((0,), (0,)), ((), ())), preferred_element_type=F32,
        )
        if block == 0:
            piece = piece * jnp.where(lax.axis_index("tgt") == 0, 0.0, 1.0)
        if block == blocks - 1:
            piece = piece * jnp.where(lax.axis_index("tgt") == devices - 1, 0.0, 1.0)
        first_out[block * 2 * hid : (block + 1) * 2 * hid] = piece.astype(BF16)
    depth = blocks * 2 * hid
    groups = blocks * 2
    row_group = lax.broadcasted_iota(jnp.int32, (groups * TAP_PAD, depth), 0) // TAP_PAD
    lane_group = lax.broadcasted_iota(jnp.int32, (groups * TAP_PAD, depth), 1) // hid
    tiled = jnp.concatenate([jnp.concatenate(branches[2:], axis=1)] * blocks, axis=1)
    tiled = jnp.concatenate([tiled] * groups, axis=0)
    tiled = jnp.where(row_group == lane_group, tiled, 0.0)
    high, low = split(tiled)
    half = second_out.shape[0] // 2
    high = jnp.dot(spread_ref[...], high, preferred_element_type=F32).astype(BF16)
    low = jnp.dot(spread_ref[...], low, preferred_element_type=F32).astype(BF16)
    second_out[:half, :depth] = high
    second_out[:half, depth:] = high
    second_out[half:, :depth] = low
    second_out[half:, depth:] = jnp.zeros_like(low)


def spread_kernel(
    source_ref, target_ref, pick_ref, scatter_ref,
    out_ref, target_out, pick_out, scatter_out, source_copy, sems,
):
    copies = [
        pltpu.make_async_copy(start, end, sems.at[number])
        for number, (start, end) in enumerate(
            (
                (source_ref, source_copy),
                (target_ref, target_out),
                (pick_ref, pick_out),
                (scatter_ref, scatter_out),
            )
        )
    ]
    for copy in copies:
        copy.start()
    copies[0].wait()
    half = out_ref.shape[2]
    for device in range(out_ref.shape[0]):
        start = device % 2 * half
        out_ref[device] = source_copy[:, start : start + half]
    for copy in copies[1:]:
        copy.wait()


def match_kernel(
    local, mine_ref, other_ref, target_ref, send_ref, source_ref, order_ref
):
    rows, padded, columns = order_ref.shape
    cells = padded - 2 * SUBLANES
    half = mine_ref.shape[1]
    side = lax.axis_index("tgt") % 2
    block = min(cells, 32)
    for first in range(0, cells, block):
        halves = [
            jnp.maximum(ref[first : first + block].astype(F32), 0.0)
            for ref in (mine_ref, other_ref)
        ]
        squares = [jnp.sum(piece * piece, axis=-1, keepdims=True) for piece in halves]
        length = jnp.sqrt(squares[0] + squares[1] + 1e-06)
        for number, piece in enumerate(halves):
            start = pl.multiple_of((side ^ number) * half, half)
            source_ref[first : first + block, pl.ds(start, half)] = (piece / length).astype(BF16)
    correlation = lax.dot_general(
        source_ref[...], target_ref[...], (((1,), (1,)), ((), ())), preferred_element_type=F32
    )
    window = max(SUBLANES, local + 4)
    blank = jnp.zeros((SUBLANES, columns), F32)
    for row in range(rows):
        order_ref[row, :SUBLANES, :] = blank
        order_ref[row, SUBLANES + cells :, :] = blank
        order_ref[row, SUBLANES : SUBLANES + cells, :] = correlation[
            :, row * columns : (row + 1) * columns
        ]
        source_best = jnp.max(order_ref[row], axis=0, keepdims=True)
        scale = 1.0 / jnp.maximum(source_best, TINY)
        root = jnp.concatenate(root_rows(source_best), axis=0)
        place = rows * window + 2 * row
        for target in range(send_ref.shape[0]):
            first = SUBLANES + target * local - 2
            send_ref[target, row * window : (row + 1) * window] = (
                order_ref[row, first : first + window, :] * scale
            )
            send_ref[target, place : place + 2] = root
    used = rows * (window + 2)
    spare = send_ref.shape[1] - used
    if spare:
        for target in range(send_ref.shape[0]):
            send_ref[target, used:] = jnp.zeros((spare, columns), F32)


def root_rows(best):
    root = jnp.sqrt(jnp.sqrt(jnp.sqrt(best)))
    high = root.astype(BF16).astype(F32)
    return high, root - high


def best_of_root(rows):
    root = rows[:1] + rows[1:]
    for _ in range(3):
        root = root * root
    return root


def row_of_column(column, lanes):
    row = lax.broadcasted_iota(jnp.int32, (column.shape[0], lanes), 0)
    lane = lax.broadcasted_iota(jnp.int32, (column.shape[0], lanes), 1)
    return jnp.sum(jnp.where(row == lane, column, 0.0), axis=0, keepdims=True)


def column_of_row(values, count):
    row = lax.broadcasted_iota(jnp.int32, (count, values.shape[1]), 0)
    lane = lax.broadcasted_iota(jnp.int32, (count, values.shape[1]), 1)
    return jnp.sum(jnp.where(row == lane, values, 0.0), axis=1, keepdims=True)


def lane_shifts(value):
    lanes = value.shape[-1]
    lane = lax.broadcasted_iota(jnp.int32, value.shape, value.ndim - 1)
    axis = value.ndim - 1
    left = jnp.where(lane == 0, 0.0, pltpu.roll(value, 1, axis))
    right = jnp.where(lane == lanes - 1, 0.0, pltpu.roll(value, lanes - 1, axis))
    return left, right


def consensus_kernel(
    parts, local, rows, came_ref, first_ref, second_ref, send_ref, tile_ref, partial_ref, rows_ref
):
    devices, _, columns = came_ref.shape
    window = max(SUBLANES, local + 4)
    grid_rows = devices * rows
    tile = len(ORDER) * SUBLANES
    again = REPEATED * SUBLANES
    zero = jnp.zeros((SUBLANES, columns), F32)

    def piece_of(device, row, first):
        return rows_ref[device * rows + row, first : first + SUBLANES, :]

    def survey(device, best):
        best = list(best)
        for row in range(rows):
            place = rows * window + 2 * row
            largest = best_of_root(came_ref[device, place : place + 2])
            block = came_ref[device, row * window : (row + 1) * window] * largest
            rows_ref[device * rows + row, :window] = block
            rows_ref[device * rows + row, window : window + 1] = 1.0 / (largest + EPSILON)
            for number, (first, _, _) in enumerate(parts):
                best[number] = jnp.maximum(best[number], block[first : first + SUBLANES])
        return tuple(best)

    best = lax.fori_loop(0, devices, survey, (zero,) * len(parts), unroll=4)
    scales = [
        jnp.broadcast_to(1.0 / (jnp.max(most, axis=1, keepdims=True) + EPSILON), most.shape)
        for most in best
    ]

    blank = jnp.zeros((tile, columns), BF16)
    for number in range(len(parts)):
        tile_ref[0, number] = blank

    def build(device, present):
        source = jnp.minimum(device, devices - 1)
        for row in range(rows):
            inverse = rows_ref[source * rows + row, window : window + 1, :] * present
            for number, (first, _, _) in enumerate(parts):
                value = piece_of(source, row, first)
                value = value * (value * inverse) * (value * scales[number])
                left, right = lane_shifts(value)
                moved = (left, value, right)
                high = [piece.astype(BF16).astype(F32) for piece in moved]
                low = [piece - rounded for piece, rounded in zip(moved, high)]
                stacked = jnp.concatenate(
                    [(low if part else high)[offset] for offset, part in ORDER], axis=0
                )
                tile_ref[device * rows + row + 1, number] = stacked.astype(BF16)

    partial_rows = second_ref.shape[0] // 2
    empty = jnp.zeros((partial_rows, columns), F32)
    partial_ref[0] = empty
    partial_ref[grid_rows + 1] = empty

    def layers(device):
        base = device * rows
        hidden = []
        offset = 0
        for number, (_, _, size) in enumerate(parts):
            taps = []
            for side in range(rows):
                pieces = [tile_ref[base + side + c, number] for c in range(3)]
                pieces += [tile_ref[base + side + c, number, :again] for c in range(3)]
                taps.append(jnp.concatenate(pieces, axis=0))
            count = size * first_ref.shape[0] // (local + 2)
            hidden.append(
                jnp.dot(
                    first_ref[offset : offset + count],
                    jnp.concatenate(taps, axis=1),
                    preferred_element_type=F32,
                )
            )
            offset += count
        halves = [split(jnp.maximum(piece, 0.0)) for piece in hidden]
        pair = jnp.concatenate([high for high, _ in halves] + [low for _, low in halves], axis=0)
        deep = pair.shape[0]
        cut = deep // MATRIX * MATRIX
        if 2 * cut < deep:
            cut = deep
        partial = jnp.dot(second_ref[:, :cut], pair[:cut], preferred_element_type=F32)
        partial = partial[:partial_rows] + partial[partial_rows:]
        if cut < deep:
            partial = partial + jnp.dot(
                second_ref[:partial_rows, cut:], pair[cut:], preferred_element_type=F32
            )
        for side in range(rows):
            partial_ref[base + side + 1] = partial[:, side * columns : (side + 1) * columns]

    def gather(device, most):
        for row in range(rows):
            total = None
            for branch in range(2):
                sums = []
                for d in range(3):
                    value = None
                    for c in range(3):
                        start = ((c * 3 + d) * 2 + branch) * SUBLANES
                        piece = partial_ref[device * rows + row + c, start : start + SUBLANES, :]
                        value = piece if value is None else value + piece
                    sums.append(value)
                output = lane_shifts(sums[0])[0] + sums[1] + lane_shifts(sums[2])[1]
                output = jnp.maximum(output, 0.0)
                total = output if total is None else total + output
            send_ref[device, row * SUBLANES : (row + 1) * SUBLANES] = total
            most = jnp.maximum(most, total)
        return most

    def present(device):
        return jnp.where(device < devices, 1.0, 0.0).astype(F32)

    build(0, 1.0)
    build(1, 1.0)
    layers(0)
    build(2, present(2))
    layers(1)
    build(3, present(3))

    def step(device, most):
        layers(device)
        build(device + 2, present(device + 2))
        return gather(device - 2, most)

    most = lax.fori_loop(2, devices, step, zero, unroll=min(14, devices - 2))
    most = gather(devices - 2, most)
    most = gather(devices - 1, most)
    best = jnp.max(most, axis=1, keepdims=True)
    scale = 1.0 / jnp.maximum(best, TINY)
    root = jnp.concatenate(
        [row_of_column(piece, columns) for piece in root_rows(best)]
        + [jnp.zeros((SUBLANES - 2, columns), F32)],
        axis=0,
    )
    for device in range(devices):
        for row in range(rows):
            start = row * SUBLANES
            send_ref[device, start : start + SUBLANES] = (
                send_ref[device, start : start + SUBLANES] * scale
            )
        send_ref[device, rows * SUBLANES :] = root


def finish_kernel(local, came_ref, out_ref):
    devices, _, columns = came_ref.shape
    rows = out_ref.shape[1]
    place = rows * SUBLANES
    bests = [
        column_of_row(best_of_root(came_ref[device, place : place + 2]), SUBLANES)
        for device in range(devices)
    ]
    for row in range(rows):
        first = row * SUBLANES
        most = jnp.zeros((SUBLANES, columns), F32)
        for device in range(devices):
            most = jnp.maximum(most, came_ref[device, first : first + SUBLANES] * bests[device])
        inverse = 1.0 / (jnp.max(most, axis=0, keepdims=True) + EPSILON)
        for device in range(devices):
            value = came_ref[device, first : first + SUBLANES] * bests[device]
            value = value * (value * inverse) * (value * (1.0 / (bests[device] + EPSILON)))
            out_ref[device * local : (device + 1) * local, row, :] = value[:local]


def exchange(slots):
    return lax.all_to_all(slots, "tgt", 0, 0, tiled=True)


def exchange_relative(slots):
    return exchange(slots.astype(jnp.float16)).astype(F32)


def room(*shapes):
    scratch = sum(int(np.prod(shape)) * jnp.dtype(kind).itemsize for shape, kind in shapes)
    return pltpu.CompilerParams(vmem_limit_bytes=scratch + 6 * 2**20)


VMEM = pl.BlockSpec(memory_space=pltpu.VMEM)
ANY = pl.BlockSpec(memory_space=pltpu.HBM)


def shards(source_features, target_features, conv_first, conv_second):
    devices = lax.axis_size("tgt")
    rows, columns, channels = target_features.shape
    cells = source_features.shape[0] * devices
    hid = conv_first.shape[0]
    local = cells // devices
    parts = parts_of(local)
    hidden = local + 2
    window = max(SUBLANES, local + 4)
    tile = len(ORDER) * SUBLANES
    width = 3 * (tile + REPEATED * SUBLANES)
    depth = hidden * 2 * hid
    assert local <= SUBLANES and rows * devices % 4 == 0

    pick = jnp.asarray(first_selector(parts), BF16)
    scatter = jnp.asarray(second_selector(local), BF16)
    spread, target_features, pick, scatter = pl.pallas_call(
        spread_kernel,
        out_shape=(
            jax.ShapeDtypeStruct((devices, source_features.shape[0], channels // 2), BF16),
            jax.ShapeDtypeStruct(target_features.shape, BF16),
            jax.ShapeDtypeStruct(pick.shape, BF16),
            jax.ShapeDtypeStruct(scatter.shape, BF16),
        ),
        in_specs=[ANY] * 4,
        out_specs=(VMEM,) * 4,
        scratch_shapes=[
            pltpu.VMEM(source_features.shape, BF16),
            pltpu.SemaphoreType.DMA((4,)),
        ],
        compiler_params=room(),
        name="spread",
    )(
        *(
            pltpu.with_memory_space_constraint(value, pltpu.HBM)
            for value in (source_features, target_features, pick, scatter)
        )
    )
    mine = exchange(spread).reshape(cells, channels // 2)
    other = lax.ppermute(mine, "tgt", [(i, i ^ 1) for i in range(devices)])

    second_rows = 18 * SUBLANES
    target_unit, first_weights, second_weights = pl.pallas_call(
        functools.partial(prepare_kernel, devices),
        out_shape=(
            jax.ShapeDtypeStruct((rows * columns, channels), BF16),
            jax.ShapeDtypeStruct((depth, width), BF16),
            jax.ShapeDtypeStruct((2 * second_rows, 2 * depth), BF16),
        ),
        in_specs=[VMEM] * 5 + [pl.BlockSpec(memory_space=pl.ANY)],
        out_specs=(VMEM,) * 3,
        scratch_shapes=[pltpu.VMEM((4 * TAP_PAD, 128), F32)],
        cost_estimate=pl.CostEstimate(flops=10**6, bytes_accessed=2 * 10**6, transcendentals=0),
        compiler_params=room(),
        name="prepare",
    )(
        target_features,
        jnp.transpose(conv_first, (1, 2, 3, 4, 0)),
        jnp.transpose(conv_second, (1, 2, 3, 4, 0)),
        pick,
        scatter,
        mine,
    )

    slots = pl.pallas_call(
        functools.partial(match_kernel, local),
        out_shape=jax.ShapeDtypeStruct((devices, whole_tiles(rows * (window + 2)), columns), F32),
        in_specs=[VMEM] * 3,
        out_specs=VMEM,
        scratch_shapes=[
            pltpu.VMEM((cells, channels), BF16),
            pltpu.VMEM((rows, cells + 2 * SUBLANES, columns), F32),
        ],
        compiler_params=room(),
        name="match",
    )(mine, other, target_unit)

    stores = (
        ((rows * (devices + 2) + 2, len(parts), tile, columns), BF16),
        ((rows * devices + 2, second_rows, columns), F32),
        ((rows * devices, whole_tiles(window + 1), columns), F32),
    )
    slots = pl.pallas_call(
        functools.partial(consensus_kernel, parts, local, rows),
        out_shape=jax.ShapeDtypeStruct((devices, (rows + 1) * SUBLANES, columns), F32),
        in_specs=[VMEM] * 3,
        out_specs=VMEM,
        scratch_shapes=[pltpu.VMEM(shape, kind) for shape, kind in stores],
        compiler_params=room(*stores),
        name="consensus",
    )(exchange_relative(slots), first_weights, second_weights)

    filtered = pl.pallas_call(
        functools.partial(finish_kernel, local),
        out_shape=jax.ShapeDtypeStruct((cells, rows, columns), F32),
        in_specs=[VMEM],
        out_specs=VMEM,
        compiler_params=room(),
        name="finish",
    )(exchange_relative(slots))
    return filtered[None]


def solution(mesh):
    placed = (P(("pairs", "tgt"), None), P(("pairs", "tgt"), None, None), P(), P())
    return jax.shard_map(
        shards, mesh=mesh, in_specs=placed, out_specs=P("pairs", None, "tgt", None), check_vma=False
    )
```

```python
import functools

import jax
import jax.numpy as jnp
import numpy as np
from jax import lax
from jax.experimental import pallas as pl
from jax.experimental.pallas import tpu as pltpu
from jax.sharding import PartitionSpec as P

EPSILON = 1e-05
TINY = 1e-30
MATRIX = 256
F32 = jnp.float32
BF16 = jnp.bfloat16
TAPS = 27
TAP_PAD = 32
SUBLANES = 8
ORDER = ((0, 0), (1, 0), (2, 0), (0, 1), (1, 1), (2, 1))
REPEATED = 4


def whole_tiles(count):
    return -(-count // SUBLANES) * SUBLANES


def parts_of(local):
    hidden = local + 2
    count = -(-hidden // (SUBLANES - 2))
    size = -(-hidden // count)
    parts = []
    for start in range(0, hidden, size):
        first = min(start, max(0, local + 4 - SUBLANES))
        parts.append((first, start, min(size, hidden - start)))
    return parts


def tap_fields(tap):
    return tap // 9, tap // 3 % 3, tap % 3


def first_codes(width):
    row = lax.broadcasted_iota(jnp.int32, (2 * TAP_PAD, 128), 0)
    b, c, d = tap_fields(row % TAP_PAD)
    rows = ((row // TAP_PAD * 3 + c) * 3 + d) * 16 + b
    rows = jnp.where(row % TAP_PAD < TAPS, rows, -100)[:, :1]
    column = lax.broadcasted_iota(jnp.int32, (SUBLANES, width), 1)
    tile, again = len(ORDER) * SUBLANES, REPEATED * SUBLANES
    extra = column >= 3 * tile
    rest = column - 3 * tile
    c = jnp.where(extra, rest // again, column // tile)
    place = jnp.where(extra, rest % again, column % tile) // SUBLANES
    code = ((jnp.where(extra, 3, 0) + c) * 3 + place % 3) * 16 + column % SUBLANES
    columns = jnp.where(extra & (place >= 3), -1, code)[:1]
    return rows, columns


def second_selector(local, blocks):
    height, width = 18 * SUBLANES, blocks * 2 * TAP_PAD
    row = lax.broadcasted_iota(jnp.int32, (height, 128), 0)
    rows = row // SUBLANES * 32 + row % SUBLANES
    rows = jnp.where(row % SUBLANES < local, rows, -100)[:, :1]
    column = lax.broadcasted_iota(jnp.int32, (SUBLANES, width), 1)
    tap = column % TAP_PAD
    b, c, d = tap_fields(tap)
    cell = column // (2 * TAP_PAD) - b
    code = ((c * 3 + d) * 2 + column // TAP_PAD % 2) * 32 + cell
    columns = jnp.where((tap < TAPS) & (cell >= 0), code, -1)[:1]
    return jnp.where(rows == columns, 1.0, 0.0).astype(BF16)


def unit(features):
    positive = jnp.maximum(features.astype(F32), 0.0)
    length = jnp.sqrt(jnp.sum(positive * positive, axis=-1, keepdims=True) + 1e-06)
    return (positive / length).astype(BF16)


def split(value):
    high = value.astype(BF16)
    return high, (value - high.astype(F32)).astype(BF16)


def prepare_kernel(
    devices, local, parts, first_ref, second_ref, gate_ref, first_out, second_out, taps_ref
):
    hid = first_ref.shape[-1]
    taps_ref[...] = jnp.zeros(taps_ref.shape, F32)
    for number, ref in enumerate((first_ref, second_ref)):
        base = 2 * TAP_PAD * number
        for b in range(3):
            for c in range(3):
                start = base + (b * 3 + c) * 3
                taps_ref[start : start + 3, :hid] = ref[1, b, c]
        for c in range(3):
            for d in range(3):
                piece = ref[c, d, 1]
                for b in range(3):
                    start = base + TAP_PAD + (b * 3 + c) * 3 + d
                    taps_ref[start : start + 1, :hid] = piece[b : b + 1]
    branches = [taps_ref[i * TAP_PAD : (i + 1) * TAP_PAD, :hid] for i in range(4)]
    width = first_out.shape[1]
    taps = jnp.concatenate(split(jnp.concatenate(branches[:2], axis=1)), axis=0)
    blocks = first_out.shape[0] // (2 * hid)
    rows_code, columns_code = first_codes(width)
    for block in range(blocks):
        first = [part[0] for part in parts if part[1] <= block][-1]
        pick = jnp.where(rows_code + (block - first) == columns_code, 1.0, 0.0).astype(BF16)
        piece = lax.dot_general(
            taps, pick, (((0,), (0,)), ((), ())), preferred_element_type=F32
        )
        if block == 0:
            piece = piece * jnp.where(lax.axis_index("tgt") == 0, 0.0, 1.0)
        if block == blocks - 1:
            piece = piece * jnp.where(lax.axis_index("tgt") == devices - 1, 0.0, 1.0)
        first_out[block * 2 * hid : (block + 1) * 2 * hid] = piece.astype(BF16)
    depth = blocks * 2 * hid
    groups = blocks * 2
    row_group = lax.broadcasted_iota(jnp.int32, (groups * TAP_PAD, depth), 0) // TAP_PAD
    lane_group = lax.broadcasted_iota(jnp.int32, (groups * TAP_PAD, depth), 1) // hid
    tiled = jnp.concatenate([jnp.concatenate(branches[2:], axis=1)] * blocks, axis=1)
    tiled = jnp.concatenate([tiled] * groups, axis=0)
    tiled = jnp.where(row_group == lane_group, tiled, 0.0)
    high, low = split(tiled)
    half = second_out.shape[0] // 2
    scatter = second_selector(local, blocks)
    high = jnp.dot(scatter, high, preferred_element_type=F32).astype(BF16)
    low = jnp.dot(scatter, low, preferred_element_type=F32).astype(BF16)
    second_out[:half, :depth] = high
    second_out[:half, depth:] = high
    second_out[half:, :depth] = low
    second_out[half:, depth:] = jnp.zeros_like(low)


def target_kernel(target_ref, gate_ref, unit_ref):
    rows, columns = target_ref.shape[:2]
    for row in range(rows):
        unit_ref[row * columns : (row + 1) * columns] = unit(target_ref[row])


def spread_kernel(source_ref, out_ref, source_copy, sems):
    copies = [
        pltpu.make_async_copy(start, end, sems.at[number])
        for number, (start, end) in enumerate(
            (
                (source_ref, source_copy),
            )
        )
    ]
    for copy in copies:
        copy.start()
    copies[0].wait()
    half = out_ref.shape[2]
    for device in range(out_ref.shape[0]):
        start = device % 2 * half
        out_ref[device] = source_copy[:, start : start + half]
    for copy in copies[1:]:
        copy.wait()


def match_kernel(
    local, mine_ref, other_ref, target_ref, send_ref, source_ref, order_ref
):
    rows, padded, columns = order_ref.shape
    cells = padded - 2 * SUBLANES
    half = mine_ref.shape[1]
    side = lax.axis_index("tgt") % 2
    block = min(cells, 32)
    for first in range(0, cells, block):
        halves = [
            jnp.maximum(ref[first : first + block].astype(F32), 0.0)
            for ref in (mine_ref, other_ref)
        ]
        squares = [jnp.sum(piece * piece, axis=-1, keepdims=True) for piece in halves]
        length = jnp.sqrt(squares[0] + squares[1] + 1e-06)
        for number, piece in enumerate(halves):
            start = pl.multiple_of((side ^ number) * half, half)
            source_ref[first : first + block, pl.ds(start, half)] = (piece / length).astype(BF16)
    correlation = lax.dot_general(
        source_ref[...], target_ref[...], (((1,), (1,)), ((), ())), preferred_element_type=F32
    )
    window = max(SUBLANES, local + 4)
    blank = jnp.zeros((SUBLANES, columns), F32)
    for row in range(rows):
        order_ref[row, :SUBLANES, :] = blank
        order_ref[row, SUBLANES + cells :, :] = blank
        order_ref[row, SUBLANES : SUBLANES + cells, :] = correlation[
            :, row * columns : (row + 1) * columns
        ]
        source_best = jnp.max(order_ref[row], axis=0, keepdims=True)
        scale = 1.0 / jnp.maximum(source_best, TINY)
        root = jnp.concatenate(root_rows(source_best), axis=0)
        place = rows * window + 2 * row
        for target in range(send_ref.shape[0]):
            first = SUBLANES + target * local - 2
            send_ref[target, row * window : (row + 1) * window] = (
                order_ref[row, first : first + window, :] * scale
            )
            send_ref[target, place : place + 2] = root
    used = rows * (window + 2)
    spare = send_ref.shape[1] - used
    if spare:
        for target in range(send_ref.shape[0]):
            send_ref[target, used:] = jnp.zeros((spare, columns), F32)


def root_rows(best):
    root = jnp.sqrt(jnp.sqrt(jnp.sqrt(best)))
    high = root.astype(BF16).astype(F32)
    return high, root - high


def best_of_root(rows):
    root = rows[:1] + rows[1:]
    for _ in range(3):
        root = root * root
    return root


def row_of_column(column, lanes):
    row = lax.broadcasted_iota(jnp.int32, (column.shape[0], lanes), 0)
    lane = lax.broadcasted_iota(jnp.int32, (column.shape[0], lanes), 1)
    return jnp.sum(jnp.where(row == lane, column, 0.0), axis=0, keepdims=True)


def column_of_row(values, count):
    row = lax.broadcasted_iota(jnp.int32, (count, values.shape[1]), 0)
    lane = lax.broadcasted_iota(jnp.int32, (count, values.shape[1]), 1)
    return jnp.sum(jnp.where(row == lane, values, 0.0), axis=1, keepdims=True)


def lane_shifts(value):
    lanes = value.shape[-1]
    lane = lax.broadcasted_iota(jnp.int32, value.shape, value.ndim - 1)
    axis = value.ndim - 1
    left = jnp.where(lane == 0, 0.0, pltpu.roll(value, 1, axis))
    right = jnp.where(lane == lanes - 1, 0.0, pltpu.roll(value, lanes - 1, axis))
    return left, right


def consensus_kernel(
    parts, local, rows, came_ref, first_ref, second_ref, send_ref, tile_ref, partial_ref, rows_ref
):
    devices, _, columns = came_ref.shape
    window = max(SUBLANES, local + 4)
    grid_rows = devices * rows
    tile = len(ORDER) * SUBLANES
    again = REPEATED * SUBLANES
    zero = jnp.zeros((SUBLANES, columns), F32)

    def piece_of(device, row, first):
        return rows_ref[device * rows + row, first : first + SUBLANES, :]

    def survey(device, best):
        best = list(best)
        for row in range(rows):
            place = rows * window + 2 * row
            largest = best_of_root(came_ref[device, place : place + 2])
            block = came_ref[device, row * window : (row + 1) * window] * largest
            rows_ref[device * rows + row, :window] = block
            rows_ref[device * rows + row, window : window + 1] = 1.0 / (largest + EPSILON)
            for number, (first, _, _) in enumerate(parts):
                best[number] = jnp.maximum(best[number], block[first : first + SUBLANES])
        return tuple(best)

    best = lax.fori_loop(0, devices, survey, (zero,) * len(parts), unroll=4)
    scales = [
        jnp.broadcast_to(1.0 / (jnp.max(most, axis=1, keepdims=True) + EPSILON), most.shape)
        for most in best
    ]

    blank = jnp.zeros((tile, columns), BF16)
    for number in range(len(parts)):
        tile_ref[0, number] = blank

    def build(device, present):
        source = jnp.minimum(device, devices - 1)
        for row in range(rows):
            inverse = rows_ref[source * rows + row, window : window + 1, :] * present
            for number, (first, _, _) in enumerate(parts):
                value = piece_of(source, row, first)
                value = value * (value * inverse) * (value * scales[number])
                left, right = lane_shifts(value)
                moved = (left, value, right)
                high = [piece.astype(BF16).astype(F32) for piece in moved]
                low = [piece - rounded for piece, rounded in zip(moved, high)]
                stacked = jnp.concatenate(
                    [(low if part else high)[offset] for offset, part in ORDER], axis=0
                )
                tile_ref[device * rows + row + 1, number] = stacked.astype(BF16)

    partial_rows = second_ref.shape[0] // 2
    empty = jnp.zeros((partial_rows, columns), F32)
    partial_ref[0] = empty
    partial_ref[grid_rows + 1] = empty

    def layers(device):
        base = device * rows
        hidden = []
        offset = 0
        for number, (_, _, size) in enumerate(parts):
            taps = []
            for side in range(rows):
                pieces = [tile_ref[base + side + c, number] for c in range(3)]
                pieces += [tile_ref[base + side + c, number, :again] for c in range(3)]
                taps.append(jnp.concatenate(pieces, axis=0))
            count = size * first_ref.shape[0] // (local + 2)
            hidden.append(
                jnp.dot(
                    first_ref[offset : offset + count],
                    jnp.concatenate(taps, axis=1),
                    preferred_element_type=F32,
                )
            )
            offset += count
        halves = [split(jnp.maximum(piece, 0.0)) for piece in hidden]
        pair = jnp.concatenate([high for high, _ in halves] + [low for _, low in halves], axis=0)
        deep = pair.shape[0]
        cut = deep // MATRIX * MATRIX
        if 2 * cut < deep:
            cut = deep
        partial = jnp.dot(second_ref[:, :cut], pair[:cut], preferred_element_type=F32)
        partial = partial[:partial_rows] + partial[partial_rows:]
        if cut < deep:
            partial = partial + jnp.dot(
                second_ref[:partial_rows, cut:], pair[cut:], preferred_element_type=F32
            )
        for side in range(rows):
            partial_ref[base + side + 1] = partial[:, side * columns : (side + 1) * columns]

    def gather(device, most):
        for row in range(rows):
            total = None
            for branch in range(2):
                sums = []
                for d in range(3):
                    value = None
                    for c in range(3):
                        start = ((c * 3 + d) * 2 + branch) * SUBLANES
                        piece = partial_ref[device * rows + row + c, start : start + SUBLANES, :]
                        value = piece if value is None else value + piece
                    sums.append(value)
                output = lane_shifts(sums[0])[0] + sums[1] + lane_shifts(sums[2])[1]
                output = jnp.maximum(output, 0.0)
                total = output if total is None else total + output
            send_ref[device, row * SUBLANES : (row + 1) * SUBLANES] = total
            most = jnp.maximum(most, total)
        return most

    def present(device):
        return jnp.where(device < devices, 1.0, 0.0).astype(F32)

    build(0, 1.0)
    build(1, 1.0)
    layers(0)
    build(2, present(2))
    layers(1)
    build(3, present(3))

    def step(device, most):
        layers(device)
        build(device + 2, present(device + 2))
        return gather(device - 2, most)

    most = lax.fori_loop(2, devices, step, zero, unroll=min(14, devices - 2))
    most = gather(devices - 2, most)
    most = gather(devices - 1, most)
    best = jnp.max(most, axis=1, keepdims=True)
    scale = 1.0 / jnp.maximum(best, TINY)
    root = jnp.concatenate(
        [row_of_column(piece, columns) for piece in root_rows(best)]
        + [jnp.zeros((SUBLANES - 2, columns), F32)],
        axis=0,
    )
    for device in range(devices):
        for row in range(rows):
            start = row * SUBLANES
            send_ref[device, start : start + SUBLANES] = (
                send_ref[device, start : start + SUBLANES] * scale
            )
        send_ref[device, rows * SUBLANES :] = root


def finish_kernel(local, came_ref, out_ref):
    devices, _, columns = came_ref.shape
    rows = out_ref.shape[1]
    place = rows * SUBLANES
    bests = [
        column_of_row(best_of_root(came_ref[device, place : place + 2]), SUBLANES)
        for device in range(devices)
    ]
    for row in range(rows):
        first = row * SUBLANES
        most = jnp.zeros((SUBLANES, columns), F32)
        for device in range(devices):
            most = jnp.maximum(most, came_ref[device, first : first + SUBLANES] * bests[device])
        inverse = 1.0 / (jnp.max(most, axis=0, keepdims=True) + EPSILON)
        for device in range(devices):
            value = came_ref[device, first : first + SUBLANES] * bests[device]
            value = value * (value * inverse) * (value * (1.0 / (bests[device] + EPSILON)))
            out_ref[device * local : (device + 1) * local, row, :] = value[:local]


def exchange(slots):
    return lax.all_to_all(slots, "tgt", 0, 0, tiled=True)


def exchange_relative(slots):
    return exchange(slots.astype(jnp.float16)).astype(F32)


def room(*shapes):
    scratch = sum(int(np.prod(shape)) * jnp.dtype(kind).itemsize for shape, kind in shapes)
    return pltpu.CompilerParams(vmem_limit_bytes=scratch + 6 * 2**20)


VMEM = pl.BlockSpec(memory_space=pltpu.VMEM)
ANY = pl.BlockSpec(memory_space=pltpu.HBM)


def shards(source_features, target_features, conv_first, conv_second):
    devices = lax.axis_size("tgt")
    rows, columns, channels = target_features.shape
    cells = source_features.shape[0] * devices
    hid = conv_first.shape[0]
    local = cells // devices
    parts = parts_of(local)
    hidden = local + 2
    window = max(SUBLANES, local + 4)
    tile = len(ORDER) * SUBLANES
    width = 3 * (tile + REPEATED * SUBLANES)
    depth = hidden * 2 * hid
    assert local <= SUBLANES and rows * devices % 4 == 0

    (spread,) = pl.pallas_call(
        spread_kernel,
        out_shape=(
            jax.ShapeDtypeStruct((devices, source_features.shape[0], channels // 2), BF16),
        ),
        in_specs=[ANY] * 1,
        out_specs=(VMEM,) * 1,
        scratch_shapes=[
            pltpu.VMEM(source_features.shape, BF16),
            pltpu.SemaphoreType.DMA((1,)),
        ],
        compiler_params=room(),
        name="spread",
    )(
        *(
            pltpu.with_memory_space_constraint(value, pltpu.HBM)
            for value in (source_features,)
        )
    )
    mine = exchange(spread).reshape(cells, channels // 2)
    other = lax.ppermute(mine, "tgt", [(i, i ^ 1) for i in range(devices)])

    second_rows = 18 * SUBLANES
    first_weights, second_weights = pl.pallas_call(
        functools.partial(prepare_kernel, devices, local, parts),
        out_shape=(
            jax.ShapeDtypeStruct((depth, width), BF16),
            jax.ShapeDtypeStruct((2 * second_rows, 2 * depth), BF16),
        ),
        in_specs=[VMEM] * 2 + [pl.BlockSpec(memory_space=pl.ANY)],
        out_specs=(VMEM,) * 2,
        scratch_shapes=[pltpu.VMEM((4 * TAP_PAD, 128), F32)],
        cost_estimate=pl.CostEstimate(flops=10**9, bytes_accessed=10**6, transcendentals=0),
        compiler_params=room(),
        name="prepare",
    )(
        jnp.transpose(conv_first, (1, 2, 3, 4, 0)),
        jnp.transpose(conv_second, (1, 2, 3, 4, 0)),
        mine,
    )
    target_unit = pl.pallas_call(
        target_kernel,
        out_shape=jax.ShapeDtypeStruct((rows * columns, channels), BF16),
        in_specs=[VMEM, pl.BlockSpec(memory_space=pl.ANY)],
        out_specs=VMEM,
        cost_estimate=pl.CostEstimate(flops=10**6, bytes_accessed=10**6, transcendentals=0),
        compiler_params=room(),
        name="target",
    )(target_features, first_weights)

    slots = pl.pallas_call(
        functools.partial(match_kernel, local),
        out_shape=jax.ShapeDtypeStruct((devices, whole_tiles(rows * (window + 2)), columns), F32),
        in_specs=[VMEM] * 3,
        out_specs=VMEM,
        scratch_shapes=[
            pltpu.VMEM((cells, channels), BF16),
            pltpu.VMEM((rows, cells + 2 * SUBLANES, columns), F32),
        ],
        compiler_params=room(),
        name="match",
    )(mine, other, target_unit)

    stores = (
        ((rows * (devices + 2) + 2, len(parts), tile, columns), BF16),
        ((rows * devices + 2, second_rows, columns), F32),
        ((rows * devices, whole_tiles(window + 1), columns), F32),
    )
    slots = pl.pallas_call(
        functools.partial(consensus_kernel, parts, local, rows),
        out_shape=jax.ShapeDtypeStruct((devices, (rows + 1) * SUBLANES, columns), F32),
        in_specs=[VMEM] * 3,
        out_specs=VMEM,
        scratch_shapes=[pltpu.VMEM(shape, kind) for shape, kind in stores],
        compiler_params=room(*stores),
        name="consensus",
    )(exchange_relative(slots), first_weights, second_weights)

    filtered = pl.pallas_call(
        functools.partial(finish_kernel, local),
        out_shape=jax.ShapeDtypeStruct((cells, rows, columns), F32),
        in_specs=[VMEM],
        out_specs=VMEM,
        compiler_params=room(),
        name="finish",
    )(exchange_relative(slots))
    return filtered[None]


def solution(mesh):
    placed = (P(("pairs", "tgt"), None), P(("pairs", "tgt"), None, None), P(), P())
    return jax.shard_map(
        shards, mesh=mesh, in_specs=placed, out_specs=P("pairs", None, "tgt", None), check_vma=False
    )
```

```python
import functools

import jax
import jax.numpy as jnp
import numpy as np
from jax import lax
from jax.experimental import pallas as pl
from jax.experimental.pallas import tpu as pltpu
from jax.sharding import PartitionSpec as P

EPSILON = 1e-05
TINY = 1e-30
MATRIX = 256
UNROLLED = 16
F32 = jnp.float32
BF16 = jnp.bfloat16
TAPS = 27
TAP_PAD = 32
SUBLANES = 8
ORDER = ((0, 0), (1, 0), (2, 0), (0, 1), (1, 1), (2, 1))
REPEATED = 4


def whole_tiles(count):
    return -(-count // SUBLANES) * SUBLANES


def parts_of(local):
    hidden = local + 2
    count = -(-hidden // (SUBLANES - 2))
    size = -(-hidden // count)
    parts = []
    for start in range(0, hidden, size):
        first = min(start, max(0, local + 4 - SUBLANES))
        parts.append((first, start, min(size, hidden - start)))
    return parts


def tap_fields(tap):
    return tap // 9, tap // 3 % 3, tap % 3


def first_codes(width):
    row = lax.broadcasted_iota(jnp.int32, (2 * TAP_PAD, 128), 0)
    b, c, d = tap_fields(row % TAP_PAD)
    rows = ((row // TAP_PAD * 3 + c) * 3 + d) * 16 + b
    rows = jnp.where(row % TAP_PAD < TAPS, rows, -100)[:, :1]
    column = lax.broadcasted_iota(jnp.int32, (SUBLANES, width), 1)
    tile, again = len(ORDER) * SUBLANES, REPEATED * SUBLANES
    extra = column >= 3 * tile
    rest = column - 3 * tile
    c = jnp.where(extra, rest // again, column // tile)
    place = jnp.where(extra, rest % again, column % tile) // SUBLANES
    code = ((jnp.where(extra, 3, 0) + c) * 3 + place % 3) * 16 + column % SUBLANES
    columns = jnp.where(extra & (place >= 3), -1, code)[:1]
    return rows, columns


def second_selector(local, blocks):
    height, width = 18 * SUBLANES, blocks * 2 * TAP_PAD
    row = lax.broadcasted_iota(jnp.int32, (height, 128), 0)
    rows = row // SUBLANES * 32 + row % SUBLANES
    rows = jnp.where(row % SUBLANES < local, rows, -100)[:, :1]
    column = lax.broadcasted_iota(jnp.int32, (SUBLANES, width), 1)
    tap = column % TAP_PAD
    b, c, d = tap_fields(tap)
    cell = column // (2 * TAP_PAD) - b
    code = ((c * 3 + d) * 2 + column // TAP_PAD % 2) * 32 + cell
    columns = jnp.where((tap < TAPS) & (cell >= 0), code, -1)[:1]
    return jnp.where(rows == columns, 1.0, 0.0).astype(BF16)


def unit(features):
    positive = jnp.maximum(features.astype(F32), 0.0)
    length = jnp.sqrt(jnp.sum(positive * positive, axis=-1, keepdims=True) + 1e-06)
    return (positive / length).astype(BF16)


def split(value):
    high = value.astype(BF16)
    return high, (value - high.astype(F32)).astype(BF16)


def prepare_kernel(
    devices, local, parts, first_ref, second_ref, gate_ref, first_out, second_out, taps_ref
):
    hid = first_ref.shape[-1]
    taps_ref[...] = jnp.zeros(taps_ref.shape, F32)
    for number, ref in enumerate((first_ref, second_ref)):
        base = 2 * TAP_PAD * number
        for b in range(3):
            for c in range(3):
                start = base + (b * 3 + c) * 3
                taps_ref[start : start + 3, :hid] = ref[1, b, c]
        for c in range(3):
            for d in range(3):
                piece = ref[c, d, 1]
                for b in range(3):
                    start = base + TAP_PAD + (b * 3 + c) * 3 + d
                    taps_ref[start : start + 1, :hid] = piece[b : b + 1]
    branches = [taps_ref[i * TAP_PAD : (i + 1) * TAP_PAD, :hid] for i in range(4)]
    width = first_out.shape[1]
    taps = jnp.concatenate(split(jnp.concatenate(branches[:2], axis=1)), axis=0)
    blocks = first_out.shape[0] // (2 * hid)
    rows_code, columns_code = first_codes(width)
    for block in range(blocks):
        first = [part[0] for part in parts if part[1] <= block][-1]
        pick = jnp.where(rows_code + (block - first) == columns_code, 1.0, 0.0).astype(BF16)
        piece = lax.dot_general(
            taps, pick, (((0,), (0,)), ((), ())), preferred_element_type=F32
        )
        if block == 0:
            piece = piece * jnp.where(lax.axis_index("tgt") == 0, 0.0, 1.0)
        if block == blocks - 1:
            piece = piece * jnp.where(lax.axis_index("tgt") == devices - 1, 0.0, 1.0)
        first_out[block * 2 * hid : (block + 1) * 2 * hid] = piece.astype(BF16)
    depth = blocks * 2 * hid
    groups = blocks * 2
    row_group = lax.broadcasted_iota(jnp.int32, (groups * TAP_PAD, depth), 0) // TAP_PAD
    lane_group = lax.broadcasted_iota(jnp.int32, (groups * TAP_PAD, depth), 1) // hid
    tiled = jnp.concatenate([jnp.concatenate(branches[2:], axis=1)] * blocks, axis=1)
    tiled = jnp.concatenate([tiled] * groups, axis=0)
    tiled = jnp.where(row_group == lane_group, tiled, 0.0)
    high, low = split(tiled)
    half = second_out.shape[0] // 2
    scatter = second_selector(local, blocks)
    high = jnp.dot(scatter, high, preferred_element_type=F32).astype(BF16)
    low = jnp.dot(scatter, low, preferred_element_type=F32).astype(BF16)
    second_out[:half, :depth] = high
    second_out[:half, depth:] = high
    second_out[half:, :depth] = low
    second_out[half:, depth:] = jnp.zeros_like(low)


def target_kernel(target_ref, gate_ref, unit_ref):
    rows, columns = target_ref.shape[:2]
    for row in range(rows):
        unit_ref[row * columns : (row + 1) * columns] = unit(target_ref[row])


def spread_kernel(source_ref, out_ref, source_copy, sems):
    copies = [
        pltpu.make_async_copy(start, end, sems.at[number])
        for number, (start, end) in enumerate(
            (
                (source_ref, source_copy),
            )
        )
    ]
    for copy in copies:
        copy.start()
    copies[0].wait()
    half = out_ref.shape[2]
    for device in range(out_ref.shape[0]):
        start = device % 2 * half
        out_ref[device] = source_copy[:, start : start + half]
    for copy in copies[1:]:
        copy.wait()


def match_kernel(
    local, mine_ref, other_ref, target_ref, send_ref, source_ref, order_ref
):
    rows, padded, columns = order_ref.shape
    cells = padded - 2 * SUBLANES
    half = mine_ref.shape[1]
    side = lax.axis_index("tgt") % 2
    block = min(cells, 32)
    for first in range(0, cells, block):
        halves = [
            jnp.maximum(ref[first : first + block].astype(F32), 0.0)
            for ref in (mine_ref, other_ref)
        ]
        squares = [jnp.sum(piece * piece, axis=-1, keepdims=True) for piece in halves]
        length = jnp.sqrt(squares[0] + squares[1] + 1e-06)
        for number, piece in enumerate(halves):
            start = pl.multiple_of((side ^ number) * half, half)
            source_ref[first : first + block, pl.ds(start, half)] = (piece / length).astype(BF16)
    correlation = lax.dot_general(
        source_ref[...], target_ref[...], (((1,), (1,)), ((), ())), preferred_element_type=F32
    )
    window = max(SUBLANES, local + 4)
    blank = jnp.zeros((SUBLANES, columns), F32)
    for row in range(rows):
        order_ref[row, :SUBLANES, :] = blank
        order_ref[row, SUBLANES + cells :, :] = blank
        order_ref[row, SUBLANES : SUBLANES + cells, :] = correlation[
            :, row * columns : (row + 1) * columns
        ]
        source_best = jnp.max(order_ref[row], axis=0, keepdims=True)
        scale = 1.0 / jnp.maximum(source_best, TINY)
        root = jnp.concatenate(root_rows(source_best), axis=0)
        place = rows * window + 2 * row
        for target in range(send_ref.shape[0]):
            first = SUBLANES + target * local - 2
            send_ref[target, row * window : (row + 1) * window] = (
                order_ref[row, first : first + window, :] * scale
            )
            send_ref[target, place : place + 2] = root
    used = rows * (window + 2)
    spare = send_ref.shape[1] - used
    if spare:
        for target in range(send_ref.shape[0]):
            send_ref[target, used:] = jnp.zeros((spare, columns), F32)


def root_rows(best):
    root = jnp.sqrt(jnp.sqrt(jnp.sqrt(best)))
    high = root.astype(BF16).astype(F32)
    return high, root - high


def best_of_root(rows):
    root = rows[:1] + rows[1:]
    for _ in range(3):
        root = root * root
    return root


def row_of_column(column, lanes):
    row = lax.broadcasted_iota(jnp.int32, (column.shape[0], lanes), 0)
    lane = lax.broadcasted_iota(jnp.int32, (column.shape[0], lanes), 1)
    return jnp.sum(jnp.where(row == lane, column, 0.0), axis=0, keepdims=True)


def column_of_row(values, count):
    row = lax.broadcasted_iota(jnp.int32, (count, values.shape[1]), 0)
    lane = lax.broadcasted_iota(jnp.int32, (count, values.shape[1]), 1)
    return jnp.sum(jnp.where(row == lane, values, 0.0), axis=1, keepdims=True)


def lane_shifts(value):
    lanes = value.shape[-1]
    lane = lax.broadcasted_iota(jnp.int32, value.shape, value.ndim - 1)
    axis = value.ndim - 1
    left = jnp.where(lane == 0, 0.0, pltpu.roll(value, 1, axis))
    right = jnp.where(lane == lanes - 1, 0.0, pltpu.roll(value, lanes - 1, axis))
    return left, right


def consensus_kernel(
    parts, local, rows, came_ref, first_ref, second_ref, send_ref, tile_ref, partial_ref, rows_ref, pair_ref
):
    devices, _, columns = came_ref.shape
    window = max(SUBLANES, local + 4)
    grid_rows = devices * rows
    tile = len(ORDER) * SUBLANES
    again = REPEATED * SUBLANES
    zero = jnp.zeros((SUBLANES, columns), F32)

    def piece_of(device, row, first):
        return rows_ref[device * rows + row, first : first + SUBLANES, :]

    def survey(device, best):
        best = list(best)
        for row in range(rows):
            place = rows * window + 2 * row
            largest = best_of_root(came_ref[device, place : place + 2])
            block = came_ref[device, row * window : (row + 1) * window] * largest
            rows_ref[device * rows + row, :window] = block
            rows_ref[device * rows + row, window : window + 1] = 1.0 / (largest + EPSILON)
            for number, (first, _, _) in enumerate(parts):
                best[number] = jnp.maximum(best[number], block[first : first + SUBLANES])
        return tuple(best)

    best = lax.fori_loop(0, devices, survey, (zero,) * len(parts), unroll=4)
    scales = [
        jnp.broadcast_to(1.0 / (jnp.max(most, axis=1, keepdims=True) + EPSILON), most.shape)
        for most in best
    ]

    blank = jnp.zeros((tile, columns), BF16)
    for number in range(len(parts)):
        tile_ref[0, number] = blank

    def build(device):
        if isinstance(device, int) and device == devices:
            for row in range(rows):
                for number in range(len(parts)):
                    tile_ref[device * rows + row + 1, number] = blank
            return
        source = device
        for row in range(rows):
            inverse = rows_ref[source * rows + row, window : window + 1, :]
            for number, (first, _, _) in enumerate(parts):
                value = piece_of(source, row, first)
                value = value * (value * inverse) * (value * scales[number])
                left, right = lane_shifts(value)
                moved = (left, value, right)
                high = [piece.astype(BF16).astype(F32) for piece in moved]
                low = [piece - rounded for piece, rounded in zip(moved, high)]
                stacked = jnp.concatenate(
                    [(low if part else high)[offset] for offset, part in ORDER], axis=0
                )
                tile_ref[device * rows + row + 1, number] = stacked.astype(BF16)

    partial_rows = second_ref.shape[0] // 2
    empty = jnp.zeros((partial_rows, columns), F32)
    partial_ref[0] = empty
    partial_ref[grid_rows + 1] = empty

    def layer_one(device):
        base = device * rows
        hidden = []
        offset = 0
        for number, (_, _, size) in enumerate(parts):
            taps = []
            for side in range(rows):
                pieces = [tile_ref[base + side + c, number] for c in range(3)]
                pieces += [tile_ref[base + side + c, number, :again] for c in range(3)]
                taps.append(jnp.concatenate(pieces, axis=0))
            count = size * first_ref.shape[0] // (local + 2)
            hidden.append(
                jnp.dot(
                    first_ref[offset : offset + count],
                    jnp.concatenate(taps, axis=1),
                    preferred_element_type=F32,
                )
            )
            offset += count
        place = 0
        deep = pair_ref.shape[1] // 2
        for piece in hidden:
            high, low = split(jnp.maximum(piece, 0.0))
            size = piece.shape[0]
            pair_ref[device % 2, place : place + size] = high
            pair_ref[device % 2, deep + place : deep + place + size] = low
            place += size

    def layer_two(device):
        base = device * rows
        pair = pair_ref[device % 2]
        deep = pair.shape[0]
        cut = deep // MATRIX * MATRIX
        if 2 * cut < deep:
            cut = deep
        partial = jnp.dot(second_ref[:, :cut], pair[:cut], preferred_element_type=F32)
        partial = partial[:partial_rows] + partial[partial_rows:]
        if cut < deep:
            partial = partial + jnp.dot(
                second_ref[:partial_rows, cut:], pair[cut:], preferred_element_type=F32
            )
        for side in range(rows):
            partial_ref[base + side + 1] = partial[:, side * columns : (side + 1) * columns]

    def gather(device, most):
        for row in range(rows):
            total = None
            for branch in range(2):
                sums = []
                for d in range(3):
                    value = None
                    for c in range(3):
                        start = ((c * 3 + d) * 2 + branch) * SUBLANES
                        piece = partial_ref[device * rows + row + c, start : start + SUBLANES, :]
                        value = piece if value is None else value + piece
                    sums.append(value)
                output = lane_shifts(sums[0])[0] + sums[1] + lane_shifts(sums[2])[1]
                output = jnp.maximum(output, 0.0)
                total = output if total is None else total + output
            send_ref[device, row * SUBLANES : (row + 1) * SUBLANES] = total
            most = jnp.maximum(most, total)
        return most

    def step(device, most):
        fixed = isinstance(device, int)
        if not fixed or device + 1 < devices:
            layer_one(device + 1)
        if not fixed or device >= 2:
            most = gather(device - 2, most)
        if not fixed or device + 3 <= devices:
            build(device + 3)
        layer_two(device)
        return most

    for device in range(3):
        build(device)
    layer_one(0)
    most = zero
    ahead, behind = (2, 3) if devices > UNROLLED else (devices, 0)
    for device in range(ahead):
        most = step(device, most)
    most = lax.fori_loop(ahead, devices - behind, step, most) if behind else most
    for device in range(devices - behind, devices):
        most = step(device, most)
    for device in range(devices - 2, devices):
        most = gather(device, most)
    best = jnp.max(most, axis=1, keepdims=True)
    scale = 1.0 / jnp.maximum(best, TINY)
    root = jnp.concatenate(
        [row_of_column(piece, columns) for piece in root_rows(best)]
        + [jnp.zeros((SUBLANES - 2, columns), F32)],
        axis=0,
    )
    for device in range(devices):
        for row in range(rows):
            start = row * SUBLANES
            send_ref[device, start : start + SUBLANES] = (
                send_ref[device, start : start + SUBLANES] * scale
            )
        send_ref[device, rows * SUBLANES :] = root


def finish_kernel(local, came_ref, out_ref):
    devices, _, columns = came_ref.shape
    rows = out_ref.shape[1]
    place = rows * SUBLANES
    bests = [
        column_of_row(best_of_root(came_ref[device, place : place + 2]), SUBLANES)
        for device in range(devices)
    ]
    for row in range(rows):
        first = row * SUBLANES
        most = jnp.zeros((SUBLANES, columns), F32)
        for device in range(devices):
            most = jnp.maximum(most, came_ref[device, first : first + SUBLANES] * bests[device])
        inverse = 1.0 / (jnp.max(most, axis=0, keepdims=True) + EPSILON)
        for device in range(devices):
            value = came_ref[device, first : first + SUBLANES] * bests[device]
            value = value * (value * inverse) * (value * (1.0 / (bests[device] + EPSILON)))
            out_ref[device * local : (device + 1) * local, row, :] = value[:local]


def exchange(slots):
    return lax.all_to_all(slots, "tgt", 0, 0, tiled=True)


def exchange_relative(slots):
    return exchange(slots.astype(jnp.float16)).astype(F32)


def room(*shapes):
    scratch = sum(int(np.prod(shape)) * jnp.dtype(kind).itemsize for shape, kind in shapes)
    return pltpu.CompilerParams(vmem_limit_bytes=scratch + 6 * 2**20)


VMEM = pl.BlockSpec(memory_space=pltpu.VMEM)
ANY = pl.BlockSpec(memory_space=pltpu.HBM)


def shards(source_features, target_features, conv_first, conv_second):
    devices = lax.axis_size("tgt")
    rows, columns, channels = target_features.shape
    cells = source_features.shape[0] * devices
    hid = conv_first.shape[0]
    local = cells // devices
    parts = parts_of(local)
    hidden = local + 2
    window = max(SUBLANES, local + 4)
    tile = len(ORDER) * SUBLANES
    width = 3 * (tile + REPEATED * SUBLANES)
    depth = hidden * 2 * hid
    assert local <= SUBLANES and rows * devices % 4 == 0

    (spread,) = pl.pallas_call(
        spread_kernel,
        out_shape=(
            jax.ShapeDtypeStruct((devices, source_features.shape[0], channels // 2), BF16),
        ),
        in_specs=[ANY] * 1,
        out_specs=(VMEM,) * 1,
        scratch_shapes=[
            pltpu.VMEM(source_features.shape, BF16),
            pltpu.SemaphoreType.DMA((1,)),
        ],
        compiler_params=room(),
        name="spread",
    )(
        *(
            pltpu.with_memory_space_constraint(value, pltpu.HBM)
            for value in (source_features,)
        )
    )
    mine = exchange(spread).reshape(cells, channels // 2)
    other = lax.ppermute(mine, "tgt", [(i, i ^ 1) for i in range(devices)])

    second_rows = 18 * SUBLANES
    first_weights, second_weights = pl.pallas_call(
        functools.partial(prepare_kernel, devices, local, parts),
        out_shape=(
            jax.ShapeDtypeStruct((depth, width), BF16),
            jax.ShapeDtypeStruct((2 * second_rows, 2 * depth), BF16),
        ),
        in_specs=[VMEM] * 2 + [pl.BlockSpec(memory_space=pl.ANY)],
        out_specs=(VMEM,) * 2,
        scratch_shapes=[pltpu.VMEM((4 * TAP_PAD, 128), F32)],
        cost_estimate=pl.CostEstimate(flops=10**9, bytes_accessed=10**6, transcendentals=0),
        compiler_params=room(),
        name="prepare",
    )(
        jnp.transpose(conv_first, (1, 2, 3, 4, 0)),
        jnp.transpose(conv_second, (1, 2, 3, 4, 0)),
        mine,
    )
    target_unit = pl.pallas_call(
        target_kernel,
        out_shape=jax.ShapeDtypeStruct((rows * columns, channels), BF16),
        in_specs=[VMEM, pl.BlockSpec(memory_space=pl.ANY)],
        out_specs=VMEM,
        cost_estimate=pl.CostEstimate(flops=10**6, bytes_accessed=10**6, transcendentals=0),
        compiler_params=room(),
        name="target",
    )(target_features, first_weights)

    slots = pl.pallas_call(
        functools.partial(match_kernel, local),
        out_shape=jax.ShapeDtypeStruct((devices, whole_tiles(rows * (window + 2)), columns), F32),
        in_specs=[VMEM] * 3,
        out_specs=VMEM,
        scratch_shapes=[
            pltpu.VMEM((cells, channels), BF16),
            pltpu.VMEM((rows, cells + 2 * SUBLANES, columns), F32),
        ],
        compiler_params=room(),
        name="match",
    )(mine, other, target_unit)

    stores = (
        ((rows * (devices + 1) + 1, len(parts), tile, columns), BF16),
        ((rows * devices + 2, second_rows, columns), F32),
        ((rows * devices, whole_tiles(window + 1), columns), F32),
        ((2, 2 * depth, rows * columns), BF16),
    )
    slots = pl.pallas_call(
        functools.partial(consensus_kernel, parts, local, rows),
        out_shape=jax.ShapeDtypeStruct((devices, (rows + 1) * SUBLANES, columns), F32),
        in_specs=[VMEM] * 3,
        out_specs=VMEM,
        scratch_shapes=[pltpu.VMEM(shape, kind) for shape, kind in stores],
        compiler_params=room(*stores),
        name="consensus",
    )(exchange_relative(slots), first_weights, second_weights)

    filtered = pl.pallas_call(
        functools.partial(finish_kernel, local),
        out_shape=jax.ShapeDtypeStruct((cells, rows, columns), F32),
        in_specs=[VMEM],
        out_specs=VMEM,
        compiler_params=room(),
        name="finish",
    )(exchange_relative(slots))
    return filtered[None]


def solution(mesh):
    placed = (P(("pairs", "tgt"), None), P(("pairs", "tgt"), None, None), P(), P())
    return jax.shard_map(
        shards, mesh=mesh, in_specs=placed, out_specs=P("pairs", None, "tgt", None), check_vma=False
    )
```

```python
import functools

import jax
import jax.numpy as jnp
import numpy as np
from jax import lax
from jax.experimental import pallas as pl
from jax.experimental.pallas import tpu as pltpu
from jax.sharding import PartitionSpec as P

EPSILON = 1e-05
TINY = 1e-30
MATRIX = 256
UNROLLED = 16
F32 = jnp.float32
BF16 = jnp.bfloat16
TAPS = 27
TAP_PAD = 32
SUBLANES = 8
ORDER = ((0, 0), (1, 0), (2, 0), (0, 1), (1, 1), (2, 1))
REPEATED = 4


def whole_tiles(count):
    return -(-count // SUBLANES) * SUBLANES


def parts_of(local):
    hidden = local + 2
    count = -(-hidden // (SUBLANES - 2))
    size = -(-hidden // count)
    parts = []
    for start in range(0, hidden, size):
        first = min(start, max(0, local + 4 - SUBLANES))
        parts.append((first, start, min(size, hidden - start)))
    return parts


def tap_fields(tap):
    return tap // 9, tap // 3 % 3, tap % 3


def first_codes(width):
    row = lax.broadcasted_iota(jnp.int32, (2 * TAP_PAD, 128), 0)
    b, c, d = tap_fields(row % TAP_PAD)
    rows = ((row // TAP_PAD * 3 + c) * 3 + d) * 16 + b
    rows = jnp.where(row % TAP_PAD < TAPS, rows, -100)[:, :1]
    column = lax.broadcasted_iota(jnp.int32, (SUBLANES, width), 1)
    tile, again = len(ORDER) * SUBLANES, REPEATED * SUBLANES
    extra = column >= 3 * tile
    rest = column - 3 * tile
    c = jnp.where(extra, rest // again, column // tile)
    place = jnp.where(extra, rest % again, column % tile) // SUBLANES
    code = ((jnp.where(extra, 3, 0) + c) * 3 + place % 3) * 16 + column % SUBLANES
    columns = jnp.where(extra & (place >= 3), -1, code)[:1]
    return rows, columns


def second_selector(local, blocks):
    height, width = 18 * SUBLANES, blocks * 2 * TAP_PAD
    row = lax.broadcasted_iota(jnp.int32, (height, 128), 0)
    rows = row // SUBLANES * 32 + row % SUBLANES
    rows = jnp.where(row % SUBLANES < local, rows, -100)[:, :1]
    column = lax.broadcasted_iota(jnp.int32, (SUBLANES, width), 1)
    tap = column % TAP_PAD
    b, c, d = tap_fields(tap)
    cell = column // (2 * TAP_PAD) - b
    code = ((c * 3 + d) * 2 + column // TAP_PAD % 2) * 32 + cell
    columns = jnp.where((tap < TAPS) & (cell >= 0), code, -1)[:1]
    return jnp.where(rows == columns, 1.0, 0.0).astype(BF16)


def unit(features):
    positive = jnp.maximum(features.astype(F32), 0.0)
    length = jnp.sqrt(jnp.sum(positive * positive, axis=-1, keepdims=True) + 1e-06)
    return (positive / length).astype(BF16)


def split(value):
    high = value.astype(BF16)
    return high, (value - high.astype(F32)).astype(BF16)


def prepare_kernel(
    devices, local, parts, first_ref, second_ref, gate_ref, first_out, second_out, taps_ref
):
    hid = first_ref.shape[-1]
    taps_ref[...] = jnp.zeros(taps_ref.shape, F32)
    for number, ref in enumerate((first_ref, second_ref)):
        base = 2 * TAP_PAD * number
        for b in range(3):
            for c in range(3):
                start = base + (b * 3 + c) * 3
                taps_ref[start : start + 3, :hid] = ref[1, b, c]
        for c in range(3):
            for d in range(3):
                piece = ref[c, d, 1]
                for b in range(3):
                    start = base + TAP_PAD + (b * 3 + c) * 3 + d
                    taps_ref[start : start + 1, :hid] = piece[b : b + 1]
    branches = [taps_ref[i * TAP_PAD : (i + 1) * TAP_PAD, :hid] for i in range(4)]
    width = first_out.shape[1]
    taps = jnp.concatenate(split(jnp.concatenate(branches[:2], axis=1)), axis=0)
    blocks = first_out.shape[0] // (2 * hid)
    rows_code, columns_code = first_codes(width)
    for block in range(blocks):
        first = [part[0] for part in parts if part[1] <= block][-1]
        pick = jnp.where(rows_code + (block - first) == columns_code, 1.0, 0.0).astype(BF16)
        piece = lax.dot_general(
            taps, pick, (((0,), (0,)), ((), ())), preferred_element_type=F32
        )
        if block == 0:
            piece = piece * jnp.where(lax.axis_index("tgt") == 0, 0.0, 1.0)
        if block == blocks - 1:
            piece = piece * jnp.where(lax.axis_index("tgt") == devices - 1, 0.0, 1.0)
        first_out[block * 2 * hid : (block + 1) * 2 * hid] = piece.astype(BF16)
    depth = blocks * 2 * hid
    groups = blocks * 2
    row_group = lax.broadcasted_iota(jnp.int32, (groups * TAP_PAD, depth), 0) // TAP_PAD
    lane_group = lax.broadcasted_iota(jnp.int32, (groups * TAP_PAD, depth), 1) // hid
    tiled = jnp.concatenate([jnp.concatenate(branches[2:], axis=1)] * blocks, axis=1)
    tiled = jnp.concatenate([tiled] * groups, axis=0)
    tiled = jnp.where(row_group == lane_group, tiled, 0.0)
    high, low = split(tiled)
    half = second_out.shape[0] // 2
    scatter = second_selector(local, blocks)
    high = jnp.dot(scatter, high, preferred_element_type=F32).astype(BF16)
    low = jnp.dot(scatter, low, preferred_element_type=F32).astype(BF16)
    second_out[:half, :depth] = high
    second_out[:half, depth:] = high
    second_out[half:, :depth] = low
    second_out[half:, depth:] = jnp.zeros_like(low)


def target_kernel(target_ref, gate_ref, unit_ref):
    rows, columns = target_ref.shape[:2]
    for row in range(rows):
        unit_ref[row * columns : (row + 1) * columns] = unit(target_ref[row])


def match_kernel(
    local, masks, near_ref, far_ref, target_ref, send_ref, source_ref, order_ref
):
    rows, padded, columns = order_ref.shape
    cells = padded - 2 * SUBLANES
    middle = near_ref.shape[0]
    source_ref[:middle] = unit(near_ref[...])
    source_ref[middle:] = unit(far_ref[...])
    correlation = lax.dot_general(
        source_ref[...], target_ref[...], (((1,), (1,)), ((), ())), preferred_element_type=F32
    )
    position = lax.axis_index("tgt")
    window = max(SUBLANES, local + 4)
    blank = jnp.zeros((SUBLANES, columns), F32)
    for row in range(rows):
        order_ref[row, :SUBLANES, :] = blank
        order_ref[row, SUBLANES + cells :, :] = blank
        for piece, mask in enumerate(masks):
            start = SUBLANES + (position ^ mask) * local
            if local % SUBLANES == 0:
                start = pl.multiple_of(start, SUBLANES)
            order_ref[row, pl.ds(start, local), :] = correlation[
                piece * local : (piece + 1) * local, row * columns : (row + 1) * columns
            ]
        source_best = jnp.max(order_ref[row], axis=0, keepdims=True)
        scale = 1.0 / jnp.maximum(source_best, TINY)
        root = jnp.concatenate(root_rows(source_best), axis=0)
        place = rows * window + 2 * row
        for target in range(send_ref.shape[0]):
            first = SUBLANES + target * local - 2
            send_ref[target, row * window : (row + 1) * window] = (
                order_ref[row, first : first + window, :] * scale
            )
            send_ref[target, place : place + 2] = root
    used = rows * (window + 2)
    spare = send_ref.shape[1] - used
    if spare:
        for target in range(send_ref.shape[0]):
            send_ref[target, used:] = jnp.zeros((spare, columns), F32)


def root_rows(best):
    root = jnp.sqrt(jnp.sqrt(jnp.sqrt(best)))
    high = root.astype(BF16).astype(F32)
    return high, root - high


def best_of_root(rows):
    root = rows[:1] + rows[1:]
    for _ in range(3):
        root = root * root
    return root


def row_of_column(column, lanes):
    row = lax.broadcasted_iota(jnp.int32, (column.shape[0], lanes), 0)
    lane = lax.broadcasted_iota(jnp.int32, (column.shape[0], lanes), 1)
    return jnp.sum(jnp.where(row == lane, column, 0.0), axis=0, keepdims=True)


def column_of_row(values, count):
    row = lax.broadcasted_iota(jnp.int32, (count, values.shape[1]), 0)
    lane = lax.broadcasted_iota(jnp.int32, (count, values.shape[1]), 1)
    return jnp.sum(jnp.where(row == lane, values, 0.0), axis=1, keepdims=True)


def lane_shifts(value):
    lanes = value.shape[-1]
    lane = lax.broadcasted_iota(jnp.int32, value.shape, value.ndim - 1)
    axis = value.ndim - 1
    left = jnp.where(lane == 0, 0.0, pltpu.roll(value, 1, axis))
    right = jnp.where(lane == lanes - 1, 0.0, pltpu.roll(value, lanes - 1, axis))
    return left, right


def consensus_kernel(
    parts, local, rows, came_ref, first_ref, second_ref, send_ref, tile_ref, partial_ref, rows_ref, pair_ref
):
    devices, _, columns = came_ref.shape
    window = max(SUBLANES, local + 4)
    grid_rows = devices * rows
    tile = len(ORDER) * SUBLANES
    again = REPEATED * SUBLANES
    zero = jnp.zeros((SUBLANES, columns), F32)

    def piece_of(device, row, first):
        return rows_ref[device * rows + row, first : first + SUBLANES, :]

    def survey(device, best):
        best = list(best)
        for row in range(rows):
            place = rows * window + 2 * row
            largest = best_of_root(came_ref[device, place : place + 2])
            block = came_ref[device, row * window : (row + 1) * window] * largest
            rows_ref[device * rows + row, :window] = block
            rows_ref[device * rows + row, window : window + 1] = 1.0 / (largest + EPSILON)
            for number, (first, _, _) in enumerate(parts):
                best[number] = jnp.maximum(best[number], block[first : first + SUBLANES])
        return tuple(best)

    best = lax.fori_loop(0, devices, survey, (zero,) * len(parts), unroll=4)
    scales = [
        jnp.broadcast_to(1.0 / (jnp.max(most, axis=1, keepdims=True) + EPSILON), most.shape)
        for most in best
    ]

    blank = jnp.zeros((tile, columns), BF16)
    for number in range(len(parts)):
        tile_ref[0, number] = blank

    def build(device):
        if isinstance(device, int) and device == devices:
            for row in range(rows):
                for number in range(len(parts)):
                    tile_ref[device * rows + row + 1, number] = blank
            return
        source = device
        for row in range(rows):
            inverse = rows_ref[source * rows + row, window : window + 1, :]
            for number, (first, _, _) in enumerate(parts):
                value = piece_of(source, row, first)
                value = value * (value * inverse) * (value * scales[number])
                left, right = lane_shifts(value)
                moved = (left, value, right)
                high = [piece.astype(BF16).astype(F32) for piece in moved]
                low = [piece - rounded for piece, rounded in zip(moved, high)]
                stacked = jnp.concatenate(
                    [(low if part else high)[offset] for offset, part in ORDER], axis=0
                )
                tile_ref[device * rows + row + 1, number] = stacked.astype(BF16)

    partial_rows = second_ref.shape[0] // 2
    empty = jnp.zeros((partial_rows, columns), F32)
    partial_ref[0] = empty
    partial_ref[grid_rows + 1] = empty

    def layer_one(device):
        base = device * rows
        hidden = []
        offset = 0
        for number, (_, _, size) in enumerate(parts):
            taps = []
            for side in range(rows):
                pieces = [tile_ref[base + side + c, number] for c in range(3)]
                pieces += [tile_ref[base + side + c, number, :again] for c in range(3)]
                taps.append(jnp.concatenate(pieces, axis=0))
            count = size * first_ref.shape[0] // (local + 2)
            hidden.append(
                jnp.dot(
                    first_ref[offset : offset + count],
                    jnp.concatenate(taps, axis=1),
                    preferred_element_type=F32,
                )
            )
            offset += count
        place = 0
        deep = pair_ref.shape[1] // 2
        for piece in hidden:
            high, low = split(jnp.maximum(piece, 0.0))
            size = piece.shape[0]
            pair_ref[device % 2, place : place + size] = high
            pair_ref[device % 2, deep + place : deep + place + size] = low
            place += size

    def layer_two(device):
        base = device * rows
        pair = pair_ref[device % 2]
        deep = pair.shape[0]
        cut = deep // MATRIX * MATRIX
        if 2 * cut < deep:
            cut = deep
        partial = jnp.dot(second_ref[:, :cut], pair[:cut], preferred_element_type=F32)
        partial = partial[:partial_rows] + partial[partial_rows:]
        if cut < deep:
            partial = partial + jnp.dot(
                second_ref[:partial_rows, cut:], pair[cut:], preferred_element_type=F32
            )
        for side in range(rows):
            partial_ref[base + side + 1] = partial[:, side * columns : (side + 1) * columns]

    def gather(device, most):
        for row in range(rows):
            total = None
            for branch in range(2):
                sums = []
                for d in range(3):
                    value = None
                    for c in range(3):
                        start = ((c * 3 + d) * 2 + branch) * SUBLANES
                        piece = partial_ref[device * rows + row + c, start : start + SUBLANES, :]
                        value = piece if value is None else value + piece
                    sums.append(value)
                output = lane_shifts(sums[0])[0] + sums[1] + lane_shifts(sums[2])[1]
                output = jnp.maximum(output, 0.0)
                total = output if total is None else total + output
            send_ref[device, row * SUBLANES : (row + 1) * SUBLANES] = total
            most = jnp.maximum(most, total)
        return most

    def step(device, most):
        fixed = isinstance(device, int)
        if not fixed or device + 1 < devices:
            layer_one(device + 1)
        if not fixed or device >= 2:
            most = gather(device - 2, most)
        if not fixed or device + 3 <= devices:
            build(device + 3)
        layer_two(device)
        return most

    for device in range(3):
        build(device)
    layer_one(0)
    most = zero
    ahead, behind = (2, 3) if devices > UNROLLED else (devices, 0)
    for device in range(ahead):
        most = step(device, most)
    most = lax.fori_loop(ahead, devices - behind, step, most) if behind else most
    for device in range(devices - behind, devices):
        most = step(device, most)
    for device in range(devices - 2, devices):
        most = gather(device, most)
    best = jnp.max(most, axis=1, keepdims=True)
    scale = 1.0 / jnp.maximum(best, TINY)
    root = jnp.concatenate(
        [row_of_column(piece, columns) for piece in root_rows(best)]
        + [jnp.zeros((SUBLANES - 2, columns), F32)],
        axis=0,
    )
    for device in range(devices):
        for row in range(rows):
            start = row * SUBLANES
            send_ref[device, start : start + SUBLANES] = (
                send_ref[device, start : start + SUBLANES] * scale
            )
        send_ref[device, rows * SUBLANES :] = root


def finish_kernel(local, came_ref, out_ref):
    devices, _, columns = came_ref.shape
    rows = out_ref.shape[1]
    place = rows * SUBLANES
    bests = [
        column_of_row(best_of_root(came_ref[device, place : place + 2]), SUBLANES)
        for device in range(devices)
    ]
    for row in range(rows):
        first = row * SUBLANES
        most = jnp.zeros((SUBLANES, columns), F32)
        for device in range(devices):
            most = jnp.maximum(most, came_ref[device, first : first + SUBLANES] * bests[device])
        inverse = 1.0 / (jnp.max(most, axis=0, keepdims=True) + EPSILON)
        for device in range(devices):
            value = came_ref[device, first : first + SUBLANES] * bests[device]
            value = value * (value * inverse) * (value * (1.0 / (bests[device] + EPSILON)))
            out_ref[device * local : (device + 1) * local, row, :] = value[:local]


def gather_sources(value, devices):
    bits = []
    bit = 1
    while bit < devices:
        bits.append(bit)
        bit *= 2
    upper = bits[2:]
    stages = [[2]]
    for first in range(0, len(upper), 2):
        pair = upper[first : first + 2]
        stages.append(pair if len(pair) == 1 else [pair[0], pair[0] ^ pair[1], pair[1]])
    masks = [0]
    gate = None
    for stage in stages:
        parts = [value] + [
            lax.ppermute(value, "tgt", [(i, i ^ mask) for i in range(devices)]) for mask in stage
        ]
        value = jnp.concatenate(parts, axis=0)
        masks = [mask ^ extra for extra in [0] + stage for mask in masks]
        gate = value if gate is None else gate
    return value, masks + [mask ^ 1 for mask in masks], gate


def exchange(slots):
    return lax.all_to_all(slots, "tgt", 0, 0, tiled=True)


def exchange_relative(slots):
    return exchange(slots.astype(jnp.float16)).astype(F32)


def room(*shapes):
    scratch = sum(int(np.prod(shape)) * jnp.dtype(kind).itemsize for shape, kind in shapes)
    return pltpu.CompilerParams(vmem_limit_bytes=scratch + 6 * 2**20)


VMEM = pl.BlockSpec(memory_space=pltpu.VMEM)


def shards(source_features, target_features, conv_first, conv_second):
    devices = lax.axis_size("tgt")
    rows, columns, channels = target_features.shape
    cells = source_features.shape[0] * devices
    hid = conv_first.shape[0]
    local = cells // devices
    parts = parts_of(local)
    hidden = local + 2
    window = max(SUBLANES, local + 4)
    tile = len(ORDER) * SUBLANES
    width = 3 * (tile + REPEATED * SUBLANES)
    depth = hidden * 2 * hid
    assert local <= SUBLANES and rows * devices % 4 == 0

    near, masks, mine = gather_sources(source_features, devices)

    second_rows = 18 * SUBLANES
    first_weights, second_weights = pl.pallas_call(
        functools.partial(prepare_kernel, devices, local, parts),
        out_shape=(
            jax.ShapeDtypeStruct((depth, width), BF16),
            jax.ShapeDtypeStruct((2 * second_rows, 2 * depth), BF16),
        ),
        in_specs=[VMEM] * 2 + [pl.BlockSpec(memory_space=pl.ANY)],
        out_specs=(VMEM,) * 2,
        scratch_shapes=[pltpu.VMEM((4 * TAP_PAD, 128), F32)],
        cost_estimate=pl.CostEstimate(flops=10**9, bytes_accessed=10**6, transcendentals=0),
        compiler_params=room(),
        name="prepare",
    )(
        jnp.transpose(conv_first, (1, 2, 3, 4, 0)),
        jnp.transpose(conv_second, (1, 2, 3, 4, 0)),
        mine,
    )
    target_unit = pl.pallas_call(
        target_kernel,
        out_shape=jax.ShapeDtypeStruct((rows * columns, channels), BF16),
        in_specs=[VMEM, pl.BlockSpec(memory_space=pl.ANY)],
        out_specs=VMEM,
        cost_estimate=pl.CostEstimate(flops=10**6, bytes_accessed=10**6, transcendentals=0),
        compiler_params=room(),
        name="target",
    )(target_features, first_weights)

    near, target_unit, first_weights = lax.optimization_barrier(
        (near, target_unit, first_weights)
    )
    far = lax.ppermute(near, "tgt", [(i, i ^ 1) for i in range(devices)])
    slots = pl.pallas_call(
        functools.partial(match_kernel, local, masks),
        out_shape=jax.ShapeDtypeStruct((devices, whole_tiles(rows * (window + 2)), columns), F32),
        in_specs=[VMEM] * 3,
        out_specs=VMEM,
        scratch_shapes=[
            pltpu.VMEM((cells, channels), BF16),
            pltpu.VMEM((rows, cells + 2 * SUBLANES, columns), F32),
        ],
        compiler_params=room(),
        name="match",
    )(near, far, target_unit)

    stores = (
        ((rows * (devices + 1) + 1, len(parts), tile, columns), BF16),
        ((rows * devices + 2, second_rows, columns), F32),
        ((rows * devices, whole_tiles(window + 1), columns), F32),
        ((2, 2 * depth, rows * columns), BF16),
    )
    slots = pl.pallas_call(
        functools.partial(consensus_kernel, parts, local, rows),
        out_shape=jax.ShapeDtypeStruct((devices, (rows + 1) * SUBLANES, columns), F32),
        in_specs=[VMEM] * 3,
        out_specs=VMEM,
        scratch_shapes=[pltpu.VMEM(shape, kind) for shape, kind in stores],
        compiler_params=room(*stores),
        name="consensus",
    )(exchange_relative(slots), first_weights, second_weights)

    filtered = pl.pallas_call(
        functools.partial(finish_kernel, local),
        out_shape=jax.ShapeDtypeStruct((cells, rows, columns), F32),
        in_specs=[VMEM],
        out_specs=VMEM,
        compiler_params=room(),
        name="finish",
    )(exchange_relative(slots))
    return filtered[None]


def solution(mesh):
    placed = (P(("pairs", "tgt"), None), P(("pairs", "tgt"), None, None), P(), P())
    return jax.shard_map(
        shards, mesh=mesh, in_specs=placed, out_specs=P("pairs", None, "tgt", None), check_vma=False
    )
```

```python
import functools

import jax
import jax.numpy as jnp
import numpy as np
from jax import lax
from jax.experimental import pallas as pl
from jax.experimental.pallas import tpu as pltpu
from jax.sharding import PartitionSpec as P

EPSILON = 1e-05
TINY = 1e-30
MATRIX = 256
UNROLLED = 16
F32 = jnp.float32
BF16 = jnp.bfloat16
TAPS = 27
TAP_PAD = 32
SUBLANES = 8
ORDER = ((0, 0), (1, 0), (2, 0), (0, 1), (1, 1), (2, 1))
REPEATED = 4


def whole_tiles(count):
    return -(-count // SUBLANES) * SUBLANES


def parts_of(local):
    hidden = local + 2
    count = -(-hidden // (SUBLANES - 2))
    size = -(-hidden // count)
    parts = []
    for start in range(0, hidden, size):
        first = min(start, max(0, local + 4 - SUBLANES))
        parts.append((first, start, min(size, hidden - start)))
    return parts


def tap_fields(tap):
    return tap // 9, tap // 3 % 3, tap % 3


def first_codes(width):
    row = lax.broadcasted_iota(jnp.int32, (2 * TAP_PAD, 128), 0)
    b, c, d = tap_fields(row % TAP_PAD)
    rows = ((row // TAP_PAD * 3 + c) * 3 + d) * 16 + b
    rows = jnp.where(row % TAP_PAD < TAPS, rows, -100)[:, :1]
    column = lax.broadcasted_iota(jnp.int32, (SUBLANES, width), 1)
    tile, again = len(ORDER) * SUBLANES, REPEATED * SUBLANES
    extra = column >= 3 * tile
    rest = column - 3 * tile
    c = jnp.where(extra, rest // again, column // tile)
    place = jnp.where(extra, rest % again, column % tile) // SUBLANES
    code = ((jnp.where(extra, 3, 0) + c) * 3 + place % 3) * 16 + column % SUBLANES
    columns = jnp.where(extra & (place >= 3), -1, code)[:1]
    return rows, columns


def second_selector(local, blocks):
    height, width = 18 * SUBLANES, blocks * 2 * TAP_PAD
    row = lax.broadcasted_iota(jnp.int32, (height, 128), 0)
    rows = row // SUBLANES * 32 + row % SUBLANES
    rows = jnp.where(row % SUBLANES < local, rows, -100)[:, :1]
    column = lax.broadcasted_iota(jnp.int32, (SUBLANES, width), 1)
    tap = column % TAP_PAD
    b, c, d = tap_fields(tap)
    cell = column // (2 * TAP_PAD) - b
    code = ((c * 3 + d) * 2 + column // TAP_PAD % 2) * 32 + cell
    columns = jnp.where((tap < TAPS) & (cell >= 0), code, -1)[:1]
    return jnp.where(rows == columns, 1.0, 0.0).astype(BF16)


def unit(features):
    positive = jnp.maximum(features.astype(F32), 0.0)
    length = jnp.sqrt(jnp.sum(positive * positive, axis=-1, keepdims=True) + 1e-06)
    return (positive / length).astype(BF16)


def split(value):
    high = value.astype(BF16)
    return high, (value - high.astype(F32)).astype(BF16)


def prepare_kernel(
    devices, local, parts, first_ref, second_ref, gate_ref, first_out, second_out, taps_ref
):
    hid = first_ref.shape[-1]
    taps_ref[...] = jnp.zeros(taps_ref.shape, F32)
    for number, ref in enumerate((first_ref, second_ref)):
        base = 2 * TAP_PAD * number
        for b in range(3):
            for c in range(3):
                start = base + (b * 3 + c) * 3
                taps_ref[start : start + 3, :hid] = ref[1, b, c]
        for c in range(3):
            for d in range(3):
                piece = ref[c, d, 1]
                for b in range(3):
                    start = base + TAP_PAD + (b * 3 + c) * 3 + d
                    taps_ref[start : start + 1, :hid] = piece[b : b + 1]
    branches = [taps_ref[i * TAP_PAD : (i + 1) * TAP_PAD, :hid] for i in range(4)]
    width = first_out.shape[1]
    taps = jnp.concatenate(split(jnp.concatenate(branches[:2], axis=1)), axis=0)
    blocks = first_out.shape[0] // (2 * hid)
    rows_code, columns_code = first_codes(width)
    for block in range(blocks):
        first = [part[0] for part in parts if part[1] <= block][-1]
        pick = jnp.where(rows_code + (block - first) == columns_code, 1.0, 0.0).astype(BF16)
        piece = lax.dot_general(
            taps, pick, (((0,), (0,)), ((), ())), preferred_element_type=F32
        )
        if block == 0:
            piece = piece * jnp.where(lax.axis_index("tgt") == 0, 0.0, 1.0)
        if block == blocks - 1:
            piece = piece * jnp.where(lax.axis_index("tgt") == devices - 1, 0.0, 1.0)
        first_out[block * 2 * hid : (block + 1) * 2 * hid] = piece.astype(BF16)
    depth = blocks * 2 * hid
    groups = blocks * 2
    row_group = lax.broadcasted_iota(jnp.int32, (groups * TAP_PAD, depth), 0) // TAP_PAD
    lane_group = lax.broadcasted_iota(jnp.int32, (groups * TAP_PAD, depth), 1) // hid
    tiled = jnp.concatenate([jnp.concatenate(branches[2:], axis=1)] * blocks, axis=1)
    tiled = jnp.concatenate([tiled] * groups, axis=0)
    tiled = jnp.where(row_group == lane_group, tiled, 0.0)
    high, low = split(tiled)
    half = second_out.shape[0] // 2
    scatter = second_selector(local, blocks)
    high = jnp.dot(scatter, high, preferred_element_type=F32).astype(BF16)
    low = jnp.dot(scatter, low, preferred_element_type=F32).astype(BF16)
    second_out[:half, :depth] = high
    second_out[:half, depth:] = high
    second_out[half:, :depth] = low
    second_out[half:, depth:] = jnp.zeros_like(low)


def target_kernel(target_ref, gate_ref, unit_ref):
    rows, columns = target_ref.shape[:2]
    for row in range(rows):
        unit_ref[row * columns : (row + 1) * columns] = unit(target_ref[row])


def correlate(source, target):
    return lax.dot_general(
        unit(source), target, (((1,), (1,)), ((), ())), preferred_element_type=F32
    )


def near_kernel(near_ref, target_ref, out_ref):
    out_ref[...] = correlate(near_ref[...], target_ref[...])


def match_kernel(local, masks, near_ref, far_ref, target_ref, send_ref, order_ref):
    rows, padded, columns = order_ref.shape
    cells = padded - 2 * SUBLANES
    far = correlate(far_ref[...], target_ref[...])
    position = lax.axis_index("tgt")
    window = max(SUBLANES, local + 4)
    blank = jnp.zeros((SUBLANES, columns), F32)
    for row in range(rows):
        order_ref[row, :SUBLANES, :] = blank
        order_ref[row, SUBLANES + cells :, :] = blank
        lanes = slice(row * columns, (row + 1) * columns)
        middle = len(masks) // 2
        for piece, mask in enumerate(masks):
            start = SUBLANES + (position ^ mask) * local
            if local % SUBLANES == 0:
                start = pl.multiple_of(start, SUBLANES)
            held, first = (near_ref, piece) if piece < middle else (far, piece - middle)
            order_ref[row, pl.ds(start, local), :] = held[
                first * local : (first + 1) * local, lanes
            ]
        source_best = jnp.max(order_ref[row], axis=0, keepdims=True)
        scale = 1.0 / jnp.maximum(source_best, TINY)
        root = jnp.concatenate(root_rows(source_best), axis=0)
        place = rows * window + 2 * row
        for target in range(send_ref.shape[0]):
            first = SUBLANES + target * local - 2
            send_ref[target, row * window : (row + 1) * window] = (
                order_ref[row, first : first + window, :] * scale
            )
            send_ref[target, place : place + 2] = root
    used = rows * (window + 2)
    spare = send_ref.shape[1] - used
    if spare:
        for target in range(send_ref.shape[0]):
            send_ref[target, used:] = jnp.zeros((spare, columns), F32)


def root_rows(best):
    root = jnp.sqrt(jnp.sqrt(jnp.sqrt(best)))
    high = root.astype(BF16).astype(F32)
    return high, root - high


def best_of_root(rows):
    root = rows[:1] + rows[1:]
    for _ in range(3):
        root = root * root
    return root


def row_of_column(column, lanes):
    row = lax.broadcasted_iota(jnp.int32, (column.shape[0], lanes), 0)
    lane = lax.broadcasted_iota(jnp.int32, (column.shape[0], lanes), 1)
    return jnp.sum(jnp.where(row == lane, column, 0.0), axis=0, keepdims=True)


def column_of_row(values, count):
    row = lax.broadcasted_iota(jnp.int32, (count, values.shape[1]), 0)
    lane = lax.broadcasted_iota(jnp.int32, (count, values.shape[1]), 1)
    return jnp.sum(jnp.where(row == lane, values, 0.0), axis=1, keepdims=True)


def lane_shifts(value):
    lanes = value.shape[-1]
    lane = lax.broadcasted_iota(jnp.int32, value.shape, value.ndim - 1)
    axis = value.ndim - 1
    left = jnp.where(lane == 0, 0.0, pltpu.roll(value, 1, axis))
    right = jnp.where(lane == lanes - 1, 0.0, pltpu.roll(value, lanes - 1, axis))
    return left, right


def consensus_kernel(
    parts, local, rows, came_ref, first_ref, second_ref, send_ref, tile_ref, partial_ref, rows_ref, pair_ref
):
    devices, _, columns = came_ref.shape
    window = max(SUBLANES, local + 4)
    grid_rows = devices * rows
    tile = len(ORDER) * SUBLANES
    again = REPEATED * SUBLANES
    zero = jnp.zeros((SUBLANES, columns), F32)

    def piece_of(device, row, first):
        return rows_ref[device * rows + row, first : first + SUBLANES, :]

    def survey(device, best):
        best = list(best)
        for row in range(rows):
            place = rows * window + 2 * row
            largest = best_of_root(came_ref[device, place : place + 2])
            block = came_ref[device, row * window : (row + 1) * window] * largest
            rows_ref[device * rows + row, :window] = block
            rows_ref[device * rows + row, window : window + 1] = 1.0 / (largest + EPSILON)
            for number, (first, _, _) in enumerate(parts):
                best[number] = jnp.maximum(best[number], block[first : first + SUBLANES])
        return tuple(best)

    best = lax.fori_loop(0, devices, survey, (zero,) * len(parts), unroll=4)
    scales = [
        jnp.broadcast_to(1.0 / (jnp.max(most, axis=1, keepdims=True) + EPSILON), most.shape)
        for most in best
    ]

    blank = jnp.zeros((tile, columns), BF16)
    for number in range(len(parts)):
        tile_ref[0, number] = blank

    def build(device):
        if isinstance(device, int) and device == devices:
            for row in range(rows):
                for number in range(len(parts)):
                    tile_ref[device * rows + row + 1, number] = blank
            return
        source = device
        for row in range(rows):
            inverse = rows_ref[source * rows + row, window : window + 1, :]
            for number, (first, _, _) in enumerate(parts):
                value = piece_of(source, row, first)
                value = value * (value * inverse) * (value * scales[number])
                left, right = lane_shifts(value)
                moved = (left, value, right)
                high = [piece.astype(BF16).astype(F32) for piece in moved]
                low = [piece - rounded for piece, rounded in zip(moved, high)]
                stacked = jnp.concatenate(
                    [(low if part else high)[offset] for offset, part in ORDER], axis=0
                )
                tile_ref[device * rows + row + 1, number] = stacked.astype(BF16)

    partial_rows = second_ref.shape[0] // 2
    empty = jnp.zeros((partial_rows, columns), F32)
    partial_ref[0] = empty
    partial_ref[grid_rows + 1] = empty

    def layer_one(device):
        base = device * rows
        hidden = []
        offset = 0
        for number, (_, _, size) in enumerate(parts):
            taps = []
            for side in range(rows):
                pieces = [tile_ref[base + side + c, number] for c in range(3)]
                pieces += [tile_ref[base + side + c, number, :again] for c in range(3)]
                taps.append(jnp.concatenate(pieces, axis=0))
            count = size * first_ref.shape[0] // (local + 2)
            hidden.append(
                jnp.dot(
                    first_ref[offset : offset + count],
                    jnp.concatenate(taps, axis=1),
                    preferred_element_type=F32,
                )
            )
            offset += count
        place = 0
        deep = pair_ref.shape[1] // 2
        for piece in hidden:
            high, low = split(jnp.maximum(piece, 0.0))
            size = piece.shape[0]
            pair_ref[device % 2, place : place + size] = high
            pair_ref[device % 2, deep + place : deep + place + size] = low
            place += size

    def layer_two(device):
        base = device * rows
        pair = pair_ref[device % 2]
        deep = pair.shape[0]
        cut = deep // MATRIX * MATRIX
        if 2 * cut < deep:
            cut = deep
        partial = jnp.dot(second_ref[:, :cut], pair[:cut], preferred_element_type=F32)
        partial = partial[:partial_rows] + partial[partial_rows:]
        if cut < deep:
            partial = partial + jnp.dot(
                second_ref[:partial_rows, cut:], pair[cut:], preferred_element_type=F32
            )
        for side in range(rows):
            partial_ref[base + side + 1] = partial[:, side * columns : (side + 1) * columns]

    def gather(device, most):
        for row in range(rows):
            total = None
            for branch in range(2):
                sums = []
                for d in range(3):
                    value = None
                    for c in range(3):
                        start = ((c * 3 + d) * 2 + branch) * SUBLANES
                        piece = partial_ref[device * rows + row + c, start : start + SUBLANES, :]
                        value = piece if value is None else value + piece
                    sums.append(value)
                output = lane_shifts(sums[0])[0] + sums[1] + lane_shifts(sums[2])[1]
                output = jnp.maximum(output, 0.0)
                total = output if total is None else total + output
            send_ref[device, row * SUBLANES : (row + 1) * SUBLANES] = total
            most = jnp.maximum(most, total)
        return most

    def step(device, most):
        fixed = isinstance(device, int)
        if not fixed or device + 1 < devices:
            layer_one(device + 1)
        if not fixed or device >= 2:
            most = gather(device - 2, most)
        if not fixed or device + 3 <= devices:
            build(device + 3)
        layer_two(device)
        return most

    for device in range(3):
        build(device)
    layer_one(0)
    most = zero
    ahead, behind = (2, 3) if devices > UNROLLED else (devices, 0)
    for device in range(ahead):
        most = step(device, most)
    most = lax.fori_loop(ahead, devices - behind, step, most) if behind else most
    for device in range(devices - behind, devices):
        most = step(device, most)
    for device in range(devices - 2, devices):
        most = gather(device, most)
    best = jnp.max(most, axis=1, keepdims=True)
    scale = 1.0 / jnp.maximum(best, TINY)
    root = jnp.concatenate(
        [row_of_column(piece, columns) for piece in root_rows(best)]
        + [jnp.zeros((SUBLANES - 2, columns), F32)],
        axis=0,
    )
    for device in range(devices):
        for row in range(rows):
            start = row * SUBLANES
            send_ref[device, start : start + SUBLANES] = (
                send_ref[device, start : start + SUBLANES] * scale
            )
        send_ref[device, rows * SUBLANES :] = root


def finish_kernel(local, came_ref, out_ref):
    devices, _, columns = came_ref.shape
    rows = out_ref.shape[1]
    place = rows * SUBLANES
    bests = [
        column_of_row(best_of_root(came_ref[device, place : place + 2]), SUBLANES)
        for device in range(devices)
    ]
    for row in range(rows):
        first = row * SUBLANES
        most = jnp.zeros((SUBLANES, columns), F32)
        for device in range(devices):
            most = jnp.maximum(most, came_ref[device, first : first + SUBLANES] * bests[device])
        inverse = 1.0 / (jnp.max(most, axis=0, keepdims=True) + EPSILON)
        for device in range(devices):
            value = came_ref[device, first : first + SUBLANES] * bests[device]
            value = value * (value * inverse) * (value * (1.0 / (bests[device] + EPSILON)))
            out_ref[device * local : (device + 1) * local, row, :] = value[:local]


def gather_sources(value, devices):
    bits = []
    bit = 1
    while bit < devices:
        bits.append(bit)
        bit *= 2
    upper = bits[2:]
    stages = [[2]]
    for first in range(0, len(upper), 2):
        pair = upper[first : first + 2]
        stages.append(pair if len(pair) == 1 else [pair[0], pair[0] ^ pair[1], pair[1]])
    masks = [0]
    gate = None
    for stage in stages:
        parts = [value] + [
            lax.ppermute(value, "tgt", [(i, i ^ mask) for i in range(devices)]) for mask in stage
        ]
        value = jnp.concatenate(parts, axis=0)
        masks = [mask ^ extra for extra in [0] + stage for mask in masks]
        gate = value if gate is None else gate
    return value, masks + [mask ^ 1 for mask in masks], gate


def exchange(slots):
    return lax.all_to_all(slots, "tgt", 0, 0, tiled=True)


def exchange_relative(slots):
    return exchange(slots.astype(jnp.float16)).astype(F32)


def room(*shapes):
    scratch = sum(int(np.prod(shape)) * jnp.dtype(kind).itemsize for shape, kind in shapes)
    return pltpu.CompilerParams(vmem_limit_bytes=scratch + 6 * 2**20)


VMEM = pl.BlockSpec(memory_space=pltpu.VMEM)


def shards(source_features, target_features, conv_first, conv_second):
    devices = lax.axis_size("tgt")
    rows, columns, channels = target_features.shape
    cells = source_features.shape[0] * devices
    hid = conv_first.shape[0]
    local = cells // devices
    parts = parts_of(local)
    hidden = local + 2
    window = max(SUBLANES, local + 4)
    tile = len(ORDER) * SUBLANES
    width = 3 * (tile + REPEATED * SUBLANES)
    depth = hidden * 2 * hid
    assert local <= SUBLANES and rows * devices % 4 == 0

    near, masks, mine = gather_sources(source_features, devices)

    second_rows = 18 * SUBLANES
    first_weights, second_weights = pl.pallas_call(
        functools.partial(prepare_kernel, devices, local, parts),
        out_shape=(
            jax.ShapeDtypeStruct((depth, width), BF16),
            jax.ShapeDtypeStruct((2 * second_rows, 2 * depth), BF16),
        ),
        in_specs=[VMEM] * 2 + [pl.BlockSpec(memory_space=pl.ANY)],
        out_specs=(VMEM,) * 2,
        scratch_shapes=[pltpu.VMEM((4 * TAP_PAD, 128), F32)],
        cost_estimate=pl.CostEstimate(flops=10**9, bytes_accessed=10**6, transcendentals=0),
        compiler_params=room(),
        name="prepare",
    )(
        jnp.transpose(conv_first, (1, 2, 3, 4, 0)),
        jnp.transpose(conv_second, (1, 2, 3, 4, 0)),
        mine,
    )
    target_unit = pl.pallas_call(
        target_kernel,
        out_shape=jax.ShapeDtypeStruct((rows * columns, channels), BF16),
        in_specs=[VMEM, pl.BlockSpec(memory_space=pl.ANY)],
        out_specs=VMEM,
        cost_estimate=pl.CostEstimate(flops=10**6, bytes_accessed=10**6, transcendentals=0),
        compiler_params=room(),
        name="target",
    )(target_features, first_weights)

    near, target_unit, first_weights = lax.optimization_barrier(
        (near, target_unit, first_weights)
    )
    far = lax.ppermute(near, "tgt", [(i, i ^ 1) for i in range(devices)])
    near = pl.pallas_call(
        near_kernel,
        out_shape=jax.ShapeDtypeStruct((cells // 2, rows * columns), F32),
        in_specs=[VMEM] * 2,
        out_specs=VMEM,
        cost_estimate=pl.CostEstimate(flops=10**8, bytes_accessed=10**6, transcendentals=0),
        compiler_params=room(),
        name="near",
    )(near, target_unit)
    slots = pl.pallas_call(
        functools.partial(match_kernel, local, masks),
        out_shape=jax.ShapeDtypeStruct((devices, whole_tiles(rows * (window + 2)), columns), F32),
        in_specs=[VMEM] * 3,
        out_specs=VMEM,
        scratch_shapes=[
            pltpu.VMEM((rows, cells + 2 * SUBLANES, columns), F32),
        ],
        compiler_params=room(),
        name="match",
    )(near, far, target_unit)

    stores = (
        ((rows * (devices + 1) + 1, len(parts), tile, columns), BF16),
        ((rows * devices + 2, second_rows, columns), F32),
        ((rows * devices, whole_tiles(window + 1), columns), F32),
        ((2, 2 * depth, rows * columns), BF16),
    )
    slots = pl.pallas_call(
        functools.partial(consensus_kernel, parts, local, rows),
        out_shape=jax.ShapeDtypeStruct((devices, (rows + 1) * SUBLANES, columns), F32),
        in_specs=[VMEM] * 3,
        out_specs=VMEM,
        scratch_shapes=[pltpu.VMEM(shape, kind) for shape, kind in stores],
        compiler_params=room(*stores),
        name="consensus",
    )(exchange_relative(slots), first_weights, second_weights)

    filtered = pl.pallas_call(
        functools.partial(finish_kernel, local),
        out_shape=jax.ShapeDtypeStruct((cells, rows, columns), F32),
        in_specs=[VMEM],
        out_specs=VMEM,
        compiler_params=room(),
        name="finish",
    )(exchange_relative(slots))
    return filtered[None]


def solution(mesh):
    placed = (P(("pairs", "tgt"), None), P(("pairs", "tgt"), None, None), P(), P())
    return jax.shard_map(
        shards, mesh=mesh, in_specs=placed, out_specs=P("pairs", None, "tgt", None), check_vma=False
    )
```

```python
import functools

import jax
import jax.numpy as jnp
import numpy as np
from jax import lax
from jax.experimental import pallas as pl
from jax.experimental.pallas import tpu as pltpu
from jax.sharding import PartitionSpec as P

EPSILON = 1e-05
TINY = 1e-30
MATRIX = 256
UNROLLED = 16
F32 = jnp.float32
BF16 = jnp.bfloat16
TAPS = 27
TAP_PAD = 32
SUBLANES = 8
ORDER = ((0, 0), (1, 0), (2, 0), (0, 1), (1, 1), (2, 1))
REPEATED = 4


def whole_tiles(count):
    return -(-count // SUBLANES) * SUBLANES


def parts_of(local):
    hidden = local + 2
    count = -(-hidden // (SUBLANES - 2))
    size = -(-hidden // count)
    parts = []
    for start in range(0, hidden, size):
        first = min(start, max(0, local + 4 - SUBLANES))
        parts.append((first, start, min(size, hidden - start)))
    return parts


def tap_fields(tap):
    return tap // 9, tap // 3 % 3, tap % 3


def first_codes(width):
    row = lax.broadcasted_iota(jnp.int32, (2 * TAP_PAD, 128), 0)
    b, c, d = tap_fields(row % TAP_PAD)
    rows = ((row // TAP_PAD * 3 + c) * 3 + d) * 16 + b
    rows = jnp.where(row % TAP_PAD < TAPS, rows, -100)[:, :1]
    column = lax.broadcasted_iota(jnp.int32, (SUBLANES, width), 1)
    tile, again = len(ORDER) * SUBLANES, REPEATED * SUBLANES
    extra = column >= 3 * tile
    rest = column - 3 * tile
    c = jnp.where(extra, rest // again, column // tile)
    place = jnp.where(extra, rest % again, column % tile) // SUBLANES
    code = ((jnp.where(extra, 3, 0) + c) * 3 + place % 3) * 16 + column % SUBLANES
    columns = jnp.where(extra & (place >= 3), -1, code)[:1]
    return rows, columns


def second_selector(local, blocks):
    height, width = 18 * SUBLANES, blocks * 2 * TAP_PAD
    row = lax.broadcasted_iota(jnp.int32, (height, 128), 0)
    rows = row // SUBLANES * 32 + row % SUBLANES
    rows = jnp.where(row % SUBLANES < local, rows, -100)[:, :1]
    column = lax.broadcasted_iota(jnp.int32, (SUBLANES, width), 1)
    tap = column % TAP_PAD
    b, c, d = tap_fields(tap)
    cell = column // (2 * TAP_PAD) - b
    code = ((c * 3 + d) * 2 + column // TAP_PAD % 2) * 32 + cell
    columns = jnp.where((tap < TAPS) & (cell >= 0), code, -1)[:1]
    return jnp.where(rows == columns, 1.0, 0.0).astype(BF16)


def unit(features):
    positive = jnp.maximum(features.astype(F32), 0.0)
    length = jnp.sqrt(jnp.sum(positive * positive, axis=-1, keepdims=True) + 1e-06)
    return (positive / length).astype(BF16)


def split(value):
    high = value.astype(BF16)
    return high, (value - high.astype(F32)).astype(BF16)


def prepare_kernel(
    devices, local, parts, first_ref, second_ref, gate_ref, first_out, second_out, taps_ref
):
    hid = first_ref.shape[-1]
    taps_ref[...] = jnp.zeros(taps_ref.shape, F32)
    for number, ref in enumerate((first_ref, second_ref)):
        base = 2 * TAP_PAD * number
        for b in range(3):
            for c in range(3):
                start = base + (b * 3 + c) * 3
                taps_ref[start : start + 3, :hid] = ref[1, b, c]
        for c in range(3):
            for d in range(3):
                piece = ref[c, d, 1]
                for b in range(3):
                    start = base + TAP_PAD + (b * 3 + c) * 3 + d
                    taps_ref[start : start + 1, :hid] = piece[b : b + 1]
    branches = [taps_ref[i * TAP_PAD : (i + 1) * TAP_PAD, :hid] for i in range(4)]
    width = first_out.shape[1]
    taps = jnp.concatenate(split(jnp.concatenate(branches[:2], axis=1)), axis=0)
    blocks = first_out.shape[0] // (2 * hid)
    rows_code, columns_code = first_codes(width)
    for block in range(blocks):
        first = [part[0] for part in parts if part[1] <= block][-1]
        pick = jnp.where(rows_code + (block - first) == columns_code, 1.0, 0.0).astype(BF16)
        piece = lax.dot_general(
            taps, pick, (((0,), (0,)), ((), ())), preferred_element_type=F32
        )
        if block == 0:
            piece = piece * jnp.where(lax.axis_index("tgt") == 0, 0.0, 1.0)
        if block == blocks - 1:
            piece = piece * jnp.where(lax.axis_index("tgt") == devices - 1, 0.0, 1.0)
        first_out[block * 2 * hid : (block + 1) * 2 * hid] = piece.astype(BF16)
    depth = blocks * 2 * hid
    groups = blocks * 2
    row_group = lax.broadcasted_iota(jnp.int32, (groups * TAP_PAD, depth), 0) // TAP_PAD
    lane_group = lax.broadcasted_iota(jnp.int32, (groups * TAP_PAD, depth), 1) // hid
    tiled = jnp.concatenate([jnp.concatenate(branches[2:], axis=1)] * blocks, axis=1)
    tiled = jnp.concatenate([tiled] * groups, axis=0)
    tiled = jnp.where(row_group == lane_group, tiled, 0.0)
    high, low = split(tiled)
    half = second_out.shape[0] // 2
    scatter = second_selector(local, blocks)
    high = jnp.dot(scatter, high, preferred_element_type=F32).astype(BF16)
    low = jnp.dot(scatter, low, preferred_element_type=F32).astype(BF16)
    second_out[:half, :depth] = high
    second_out[:half, depth:] = high
    second_out[half:, :depth] = low
    second_out[half:, depth:] = jnp.zeros_like(low)


def target_kernel(target_ref, gate_ref, unit_ref):
    rows, columns = target_ref.shape[:2]
    for row in range(rows):
        unit_ref[row * columns : (row + 1) * columns] = unit(target_ref[row])


def correlate(source, target):
    return lax.dot_general(
        unit(source), target, (((1,), (1,)), ((), ())), preferred_element_type=F32
    )


def near_kernel(near_ref, target_ref, out_ref):
    out_ref[...] = correlate(near_ref[...], target_ref[...])


def match_kernel(local, masks, near_ref, far_ref, target_ref, send_ref, order_ref):
    rows, padded, columns = order_ref.shape
    cells = padded - 2 * SUBLANES
    far = correlate(far_ref[...], target_ref[...])
    position = lax.axis_index("tgt")
    window = max(SUBLANES, local + 4)
    blank = jnp.zeros((SUBLANES, columns), F32)
    for row in range(rows):
        order_ref[row, :SUBLANES, :] = blank
        order_ref[row, SUBLANES + cells :, :] = blank
        lanes = slice(row * columns, (row + 1) * columns)
        middle = len(masks) // 2
        for piece, mask in enumerate(masks):
            start = SUBLANES + (position ^ mask) * local
            if local % SUBLANES == 0:
                start = pl.multiple_of(start, SUBLANES)
            held, first = (near_ref, piece) if piece < middle else (far, piece - middle)
            order_ref[row, pl.ds(start, local), :] = held[
                first * local : (first + 1) * local, lanes
            ]
        source_best = jnp.max(order_ref[row], axis=0, keepdims=True)
        scale = 1.0 / jnp.maximum(source_best, TINY)
        root = jnp.concatenate(root_rows(source_best), axis=0)
        place = rows * window + 2 * row
        for target in range(send_ref.shape[0]):
            first = SUBLANES + target * local - 2
            send_ref[target, row * window : (row + 1) * window] = (
                order_ref[row, first : first + window, :] * scale
            )
            send_ref[target, place : place + 2] = root
    used = rows * (window + 2)
    spare = send_ref.shape[1] - used
    if spare:
        for target in range(send_ref.shape[0]):
            send_ref[target, used:] = jnp.zeros((spare, columns), F32)


def root_rows(best):
    root = jnp.sqrt(jnp.sqrt(jnp.sqrt(best)))
    high = root.astype(BF16).astype(F32)
    return high, root - high


def best_of_root(rows):
    root = rows[:1] + rows[1:]
    for _ in range(3):
        root = root * root
    return root


def row_of_column(column, lanes):
    row = lax.broadcasted_iota(jnp.int32, (column.shape[0], lanes), 0)
    lane = lax.broadcasted_iota(jnp.int32, (column.shape[0], lanes), 1)
    return jnp.sum(jnp.where(row == lane, column, 0.0), axis=0, keepdims=True)


def column_of_row(values, count):
    row = lax.broadcasted_iota(jnp.int32, (count, values.shape[1]), 0)
    lane = lax.broadcasted_iota(jnp.int32, (count, values.shape[1]), 1)
    return jnp.sum(jnp.where(row == lane, values, 0.0), axis=1, keepdims=True)


def lane_shifts(value):
    lanes = value.shape[-1]
    lane = lax.broadcasted_iota(jnp.int32, value.shape, value.ndim - 1)
    axis = value.ndim - 1
    left = jnp.where(lane == 0, 0.0, pltpu.roll(value, 1, axis))
    right = jnp.where(lane == lanes - 1, 0.0, pltpu.roll(value, lanes - 1, axis))
    return left, right


def consensus_kernel(
    parts, local, rows, came_ref, first_ref, second_ref, send_ref, tile_ref, partial_ref, rows_ref, pair_ref
):
    devices, _, columns = came_ref.shape
    window = max(SUBLANES, local + 4)
    grid_rows = devices * rows
    tile = len(ORDER) * SUBLANES
    again = REPEATED * SUBLANES
    zero = jnp.zeros((SUBLANES, columns), F32)

    def piece_of(device, row, first):
        return rows_ref[device * rows + row, first : first + SUBLANES, :]

    def survey(device, best):
        best = list(best)
        for row in range(rows):
            place = rows * window + 2 * row
            largest = best_of_root(came_ref[device, place : place + 2])
            block = came_ref[device, row * window : (row + 1) * window] * largest
            rows_ref[device * rows + row, :window] = block
            rows_ref[device * rows + row, window : window + 1] = 1.0 / (largest + EPSILON)
            for number, (first, _, _) in enumerate(parts):
                best[number] = jnp.maximum(best[number], block[first : first + SUBLANES])
        return tuple(best)

    best = lax.fori_loop(0, devices, survey, (zero,) * len(parts), unroll=min(16, devices))
    scales = [
        jnp.broadcast_to(1.0 / (jnp.max(most, axis=1, keepdims=True) + EPSILON), most.shape)
        for most in best
    ]

    blank = jnp.zeros((tile, columns), BF16)
    for number in range(len(parts)):
        tile_ref[0, number] = blank

    def build(device):
        if isinstance(device, int) and device == devices:
            for row in range(rows):
                for number in range(len(parts)):
                    tile_ref[device * rows + row + 1, number] = blank
            return
        source = device
        for row in range(rows):
            inverse = rows_ref[source * rows + row, window : window + 1, :]
            for number, (first, _, _) in enumerate(parts):
                value = piece_of(source, row, first)
                value = value * (value * inverse) * (value * scales[number])
                left, right = lane_shifts(value)
                moved = (left, value, right)
                high = [piece.astype(BF16).astype(F32) for piece in moved]
                low = [piece - rounded for piece, rounded in zip(moved, high)]
                stacked = jnp.concatenate(
                    [(low if part else high)[offset] for offset, part in ORDER], axis=0
                )
                tile_ref[device * rows + row + 1, number] = stacked.astype(BF16)

    partial_rows = second_ref.shape[0] // 2
    empty = jnp.zeros((partial_rows, columns), F32)
    partial_ref[0] = empty
    partial_ref[grid_rows + 1] = empty

    def layer_one(device):
        base = device * rows
        hidden = []
        offset = 0
        for number, (_, _, size) in enumerate(parts):
            taps = []
            for side in range(rows):
                pieces = [tile_ref[base + side + c, number] for c in range(3)]
                pieces += [tile_ref[base + side + c, number, :again] for c in range(3)]
                taps.append(jnp.concatenate(pieces, axis=0))
            count = size * first_ref.shape[0] // (local + 2)
            hidden.append(
                jnp.dot(
                    first_ref[offset : offset + count],
                    jnp.concatenate(taps, axis=1),
                    preferred_element_type=F32,
                )
            )
            offset += count
        place = 0
        deep = pair_ref.shape[1] // 2
        for piece in hidden:
            high, low = split(jnp.maximum(piece, 0.0))
            size = piece.shape[0]
            pair_ref[device % 2, place : place + size] = high
            pair_ref[device % 2, deep + place : deep + place + size] = low
            place += size

    def layer_two(device):
        base = device * rows
        pair = pair_ref[device % 2]
        deep = pair.shape[0]
        cut = deep // MATRIX * MATRIX
        if 2 * cut < deep:
            cut = deep
        partial = jnp.dot(second_ref[:, :cut], pair[:cut], preferred_element_type=F32)
        partial = partial[:partial_rows] + partial[partial_rows:]
        if cut < deep:
            partial = partial + jnp.dot(
                second_ref[:partial_rows, cut:], pair[cut:], preferred_element_type=F32
            )
        for side in range(rows):
            partial_ref[base + side + 1] = partial[:, side * columns : (side + 1) * columns]

    def gather(device, most):
        for row in range(rows):
            total = None
            for branch in range(2):
                sums = []
                for d in range(3):
                    value = None
                    for c in range(3):
                        start = ((c * 3 + d) * 2 + branch) * SUBLANES
                        piece = partial_ref[device * rows + row + c, start : start + SUBLANES, :]
                        value = piece if value is None else value + piece
                    sums.append(value)
                output = lane_shifts(sums[0])[0] + sums[1] + lane_shifts(sums[2])[1]
                output = jnp.maximum(output, 0.0)
                total = output if total is None else total + output
            send_ref[device, row * SUBLANES : (row + 1) * SUBLANES] = total
            most = jnp.maximum(most, total)
        return most

    def step(device, most):
        fixed = isinstance(device, int)
        if not fixed or device + 1 < devices:
            layer_one(device + 1)
        if not fixed or device >= 2:
            most = gather(device - 2, most)
        if not fixed or device + 3 <= devices:
            build(device + 3)
        layer_two(device)
        return most

    for device in range(3):
        build(device)
    layer_one(0)
    most = zero
    ahead, behind = (2, 3) if devices > UNROLLED else (devices, 0)
    for device in range(ahead):
        most = step(device, most)
    most = lax.fori_loop(ahead, devices - behind, step, most) if behind else most
    for device in range(devices - behind, devices):
        most = step(device, most)
    for device in range(devices - 2, devices):
        most = gather(device, most)
    best = jnp.max(most, axis=1, keepdims=True)
    scale = 1.0 / jnp.maximum(best, TINY)
    root = jnp.concatenate(
        [row_of_column(piece, columns) for piece in root_rows(best)]
        + [jnp.zeros((SUBLANES - 2, columns), F32)],
        axis=0,
    )
    for device in range(devices):
        for row in range(rows):
            start = row * SUBLANES
            send_ref[device, start : start + SUBLANES] = (
                send_ref[device, start : start + SUBLANES] * scale
            )
        send_ref[device, rows * SUBLANES :] = root


def finish_kernel(local, came_ref, out_ref):
    devices, _, columns = came_ref.shape
    rows = out_ref.shape[1]
    place = rows * SUBLANES
    bests = [
        column_of_row(best_of_root(came_ref[device, place : place + 2]), SUBLANES)
        for device in range(devices)
    ]
    for row in range(rows):
        first = row * SUBLANES
        most = jnp.zeros((SUBLANES, columns), F32)
        for device in range(devices):
            most = jnp.maximum(most, came_ref[device, first : first + SUBLANES] * bests[device])
        inverse = 1.0 / (jnp.max(most, axis=0, keepdims=True) + EPSILON)
        for device in range(devices):
            value = came_ref[device, first : first + SUBLANES] * bests[device]
            value = value * (value * inverse) * (value * (1.0 / (bests[device] + EPSILON)))
            out_ref[device * local : (device + 1) * local, row, :] = value[:local]


def gather_sources(value, devices):
    bits = []
    bit = 1
    while bit < devices:
        bits.append(bit)
        bit *= 2
    upper = bits[2:]
    stages = [[2]]
    for first in range(0, len(upper), 2):
        pair = upper[first : first + 2]
        stages.append(pair if len(pair) == 1 else [pair[0], pair[0] ^ pair[1], pair[1]])
    masks = [0]
    gate = None
    for stage in stages:
        parts = [value] + [
            lax.ppermute(value, "tgt", [(i, i ^ mask) for i in range(devices)]) for mask in stage
        ]
        value = jnp.concatenate(parts, axis=0)
        masks = [mask ^ extra for extra in [0] + stage for mask in masks]
        gate = value if gate is None else gate
    return value, masks + [mask ^ 1 for mask in masks], gate


def exchange(slots):
    return lax.all_to_all(slots, "tgt", 0, 0, tiled=True)


def exchange_relative(slots):
    return exchange(slots.astype(jnp.float16)).astype(F32)


def room(*shapes):
    scratch = sum(int(np.prod(shape)) * jnp.dtype(kind).itemsize for shape, kind in shapes)
    return pltpu.CompilerParams(vmem_limit_bytes=scratch + 6 * 2**20)


VMEM = pl.BlockSpec(memory_space=pltpu.VMEM)


def shards(source_features, target_features, conv_first, conv_second):
    devices = lax.axis_size("tgt")
    rows, columns, channels = target_features.shape
    cells = source_features.shape[0] * devices
    hid = conv_first.shape[0]
    local = cells // devices
    parts = parts_of(local)
    hidden = local + 2
    window = max(SUBLANES, local + 4)
    tile = len(ORDER) * SUBLANES
    width = 3 * (tile + REPEATED * SUBLANES)
    depth = hidden * 2 * hid
    assert local <= SUBLANES and rows * devices % 4 == 0

    near, masks, mine = gather_sources(source_features, devices)

    second_rows = 18 * SUBLANES
    first_weights, second_weights = pl.pallas_call(
        functools.partial(prepare_kernel, devices, local, parts),
        out_shape=(
            jax.ShapeDtypeStruct((depth, width), BF16),
            jax.ShapeDtypeStruct((2 * second_rows, 2 * depth), BF16),
        ),
        in_specs=[VMEM] * 2 + [pl.BlockSpec(memory_space=pl.ANY)],
        out_specs=(VMEM,) * 2,
        scratch_shapes=[pltpu.VMEM((4 * TAP_PAD, 128), F32)],
        cost_estimate=pl.CostEstimate(flops=10**9, bytes_accessed=10**6, transcendentals=0),
        compiler_params=room(),
        name="prepare",
    )(
        jnp.transpose(conv_first, (1, 2, 3, 4, 0)),
        jnp.transpose(conv_second, (1, 2, 3, 4, 0)),
        mine,
    )
    target_unit = pl.pallas_call(
        target_kernel,
        out_shape=jax.ShapeDtypeStruct((rows * columns, channels), BF16),
        in_specs=[VMEM, pl.BlockSpec(memory_space=pl.ANY)],
        out_specs=VMEM,
        cost_estimate=pl.CostEstimate(flops=10**6, bytes_accessed=10**6, transcendentals=0),
        compiler_params=room(),
        name="target",
    )(target_features, first_weights)

    near, target_unit, first_weights = lax.optimization_barrier(
        (near, target_unit, first_weights)
    )
    far = lax.ppermute(near, "tgt", [(i, i ^ 1) for i in range(devices)])
    near = pl.pallas_call(
        near_kernel,
        out_shape=jax.ShapeDtypeStruct((cells // 2, rows * columns), F32),
        in_specs=[VMEM] * 2,
        out_specs=VMEM,
        cost_estimate=pl.CostEstimate(flops=10**8, bytes_accessed=10**6, transcendentals=0),
        compiler_params=room(),
        name="near",
    )(near, target_unit)
    slots = pl.pallas_call(
        functools.partial(match_kernel, local, masks),
        out_shape=jax.ShapeDtypeStruct((devices, whole_tiles(rows * (window + 2)), columns), F32),
        in_specs=[VMEM] * 3,
        out_specs=VMEM,
        scratch_shapes=[
            pltpu.VMEM((rows, cells + 2 * SUBLANES, columns), F32),
        ],
        compiler_params=room(),
        name="match",
    )(near, far, target_unit)

    stores = (
        ((rows * (devices + 1) + 1, len(parts), tile, columns), BF16),
        ((rows * devices + 2, second_rows, columns), F32),
        ((rows * devices, whole_tiles(window + 1), columns), F32),
        ((2, 2 * depth, rows * columns), BF16),
    )
    slots = pl.pallas_call(
        functools.partial(consensus_kernel, parts, local, rows),
        out_shape=jax.ShapeDtypeStruct((devices, (rows + 1) * SUBLANES, columns), F32),
        in_specs=[VMEM] * 3,
        out_specs=VMEM,
        scratch_shapes=[pltpu.VMEM(shape, kind) for shape, kind in stores],
        compiler_params=room(*stores),
        name="consensus",
    )(exchange_relative(slots), first_weights, second_weights)

    filtered = pl.pallas_call(
        functools.partial(finish_kernel, local),
        out_shape=jax.ShapeDtypeStruct((cells, rows, columns), F32),
        in_specs=[VMEM],
        out_specs=VMEM,
        compiler_params=room(),
        name="finish",
    )(exchange_relative(slots))
    return filtered[None]


def solution(mesh):
    placed = (P(("pairs", "tgt"), None), P(("pairs", "tgt"), None, None), P(), P())
    return jax.shard_map(
        shards, mesh=mesh, in_specs=placed, out_specs=P("pairs", None, "tgt", None), check_vma=False
    )
```

```python
import functools

import jax
import jax.numpy as jnp
import numpy as np
from jax import lax
from jax.experimental import pallas as pl
from jax.experimental.pallas import tpu as pltpu
from jax.sharding import PartitionSpec as P

EPSILON = 1e-05
TINY = 1e-30
MATRIX = 256
UNROLLED = 16
F32 = jnp.float32
BF16 = jnp.bfloat16
TAPS = 27
TAP_PAD = 32
SUBLANES = 8
ORDER = ((0, 0), (1, 0), (2, 0), (0, 1), (1, 1), (2, 1))
REPEATED = 4


def whole_tiles(count):
    return -(-count // SUBLANES) * SUBLANES


def parts_of(local):
    hidden = local + 2
    count = -(-hidden // (SUBLANES - 2))
    size = -(-hidden // count)
    parts = []
    for start in range(0, hidden, size):
        first = min(start, max(0, local + 4 - SUBLANES))
        parts.append((first, start, min(size, hidden - start)))
    return parts


def tap_fields(tap):
    return tap // 9, tap // 3 % 3, tap % 3


def first_codes(width):
    row = lax.broadcasted_iota(jnp.int32, (2 * TAP_PAD, 128), 0)
    b, c, d = tap_fields(row % TAP_PAD)
    rows = ((row // TAP_PAD * 3 + c) * 3 + d) * 16 + b
    rows = jnp.where(row % TAP_PAD < TAPS, rows, -100)[:, :1]
    column = lax.broadcasted_iota(jnp.int32, (SUBLANES, width), 1)
    tile, again = len(ORDER) * SUBLANES, REPEATED * SUBLANES
    extra = column >= 3 * tile
    rest = column - 3 * tile
    c = jnp.where(extra, rest // again, column // tile)
    place = jnp.where(extra, rest % again, column % tile) // SUBLANES
    code = ((jnp.where(extra, 3, 0) + c) * 3 + place % 3) * 16 + column % SUBLANES
    columns = jnp.where(extra & (place >= 3), -1, code)[:1]
    return rows, columns


def second_selector(local, blocks):
    height, width = 18 * SUBLANES, blocks * 2 * TAP_PAD
    row = lax.broadcasted_iota(jnp.int32, (height, 128), 0)
    rows = row // SUBLANES * 32 + row % SUBLANES
    rows = jnp.where(row % SUBLANES < local, rows, -100)[:, :1]
    column = lax.broadcasted_iota(jnp.int32, (SUBLANES, width), 1)
    tap = column % TAP_PAD
    b, c, d = tap_fields(tap)
    cell = column // (2 * TAP_PAD) - b
    code = ((c * 3 + d) * 2 + column // TAP_PAD % 2) * 32 + cell
    columns = jnp.where((tap < TAPS) & (cell >= 0), code, -1)[:1]
    return jnp.where(rows == columns, 1.0, 0.0).astype(BF16)


def unit(features):
    positive = jnp.maximum(features.astype(F32), 0.0)
    length = jnp.sqrt(jnp.sum(positive * positive, axis=-1, keepdims=True) + 1e-06)
    return (positive / length).astype(BF16)


def split(value):
    high = value.astype(BF16)
    return high, (value - high.astype(F32)).astype(BF16)


def prepare_kernel(
    devices, local, parts, first_ref, second_ref, gate_ref, first_out, second_out, taps_ref
):
    hid = first_ref.shape[-1]
    taps_ref[...] = jnp.zeros(taps_ref.shape, F32)
    for number, ref in enumerate((first_ref, second_ref)):
        base = 2 * TAP_PAD * number
        for b in range(3):
            for c in range(3):
                start = base + (b * 3 + c) * 3
                taps_ref[start : start + 3, :hid] = ref[1, b, c]
        for c in range(3):
            for d in range(3):
                piece = ref[c, d, 1]
                for b in range(3):
                    start = base + TAP_PAD + (b * 3 + c) * 3 + d
                    taps_ref[start : start + 1, :hid] = piece[b : b + 1]
    branches = [taps_ref[i * TAP_PAD : (i + 1) * TAP_PAD, :hid] for i in range(4)]
    width = first_out.shape[1]
    taps = jnp.concatenate(split(jnp.concatenate(branches[:2], axis=1)), axis=0)
    blocks = first_out.shape[0] // (2 * hid)
    rows_code, columns_code = first_codes(width)
    for block in range(blocks):
        first = [part[0] for part in parts if part[1] <= block][-1]
        pick = jnp.where(rows_code + (block - first) == columns_code, 1.0, 0.0).astype(BF16)
        piece = lax.dot_general(
            taps, pick, (((0,), (0,)), ((), ())), preferred_element_type=F32
        )
        if block == 0:
            piece = piece * jnp.where(lax.axis_index("tgt") == 0, 0.0, 1.0)
        if block == blocks - 1:
            piece = piece * jnp.where(lax.axis_index("tgt") == devices - 1, 0.0, 1.0)
        first_out[block * 2 * hid : (block + 1) * 2 * hid] = piece.astype(BF16)
    depth = blocks * 2 * hid
    groups = blocks * 2
    row_group = lax.broadcasted_iota(jnp.int32, (groups * TAP_PAD, depth), 0) // TAP_PAD
    lane_group = lax.broadcasted_iota(jnp.int32, (groups * TAP_PAD, depth), 1) // hid
    tiled = jnp.concatenate([jnp.concatenate(branches[2:], axis=1)] * blocks, axis=1)
    tiled = jnp.concatenate([tiled] * groups, axis=0)
    tiled = jnp.where(row_group == lane_group, tiled, 0.0)
    high, low = split(tiled)
    half = second_out.shape[0] // 2
    scatter = second_selector(local, blocks)
    high = jnp.dot(scatter, high, preferred_element_type=F32).astype(BF16)
    low = jnp.dot(scatter, low, preferred_element_type=F32).astype(BF16)
    second_out[:half, :depth] = high
    second_out[:half, depth:] = high
    second_out[half:, :depth] = low
    second_out[half:, depth:] = jnp.zeros_like(low)


def target_kernel(target_ref, gate_ref, unit_ref):
    rows, columns = target_ref.shape[:2]
    for row in range(rows):
        unit_ref[row * columns : (row + 1) * columns] = unit(target_ref[row])


def correlate(source, target):
    return lax.dot_general(
        unit(source), target, (((1,), (1,)), ((), ())), preferred_element_type=F32
    )


def near_kernel(near_ref, target_ref, out_ref):
    out_ref[...] = correlate(near_ref[...], target_ref[...])


def match_kernel(local, masks, near_ref, far_ref, target_ref, send_ref, order_ref):
    rows, padded, columns = order_ref.shape
    cells = padded - 2 * SUBLANES
    far = correlate(far_ref[...], target_ref[...])
    position = lax.axis_index("tgt")
    window = max(SUBLANES, local + 4)
    blank = jnp.zeros((SUBLANES, columns), F32)
    for row in range(rows):
        order_ref[row, :SUBLANES, :] = blank
        order_ref[row, SUBLANES + cells :, :] = blank
        lanes = slice(row * columns, (row + 1) * columns)
        middle = len(masks) // 2
        for piece, mask in enumerate(masks):
            start = SUBLANES + (position ^ mask) * local
            if local % SUBLANES == 0:
                start = pl.multiple_of(start, SUBLANES)
            held, first = (near_ref, piece) if piece < middle else (far, piece - middle)
            order_ref[row, pl.ds(start, local), :] = held[
                first * local : (first + 1) * local, lanes
            ]
        source_best = jnp.max(order_ref[row], axis=0, keepdims=True)
        scale = 1.0 / jnp.maximum(source_best, TINY)
        root = jnp.concatenate(root_rows(source_best), axis=0)
        place = rows * window + 2 * row
        for target in range(send_ref.shape[0]):
            first = SUBLANES + target * local - 2
            send_ref[target, row * window : (row + 1) * window] = (
                order_ref[row, first : first + window, :] * scale
            )
            send_ref[target, place : place + 2] = root
    used = rows * (window + 2)
    spare = send_ref.shape[1] - used
    if spare:
        for target in range(send_ref.shape[0]):
            send_ref[target, used:] = jnp.zeros((spare, columns), F32)


def root_rows(best):
    root = jnp.sqrt(jnp.sqrt(jnp.sqrt(best)))
    high = root.astype(BF16).astype(F32)
    return high, root - high


def best_of_root(rows):
    root = rows[:1] + rows[1:]
    for _ in range(3):
        root = root * root
    return root


def row_of_column(column, lanes):
    row = lax.broadcasted_iota(jnp.int32, (column.shape[0], lanes), 0)
    lane = lax.broadcasted_iota(jnp.int32, (column.shape[0], lanes), 1)
    return jnp.sum(jnp.where(row == lane, column, 0.0), axis=0, keepdims=True)


def column_of_row(values, count):
    row = lax.broadcasted_iota(jnp.int32, (count, values.shape[1]), 0)
    lane = lax.broadcasted_iota(jnp.int32, (count, values.shape[1]), 1)
    return jnp.sum(jnp.where(row == lane, values, 0.0), axis=1, keepdims=True)


def lane_shifts(value):
    lanes = value.shape[-1]
    lane = lax.broadcasted_iota(jnp.int32, value.shape, value.ndim - 1)
    axis = value.ndim - 1
    left = jnp.where(lane == 0, 0.0, pltpu.roll(value, 1, axis))
    right = jnp.where(lane == lanes - 1, 0.0, pltpu.roll(value, lanes - 1, axis))
    return left, right


def consensus_kernel(
    parts, local, rows, came_ref, first_ref, second_ref, send_ref, tile_ref, partial_ref, rows_ref, pair_ref
):
    devices, _, columns = came_ref.shape
    window = max(SUBLANES, local + 4)
    grid_rows = devices * rows
    tile = len(ORDER) * SUBLANES
    again = REPEATED * SUBLANES
    zero = jnp.zeros((SUBLANES, columns), F32)

    def piece_of(device, row, first):
        return rows_ref[device * rows + row, first : first + SUBLANES, :]

    def survey(device, best):
        best = list(best)
        for row in range(rows):
            place = rows * window + 2 * row
            largest = best_of_root(came_ref[device, place : place + 2])
            block = came_ref[device, row * window : (row + 1) * window] * largest
            rows_ref[device * rows + row, :window] = block
            rows_ref[device * rows + row, window : window + 1] = 1.0 / (largest + EPSILON)
            for number, (first, _, _) in enumerate(parts):
                best[number] = jnp.maximum(best[number], block[first : first + SUBLANES])
        return tuple(best)

    best = lax.fori_loop(0, devices, survey, (zero,) * len(parts), unroll=4)
    scales = [
        jnp.broadcast_to(1.0 / (jnp.max(most, axis=1, keepdims=True) + EPSILON), most.shape)
        for most in best
    ]

    blank = jnp.zeros((tile, columns), BF16)
    for number in range(len(parts)):
        tile_ref[0, number] = blank

    def build(device):
        if isinstance(device, int) and device == devices:
            for row in range(rows):
                for number in range(len(parts)):
                    tile_ref[device * rows + row + 1, number] = blank
            return
        source = device
        for row in range(rows):
            inverse = rows_ref[source * rows + row, window : window + 1, :]
            for number, (first, _, _) in enumerate(parts):
                value = piece_of(source, row, first)
                value = value * (value * inverse) * (value * scales[number])
                left, right = lane_shifts(value)
                moved = (left, value, right)
                high = [piece.astype(BF16).astype(F32) for piece in moved]
                low = [piece - rounded for piece, rounded in zip(moved, high)]
                stacked = jnp.concatenate(
                    [(low if part else high)[offset] for offset, part in ORDER], axis=0
                )
                tile_ref[device * rows + row + 1, number] = stacked.astype(BF16)

    partial_rows = second_ref.shape[0] // 2
    empty = jnp.zeros((partial_rows, columns), F32)
    partial_ref[0] = empty
    partial_ref[grid_rows + 1] = empty

    def layer_one(device):
        base = device * rows
        hidden = []
        offset = 0
        for number, (_, _, size) in enumerate(parts):
            taps = []
            for side in range(rows):
                pieces = [tile_ref[base + side + c, number] for c in range(3)]
                pieces += [tile_ref[base + side + c, number, :again] for c in range(3)]
                taps.append(jnp.concatenate(pieces, axis=0))
            count = size * first_ref.shape[0] // (local + 2)
            hidden.append(
                jnp.dot(
                    first_ref[offset : offset + count],
                    jnp.concatenate(taps, axis=1),
                    preferred_element_type=F32,
                )
            )
            offset += count
        place = 0
        deep = pair_ref.shape[1] // 2
        for piece in hidden:
            high, low = split(jnp.maximum(piece, 0.0))
            size = piece.shape[0]
            pair_ref[device % 2, place : place + size] = high
            pair_ref[device % 2, deep + place : deep + place + size] = low
            place += size

    def layer_two(device):
        base = device * rows
        pair = pair_ref[device % 2]
        deep = pair.shape[0]
        cut = deep // MATRIX * MATRIX
        if 2 * cut < deep:
            cut = deep
        partial = jnp.dot(second_ref[:, :cut], pair[:cut], preferred_element_type=F32)
        partial = partial[:partial_rows] + partial[partial_rows:]
        if cut < deep:
            partial = partial + jnp.dot(
                second_ref[:partial_rows, cut:], pair[cut:], preferred_element_type=F32
            )
        for side in range(rows):
            partial_ref[base + side + 1] = partial[:, side * columns : (side + 1) * columns]

    def gather(device, most):
        for row in range(rows):
            total = None
            for branch in range(2):
                sums = []
                for d in range(3):
                    value = None
                    for c in range(3):
                        start = ((c * 3 + d) * 2 + branch) * SUBLANES
                        piece = partial_ref[device * rows + row + c, start : start + SUBLANES, :]
                        value = piece if value is None else value + piece
                    sums.append(value)
                output = lane_shifts(sums[0])[0] + sums[1] + lane_shifts(sums[2])[1]
                output = jnp.maximum(output, 0.0)
                total = output if total is None else total + output
            send_ref[device, row * SUBLANES : (row + 1) * SUBLANES] = total
            most = jnp.maximum(most, total)
        return most

    def step(device, most):
        fixed = isinstance(device, int)
        if not fixed or device + 1 < devices:
            layer_one(device + 1)
        if not fixed or device >= 2:
            most = gather(device - 2, most)
        if not fixed or device + 3 <= devices:
            build(device + 3)
        layer_two(device)
        return most

    for device in range(3):
        build(device)
    layer_one(0)
    most = zero
    ahead, behind = (2, 3) if devices > UNROLLED else (devices, 0)
    for device in range(ahead):
        most = step(device, most)
    most = lax.fori_loop(ahead, devices - behind, step, most) if behind else most
    for device in range(devices - behind, devices):
        most = step(device, most)
    for device in range(devices - 2, devices):
        most = gather(device, most)
    best = jnp.max(most, axis=1, keepdims=True)
    scale = 1.0 / jnp.maximum(best, TINY)
    root = jnp.concatenate(
        [row_of_column(piece, columns) for piece in root_rows(best)]
        + [jnp.zeros((SUBLANES - 2, columns), F32)],
        axis=0,
    )
    for device in range(devices):
        for row in range(rows):
            start = row * SUBLANES
            send_ref[device, start : start + SUBLANES] = (
                send_ref[device, start : start + SUBLANES] * scale
            )
        send_ref[device, rows * SUBLANES :] = root


def finish_kernel(local, came_ref, out_ref):
    devices, _, columns = came_ref.shape
    rows = out_ref.shape[1]
    place = rows * SUBLANES
    bests = [
        column_of_row(best_of_root(came_ref[device, place : place + 2]), SUBLANES)
        for device in range(devices)
    ]
    for row in range(rows):
        first = row * SUBLANES
        most = jnp.zeros((SUBLANES, columns), F32)
        for device in range(devices):
            most = jnp.maximum(most, came_ref[device, first : first + SUBLANES] * bests[device])
        inverse = 1.0 / (jnp.max(most, axis=0, keepdims=True) + EPSILON)
        for device in range(devices):
            value = came_ref[device, first : first + SUBLANES] * bests[device]
            value = value * (value * inverse) * (value * (1.0 / (bests[device] + EPSILON)))
            out_ref[device * local : (device + 1) * local, row, :] = value[:local]


def gather_sources(value, devices):
    bits = []
    bit = 1
    while bit < devices:
        bits.append(bit)
        bit *= 2
    upper = bits[2:]
    stages = [[2]]
    for first in range(0, len(upper), 2):
        pair = upper[first : first + 2]
        stages.append(pair if len(pair) == 1 else [pair[0], pair[1], pair[0] ^ pair[1]])
    masks = [0]
    gate = None
    for stage in stages:
        parts = [value] + [
            lax.ppermute(value, "tgt", [(i, i ^ mask) for i in range(devices)]) for mask in stage
        ]
        value = jnp.concatenate(parts, axis=0)
        masks = [mask ^ extra for extra in [0] + stage for mask in masks]
        gate = value if gate is None else gate
    return value, masks + [mask ^ 1 for mask in masks], gate


def exchange(slots):
    return lax.all_to_all(slots, "tgt", 0, 0, tiled=True)


def exchange_relative(slots):
    return exchange(slots.astype(jnp.float16)).astype(F32)


def room(*shapes):
    scratch = sum(int(np.prod(shape)) * jnp.dtype(kind).itemsize for shape, kind in shapes)
    return pltpu.CompilerParams(vmem_limit_bytes=scratch + 6 * 2**20)


VMEM = pl.BlockSpec(memory_space=pltpu.VMEM)


def shards(source_features, target_features, conv_first, conv_second):
    devices = lax.axis_size("tgt")
    rows, columns, channels = target_features.shape
    cells = source_features.shape[0] * devices
    hid = conv_first.shape[0]
    local = cells // devices
    parts = parts_of(local)
    hidden = local + 2
    window = max(SUBLANES, local + 4)
    tile = len(ORDER) * SUBLANES
    width = 3 * (tile + REPEATED * SUBLANES)
    depth = hidden * 2 * hid
    assert local <= SUBLANES and rows * devices % 4 == 0

    near, masks, mine = gather_sources(source_features, devices)

    second_rows = 18 * SUBLANES
    first_weights, second_weights = pl.pallas_call(
        functools.partial(prepare_kernel, devices, local, parts),
        out_shape=(
            jax.ShapeDtypeStruct((depth, width), BF16),
            jax.ShapeDtypeStruct((2 * second_rows, 2 * depth), BF16),
        ),
        in_specs=[VMEM] * 2 + [pl.BlockSpec(memory_space=pl.ANY)],
        out_specs=(VMEM,) * 2,
        scratch_shapes=[pltpu.VMEM((4 * TAP_PAD, 128), F32)],
        cost_estimate=pl.CostEstimate(flops=10**9, bytes_accessed=10**6, transcendentals=0),
        compiler_params=room(),
        name="prepare",
    )(
        jnp.transpose(conv_first, (1, 2, 3, 4, 0)),
        jnp.transpose(conv_second, (1, 2, 3, 4, 0)),
        mine,
    )
    target_unit = pl.pallas_call(
        target_kernel,
        out_shape=jax.ShapeDtypeStruct((rows * columns, channels), BF16),
        in_specs=[VMEM, pl.BlockSpec(memory_space=pl.ANY)],
        out_specs=VMEM,
        cost_estimate=pl.CostEstimate(flops=10**6, bytes_accessed=10**6, transcendentals=0),
        compiler_params=room(),
        name="target",
    )(target_features, first_weights)

    near, target_unit, first_weights = lax.optimization_barrier(
        (near, target_unit, first_weights)
    )
    far = lax.ppermute(near, "tgt", [(i, i ^ 1) for i in range(devices)])
    near = pl.pallas_call(
        near_kernel,
        out_shape=jax.ShapeDtypeStruct((cells // 2, rows * columns), F32),
        in_specs=[VMEM] * 2,
        out_specs=VMEM,
        cost_estimate=pl.CostEstimate(flops=10**8, bytes_accessed=10**6, transcendentals=0),
        compiler_params=room(),
        name="near",
    )(near, target_unit)
    slots = pl.pallas_call(
        functools.partial(match_kernel, local, masks),
        out_shape=jax.ShapeDtypeStruct((devices, whole_tiles(rows * (window + 2)), columns), F32),
        in_specs=[VMEM] * 3,
        out_specs=VMEM,
        scratch_shapes=[
            pltpu.VMEM((rows, cells + 2 * SUBLANES, columns), F32),
        ],
        compiler_params=room(),
        name="match",
    )(near, far, target_unit)

    stores = (
        ((rows * (devices + 1) + 1, len(parts), tile, columns), BF16),
        ((rows * devices + 2, second_rows, columns), F32),
        ((rows * devices, whole_tiles(window + 1), columns), F32),
        ((2, 2 * depth, rows * columns), BF16),
    )
    slots = pl.pallas_call(
        functools.partial(consensus_kernel, parts, local, rows),
        out_shape=jax.ShapeDtypeStruct((devices, (rows + 1) * SUBLANES, columns), F32),
        in_specs=[VMEM] * 3,
        out_specs=VMEM,
        scratch_shapes=[pltpu.VMEM(shape, kind) for shape, kind in stores],
        compiler_params=room(*stores),
        name="consensus",
    )(exchange_relative(slots), first_weights, second_weights)

    filtered = pl.pallas_call(
        functools.partial(finish_kernel, local),
        out_shape=jax.ShapeDtypeStruct((cells, rows, columns), F32),
        in_specs=[VMEM],
        out_specs=VMEM,
        compiler_params=room(),
        name="finish",
    )(exchange_relative(slots))
    return filtered[None]


def solution(mesh):
    placed = (P(("pairs", "tgt"), None), P(("pairs", "tgt"), None, None), P(), P())
    return jax.shard_map(
        shards, mesh=mesh, in_specs=placed, out_specs=P("pairs", None, "tgt", None), check_vma=False
    )
```
